32 devices in a mesh: fsdp: 8 (over z, y), tp: 4 (over x, core).
Axes of the slice: x: 2, y: 2, z: 4, core: 2. Of those that a mesh axis runs over, the one named last changes fastest.
Arguments:
- inputs: bfloat16 [16384, 1024], P(('fsdp', 'tp')), may hold values from -6 to 6
- doc_lengths: int32 [16, 4], P('fsdp'), may hold values from 1 to 512, 1024 in all within a row
- first_gain: float32 [1024], replicated, may hold values from 0.1 to 1.9
- first_bias: float32 [1024], replicated, may hold values from -3 to 3
- w_query: bfloat16 [1024, 1024], P('fsdp', 'tp'), may hold values from -0.25 to 0.25
- b_query: float32 [1024], P('tp'), may hold values from -3 to 3
- w_key: bfloat16 [1024, 1024], P('fsdp', 'tp'), may hold values from -0.25 to 0.25
- w_value: bfloat16 [1024, 1024], P('fsdp', 'tp'), may hold values from -0.1875 to 0.1875
- b_value: float32 [1024], P('tp'), may hold values from -3 to 3
- w_out: bfloat16 [1024, 1024], P('tp', 'fsdp'), may hold values from -0.75 to 0.75
- b_out: float32 [1024], replicated, may hold values from -3 to 3
- second_gain: float32 [1024], replicated, may hold values from 0.1 to 1.9
- second_bias: float32 [1024], replicated, may hold values from -3 to 3
- w_up: bfloat16 [1024, 4096], P('fsdp', 'tp'), may hold values from -0.1875 to 0.1875
- b_up: float32 [4096], P('tp'), may hold values from -3 to 3
- w_down: bfloat16 [4096, 1024], P('tp', 'fsdp'), may hold values from -0.09375 to 0.09375
- b_down: float32 [1024], replicated, may hold values from -3 to 3
- cotangent: float32 [16384, 1024], P(('fsdp', 'tp')), may hold values from -6 to 6
Outputs:
- layer_out: bfloat16 [16384, 1024], P(('fsdp', 'tp'))
- input_grad: float32 [16384, 1024], P(('fsdp', 'tp'))
- grad_first_gain: float32 [1024], replicated
- grad_first_bias: float32 [1024], replicated
- grad_w_query: float32 [1024, 1024], P('fsdp', 'tp')
- grad_b_query: float32 [1024], P('tp')
- grad_w_key: float32 [1024, 1024], P('fsdp', 'tp')
- grad_w_value: float32 [1024, 1024], P('fsdp', 'tp')
- grad_b_value: float32 [1024], P('tp')
- grad_w_out: float32 [1024, 1024], P('tp', 'fsdp')
- grad_b_out: float32 [1024], replicated
- grad_second_gain: float32 [1024], replicated
- grad_second_bias: float32 [1024], replicated
- grad_w_up: float32 [1024, 4096], P('fsdp', 'tp')
- grad_b_up: float32 [4096], P('tp')
- grad_w_down: float32 [4096, 1024], P('tp', 'fsdp')
- grad_b_down: float32 [1024], replicated
The draws below stay inside these ranges and needn't reach their ends.
Inputs may be any that keep to these rules, and one draw needn't show every extreme that they name: `doc_lengths`: each row holds the lengths of the 4 documents of one sequence, in order, summing to 1024; the longest document of every row has 512 tokens.
All inputs are finite; a program needn't handle non-finite values.
Results may differ from the reference program's by a relative error of at most 0.018.
Values may be sent and summed in bfloat16 or wider, within the bound.
No kernel may reach another device: no remote copies, remote signals or barrier semaphores. Data moves between devices by JAX's collectives and lax.ppermute only.
A program may use at most 192 MiB of HBM per device.

```python
import math
import jax
import jax.numpy as jnp
import numpy as np
from jax import lax

D = 1024
HEADS = 16
HEAD_DIM = 64
FF = 4096
LENGTH = 1024
SEQS = 2
DOCS = 4
SEQUENCES = 16
TOKENS = 16384
N_FSDP = 8


def raised(values, key, source, target, blocks, factor):
    def block_of(axis_at):
        return (jnp.arange(values.shape[axis_at]) // (values.shape[axis_at] // blocks)).reshape((-1,) + (1,) * (values.ndim - 1 - axis_at))

    near = jax.random.permutation(key, blocks)[block_of(target)]
    second = (block_of(target) + blocks // 2) % blocks
    return jnp.where((block_of(source) == near) | (block_of(source) == second), factor * values, values)


def level_of(key, extent, shards, low, top_value):
    level, own = 1.0, jax.random.fold_in(key, 6)
    for dim, parts in shards:
        draws = jnp.exp(jax.random.uniform(jax.random.fold_in(own, dim), (parts,), jnp.float32, low / len(shards), top_value / len(shards)))
        level = level * jnp.repeat(draws, extent[dim] // parts).reshape([-1 if axis == dim else 1 for axis in range(len(extent))])
    return level


def profile(amount, total, most, skew):
    loads = [(1 << 20) // math.isqrt(grade ** skew) + 1 for grade in range(2, amount + 1)]
    rest, holding = total - most - (amount - 1), [1] * (amount - 1)
    while rest > 0:
        candidates = [i for i in range(amount - 1) if holding[i] < most]
        pool, left = sum([loads[i] for i in candidates]), rest
        for i in candidates:
            extra = min(most - holding[i], max(1, left * loads[i] // pool), rest)
            holding[i] = holding[i] + extra
            rest = rest - extra
    return np.array([most] + holding)


def uneven_parts(own_key, amount, total, most, skew):
    if amount == 2:
        one = jax.random.randint(own_key, (), max(1, total - most), min(most, total - 1) + 1)
        return jnp.stack([one, total - one])
    sizes = jnp.asarray(profile(amount, total, most, skew), jnp.int32)
    couples = (amount - 1) // 2
    donor, sink = sizes[1:1 + 2 * couples:2], sizes[2:2 + 2 * couples:2]
    margin = jnp.minimum(donor - 1, most - sink)
    passed = jax.random.randint(jax.random.fold_in(own_key, 1), (couples,), 0, 1 << 20) % (margin + 1)
    sizes = sizes.at[1:1 + 2 * couples:2].set(donor - passed).at[2:2 + 2 * couples:2].set(sink + passed)
    return sizes[jax.random.permutation(jax.random.fold_in(own_key, 2), amount)]


def normal_values(key, dims, width, reach, cuts=(), held_as=jnp.bfloat16):
    level = level_of(key, dims, cuts, -0.22, 0.18) if cuts else 1.0
    values = jax.random.normal(key, dims, jnp.float32) * width * level
    return jnp.minimum(jnp.maximum(values, -reach), reach).astype(held_as)


def noise_with(rng, shape, scale, most, cuts, heavy, kind=jnp.bfloat16):
    values = scale * jax.random.normal(rng, shape, jnp.float32)
    if cuts:
        values = values * level_of(rng, shape, cuts, -0.22, 0.18)
    return jnp.clip(raised(values, jax.random.fold_in(rng, 3), *heavy), -most, most).astype(kind)


def setup_inputs(seed: int = 0) -> dict:
    splits = jax.random.split(jax.random.key(seed), 19)
    inputs = noise_with(splits[0], (TOKENS, D), 1.0, 6.0, ((0, 32),), (0, 1, 32, 2.75))
    doc_lengths = jax.vmap(lambda own: uneven_parts(own, DOCS, LENGTH, LENGTH // 2, 1))(jax.random.split(splits[1], SEQUENCES)).reshape((SEQUENCES, DOCS)).astype(jnp.int32)
    first_gain = jnp.clip(1.0 + 0.18 * jax.random.normal(splits[2], (D,), jnp.float32), 0.1, 1.9)
    first_bias = normal_values(splits[3], (D,), 0.3, 3.0, (), jnp.float32)
    w_query = normal_values(splits[4], (D, D), (D // 2) ** -0.5, 0.25, ((0, 8), (1, 4)))
    b_query = normal_values(splits[5], (D,), 0.5, 3.0, ((0, 4),), jnp.float32)
    w_key = normal_values(splits[6], (D, D), (D // 2) ** -0.5, 0.25, ((0, 8), (1, 4)))
    w_value = normal_values(splits[7], (D, D), D ** -0.5, 0.1875, ((0, 8), (1, 4)))
    b_value = normal_values(splits[8], (D,), 0.3, 3.0, ((0, 4),), jnp.float32)
    w_out = normal_values(splits[9], (D, D), (D // 16) ** -0.5, 0.75, ((0, 4), (1, 8)))
    b_out = normal_values(splits[10], (D,), 0.3, 3.0, (), jnp.float32)
    second_gain = jnp.clip(1.0 + 0.18 * jax.random.normal(splits[11], (D,), jnp.float32), 0.1, 1.9)
    second_bias = normal_values(splits[12], (D,), 0.3, 3.0, (), jnp.float32)
    w_up = normal_values(splits[13], (D, FF), D ** -0.5, 0.1875, ((0, 8), (1, 4)))
    b_up = normal_values(splits[14], (FF,), 0.5, 3.0, ((0, 4),), jnp.float32)
    w_down = normal_values(splits[15], (FF, D), FF ** -0.5, 0.09375, ((0, 4), (1, 8)))
    b_down = normal_values(splits[16], (D,), 0.6, 3.0, (), jnp.float32)
    cotangent = noise_with(splits[17], (TOKENS, D), 1.0, 6.0, ((0, 32),), (0, 1, 32, 2.75), jnp.float32)
    return {"inputs": inputs, "doc_lengths": doc_lengths, "first_gain": first_gain, "first_bias": first_bias, "w_query": w_query, "b_query": b_query, "w_key": w_key, "w_value": w_value, "b_value": b_value, "w_out": w_out, "b_out": b_out, "second_gain": second_gain, "second_bias": second_bias, "w_up": w_up, "b_up": b_up, "w_down": w_down, "b_down": b_down, "cotangent": cotangent}


EPSILON = 1e-05
HIGH = lax.Precision.HIGHEST

@jax.custom_vjp
def low(v):
    return lax.optimization_barrier(v.astype(jnp.bfloat16)).astype(jnp.float32)

@jax.custom_vjp
def low_back(v):
    return v

def low_keep(v):
    return (low(v), None)

def low_pass(kept, grad):
    return (grad,)

def back_keep(v):
    return (v, None)

def back_low(kept, grad):
    return (low(grad),)
low.defvjp(low_keep, low_pass)
low_back.defvjp(back_keep, back_low)

def matmul(left, right):
    return jnp.dot(left, right, precision=HIGH)

def smooth_gate(values):
    return jax.nn.gelu(values, approximate=False)

def layer_norm(values, gain, shift):
    center = values - lax.optimization_barrier(jnp.mean(values, axis=-1, keepdims=True))
    spread = lax.optimization_barrier(jnp.mean(center * center, axis=-1, keepdims=True))
    return center * lax.rsqrt(spread + EPSILON) * gain + shift

def document_ids(doc_lengths):
    ends = jnp.cumsum(doc_lengths, axis=1).astype(jnp.int32)
    places = jnp.arange(LENGTH, dtype=jnp.int32)
    return lax.optimization_barrier(jnp.sum((places[None, :, None] >= ends[:, None, :]).astype(jnp.int32), axis=2)).astype(jnp.int32)

def attend_one(query_seq, key_seq, value_seq, ids_seq):
    block = min(LENGTH, 512)
    places = jnp.arange(LENGTH, dtype=jnp.int32)
    pieces = []
    for first in range(0, LENGTH, block):
        query_block = query_seq[first:first + block]
        raw = jnp.einsum('qhd,khd->hqk', query_block, key_seq, precision=HIGH)
        scores = low_back(raw) * HEAD_DIM ** (-0.5)
        allowed = (places[None, :] <= places[first:first + block, None]) & (ids_seq[None, :] == ids_seq[first:first + block, None])
        scores = jnp.where(allowed[None], scores, -1e+30)
        weights = jax.nn.softmax(scores, axis=-1)
        pieces.append(jnp.einsum('hqk,khd->qhd', low(weights), value_seq, precision=HIGH))
    return jnp.concatenate(pieces, axis=0)

def attention(query_all, key_all, value_all, ids):
    shape = (SEQS, LENGTH, HEADS, HEAD_DIM)
    checked = jax.checkpoint(attend_one)
    context = lax.map(lambda packed: checked(packed[0], packed[1], packed[2], packed[3]), (query_all.reshape(shape), key_all.reshape(shape), value_all.reshape(shape), ids))
    return context.reshape(SEQS * LENGTH, D)

def layer(params, tokens, ids):
    first_gain, first_bias, w_query, b_query, w_key, w_value, b_value, w_out, b_out, second_gain, second_bias, w_up, b_up, w_down, b_down = params
    normed = low(layer_norm(tokens, first_gain, first_bias))
    queries = low(low_back(matmul(normed, w_query) + b_query))
    key_rows = low(low_back(matmul(normed, w_key)))
    value_rows = low(low_back(matmul(normed, w_value) + b_value))
    context = low(low_back(attention(queries, key_rows, value_rows, ids)))
    hidden = tokens + low_back(matmul(context, w_out)) + b_out
    normed_two = low(layer_norm(hidden, second_gain, second_bias))
    before = low_back(matmul(normed_two, w_up) + b_up)
    active = low(smooth_gate(before))
    return hidden + low_back(matmul(active, w_down)) + b_down

def reference(inputs, doc_lengths, first_gain, first_bias, w_query, b_query, w_key, w_value, b_value, w_out, b_out, second_gain, second_bias, w_up, b_up, w_down, b_down, cotangent):
    params = tuple((array.astype(jnp.float32) for array in (first_gain, first_bias, w_query, b_query, w_key, w_value, b_value, w_out, b_out, second_gain, second_bias, w_up, b_up, w_down, b_down)))
    ids = document_ids(doc_lengths).reshape(N_FSDP, SEQS, LENGTH)
    group_rows = SEQS * LENGTH
    stacked = inputs.astype(jnp.float32).reshape(N_FSDP, group_rows, D)
    pulled = cotangent.astype(jnp.float32).reshape(N_FSDP, group_rows, D)

    def group(totals, packed):
        tokens, cot_rows, group_ids = packed
        result, pullback = jax.vjp(lambda weights, values: layer(weights, values, group_ids), params, tokens)
        grads, token_grad = pullback(cot_rows)
        return (jax.tree.map(jnp.add, totals, grads), (result.astype(jnp.bfloat16), token_grad))
    zeros = jax.tree.map(jnp.zeros_like, params)
    totals, (outputs, token_grads) = lax.scan(group, zeros, (stacked, pulled, ids))
    return (outputs.reshape(TOKENS, D), token_grads.reshape(TOKENS, D), totals[0], totals[1], totals[2], totals[3], totals[4], totals[5], totals[6], totals[7], totals[8], totals[9], totals[10], totals[11], totals[12], totals[13], totals[14])
```

```python
import functools

import jax
import jax.numpy as jnp
from jax import lax
from jax.experimental import pallas as pl
from jax.experimental.pallas import tpu as pltpu
from jax.sharding import Mesh, PartitionSpec as P

HEAD_DIM = 64
LENGTH = 1024
BLOCK = 256
PAIR = 2 * HEAD_DIM
EPSILON = 1e-05
SCALE = HEAD_DIM**-0.5
LOW = jnp.bfloat16
FULL = jnp.float32
SWAP = ((0, 1), (1, 0))
DEEP = 4
LANES = 128


def swap(values, axis):
    return lax.ppermute(values, axis, SWAP)


def all_sum(values, axis):
    size, step = lax.axis_size(axis), 1
    while step < size:
        values = values + lax.ppermute(values, axis, [(i, i ^ step) for i in range(size)])
        step *= 2
    return values


def call(kernel, meta, grid, ins, in_specs, outs, out_specs, scratch=(), flops=0, limit=24):
    moved = sum(a.size * a.dtype.itemsize for a in list(ins) + list(outs))
    return pl.pallas_call(
        kernel,
        out_shape=outs,
        grid_spec=pltpu.PrefetchScalarGridSpec(
            num_scalar_prefetch=1,
            grid=grid,
            in_specs=in_specs,
            out_specs=out_specs,
            scratch_shapes=scratch,
        ),
        compiler_params=pltpu.CompilerParams(vmem_limit_bytes=limit << 20),
        cost_estimate=pl.CostEstimate(flops=flops, bytes_accessed=moved, transcendentals=0),
    )(meta, *ins)


def like(shape, kind):
    return jax.ShapeDtypeStruct(shape, kind)


def fixed(shape):
    return pl.BlockSpec(shape, lambda *_: (0,) * len(shape))


def dot(left, right):
    return jnp.dot(left, right, preferred_element_type=FULL)


def nt(left, right):
    return lax.dot_general(left, right, (((1,), (1,)), ((), ())), preferred_element_type=FULL)


def chunk_of(place, at_y):
    return 2 * lax.rem(place, DEEP) + lax.rem(at_y + place // DEEP, 2)


def flip_kernel(meta, own, other, out):
    half = own.shape[0]
    out[:, :half] = own[...].T
    out[:, half:] = other[...].T


def flip(meta, own, other):
    rows, wide = own.shape
    part = pl.BlockSpec((rows, LANES), lambda p, m: (0, chunk_of(p, m[1])))
    return call(
        flip_kernel,
        meta,
        (wide // LANES,),
        [own, other],
        [part, part],
        [like((wide, 2 * rows), LOW)],
        [pl.BlockSpec((LANES, 2 * rows), lambda p, m: (p, 0))],
    )[0]


def fill_local(meta, own, other, local):
    rows = own.shape[0]
    for place in range(2 * DEEP):
        chunk = 2 * (place % DEEP) + lax.rem(meta[1] + place // DEEP, 2)
        source = pl.ds(pl.multiple_of(chunk * LANES, LANES), LANES)
        target = slice(place * LANES, (place + 1) * LANES)
        local[:rows, target] = own[:, source]
        local[rows:, target] = other[:, source]


def into_kernel(finish, meta, own, other, low, high, *rest):
    *rest, local = rest

    @pl.when(pl.program_id(0) == 0)
    def _():
        fill_local(meta, own, other, local)

    width = low.shape[-1]
    half = DEEP * LANES
    low_w = low[...].reshape(half, width)
    high_w = high[...].reshape(half, width)
    for first in range(0, local.shape[0], BLOCK):
        rows = slice(first, first + BLOCK)
        finish(rows, dot(local[rows, :half], low_w) + dot(local[rows, half:], high_w), *rest)


def into(finish, meta, own, other, low, high, extra, extra_specs, outs, out_specs, steps, low_spec, high_spec):
    rows, wide = own.shape
    width = low_spec.block_shape[-1]
    return call(
        functools.partial(into_kernel, finish),
        meta,
        (steps,),
        [own, other, low, high, *extra],
        [fixed((rows, wide)), fixed((rows, wide)), low_spec, high_spec, *extra_specs],
        outs,
        out_specs,
        [pltpu.VMEM((2 * rows, wide), LOW)],
        flops=4 * rows * wide * width * steps,
    )


def project_finish(rows, total, bias, out):
    out[0, rows, :] = (total + bias[0]).astype(LOW)


def project(meta, own, other, low, low_at, high, high_at, count, bias):
    tokens, width = 2 * own.shape[0], low.shape[-1]
    block = (DEEP, 1, LANES, width)
    return into(
        project_finish,
        meta,
        own,
        other,
        low,
        high,
        [bias],
        [pl.BlockSpec((1, 1, width), lambda j, m: (j, 0, 0))],
        [like((count, tokens, width), LOW)],
        [pl.BlockSpec((1, tokens, width), lambda j, m: (j, 0, 0))],
        count,
        pl.BlockSpec(block, lambda j, m: (0, low_at + j, 0, 0)),
        pl.BlockSpec(block, lambda j, m: (0, high_at + j, 0, 0)),
    )[0]


def gelu_finish(rows, total, bias, active, slope):
    before = total + bias[...]
    phi = 0.5 * (1.0 + lax.erf(before * (2.0**-0.5)))
    active[rows, :] = (before * phi).astype(LOW)
    slope[rows, :] = (phi + before * jnp.exp(-0.5 * before * before) * (2.0 * jnp.pi) ** -0.5).astype(LOW)


def slope_finish(rows, total, slope, out, sums):
    low = (total * slope[rows, :].astype(FULL)).astype(LOW)
    out[rows, :] = low
    part = jnp.sum(low.astype(FULL), axis=0, keepdims=True)
    sums[...] = part if rows.start == 0 else sums[...] + part


def tiles(tokens, tile):
    return pl.BlockSpec((tokens, tile), lambda j, m: (0, j))


def up_gelu(meta, own, other, low, high, bias, tile=256):
    tokens, width = 2 * own.shape[0], low.shape[-1]
    block = pl.BlockSpec((DEEP, LANES, tile), lambda j, m: (0, 0, j))
    return into(
        gelu_finish,
        meta,
        own,
        other,
        low,
        high,
        [bias],
        [pl.BlockSpec((1, tile), lambda j, m: (0, j))],
        [like((tokens, width), LOW)] * 2,
        [tiles(tokens, tile)] * 2,
        width // tile,
        block,
        block,
    )


def down_back(meta, own, other, low, high, slope, tile=256):
    tokens, width = 2 * own.shape[0], low.shape[-1]
    block = pl.BlockSpec((DEEP, LANES, tile), lambda j, m: (0, 0, j))
    return into(
        slope_finish,
        meta,
        own,
        other,
        low,
        high,
        [slope],
        [tiles(tokens, tile)],
        [like((tokens, width), LOW), like((1, width), FULL)],
        [tiles(tokens, tile), pl.BlockSpec((1, tile), lambda j, m: (0, j))],
        width // tile,
        block,
        block,
    )


def outof_kernel(terms, meta, *refs):
    own, far = refs[-2:]
    rows = own.shape[0]
    even = meta[1] == 0
    sides = []
    for term in range(terms):
        low = refs[3 * term + 1]
        high = refs[3 * term + 2]
        low = low[...].reshape(LANES, low.shape[-1])
        high = high[...].reshape(LANES, high.shape[-1])
        sides.append(jnp.concatenate([jnp.where(even, low, high), jnp.where(even, high, low)], axis=0))
    for first in range(0, 2 * rows, BLOCK):
        total = None
        for term in range(terms):
            left = refs[3 * term]
            part = left[first : first + BLOCK, :] if len(left.shape) == 2 else left[0, first : first + BLOCK, :]
            product = nt(part, sides[term])
            total = product if total is None else total + product
        if first < rows:
            own[first : first + BLOCK, :] = total
        else:
            far[first - rows : first - rows + BLOCK, :] = total.astype(LOW)


def outof(meta, terms, wide):
    ins, specs, flops = [], [], 0
    for left, left_at, low, low_at, high, high_at in terms:
        tokens, width = left.shape[-2:]
        if left_at is None:
            specs.append(fixed((tokens, width)))
        else:
            specs.append(pl.BlockSpec((1, tokens, width), lambda z, m, at=left_at: (at, 0, 0)))
        for side, at in ((low, low_at), (high, high_at)):
            if at is None:
                specs.append(pl.BlockSpec((1, LANES, width), lambda z, m: (z, 0, 0)))
            else:
                specs.append(pl.BlockSpec((1, 1, LANES, width), lambda z, m, at=at: (z, at, 0, 0)))
        ins += [left, low, high]
        flops += 2 * tokens * wide * width
    rows = tokens // 2
    tile = 2 * LANES
    out_spec = pl.BlockSpec((rows, tile), lambda z, m: (0, z))
    return call(
        functools.partial(outof_kernel, len(terms)),
        meta,
        (wide // tile,),
        ins,
        specs,
        [like((rows, wide), FULL), like((rows, wide), LOW)],
        [out_spec, out_spec],
        flops=flops,
    )


def store_blocks(flipped, right, own, far, at):
    half = DEEP * LANES
    for first in range(0, 2 * half, BLOCK):
        grad = dot(flipped[first : first + BLOCK, :], right).astype(LOW)
        target = own if first < half else far
        for part in range(BLOCK // LANES):
            place = (first % half) // LANES + part
            target[(place, *at)] = grad[part * LANES : (part + 1) * LANES, :]


def weight_kernel(meta, flipped, right, own, far):
    store_blocks(flipped, right[...], own, far, ())


def weight_grad(meta, flipped, right, tile=256):
    wide, tokens = flipped.shape
    width = right.shape[1]
    out = like((DEEP, LANES, width), LOW)
    out_spec = pl.BlockSpec((DEEP, LANES, tile), lambda j, m: (0, 0, j))
    return call(
        weight_kernel,
        meta,
        (width // tile,),
        [flipped, right],
        [fixed((wide, tokens)), tiles(tokens, tile)],
        [out, out],
        [out_spec, out_spec],
        flops=2 * wide * tokens * width,
    )


def pair_kernel(count, meta, *refs):
    own, far = refs[-2:]
    for one in range(count):

        @pl.when(pl.program_id(0) == one)
        def _(one=one):
            right = refs[2 * one + 1]
            right = right[0] if len(right.shape) == 3 else right[...]
            store_blocks(refs[2 * one], right, own, far, (0,))


def pair_grad(meta, terms):
    ins, specs = [], []
    for flipped, right, at in terms:
        tokens, width = right.shape[-2:]
        ins += [flipped, right]
        specs.append(fixed(flipped.shape))
        specs.append(
            fixed((tokens, width)) if at is None else pl.BlockSpec((1, tokens, width), lambda j, m, at=at: (at, 0, 0))
        )
    out = like((DEEP, len(terms), LANES, width), LOW)
    out_spec = pl.BlockSpec((DEEP, 1, LANES, width), lambda j, m: (0, j, 0, 0))
    return call(
        functools.partial(pair_kernel, len(terms)),
        meta,
        (len(terms),),
        ins,
        specs,
        [out, out],
        [out_spec, out_spec],
        flops=2 * flipped.size * width * len(terms),
    )


def row_ranges():
    for first in range(0, LENGTH, BLOCK):
        yield first, max(0, first - LENGTH // 2), first + BLOCK


def ordered(ref, core):
    half = LENGTH // 2
    start = pl.multiple_of(core * half, half)
    rest = pl.multiple_of((1 - core) * half, half)
    return jnp.concatenate([ref[0, pl.ds(start, half), :], ref[0, pl.ds(rest, half), :]], axis=0)


def local_row(first, core):
    return pl.multiple_of(lax.rem(first + core * (LENGTH // 2), LENGTH), BLOCK)


def allowed_tile(start_ref, first, low, high):
    shape = (BLOCK, high - low)
    keys = low + lax.broadcasted_iota(jnp.int32, shape, 1)
    rows = first + lax.broadcasted_iota(jnp.int32, shape, 0)
    return (keys <= rows) & (keys >= start_ref[first : first + BLOCK, :1])


def forward_kernel(meta, start_ref, q_ref, k_ref, v_ref, out_ref, log_ref):
    core = meta[0]
    keys = ordered(k_ref, core)
    values = ordered(v_ref, core)
    lane = lax.broadcasted_iota(jnp.int32, (BLOCK, PAIR), 1)
    first_head = lane < HEAD_DIM
    for first, low, high in row_ranges():
        here = local_row(first, core)
        query = q_ref[0, pl.ds(here, BLOCK), :] * SCALE
        allowed = allowed_tile(start_ref, first, low, high)
        outs = []
        logs = []
        for head in range(2):
            picked = jnp.where(first_head if head == 0 else ~first_head, query, jnp.zeros_like(query))
            scores = jnp.where(allowed, nt(picked, keys[low:high]), -1e30)
            highest = jnp.max(scores, axis=-1, keepdims=True)
            expos = jnp.exp(scores - highest)
            totals = jnp.sum(expos, axis=-1, keepdims=True)
            outs.append(dot(expos.astype(LOW), values[low:high]) * (1.0 / totals))
            logs.append(highest + jnp.log(totals))
        out_ref[pl.ds(here, BLOCK), :] = jnp.where(first_head, outs[0], outs[1]).astype(LOW)
        log_ref[pl.ds(here, BLOCK), :] = jnp.where(first_head, logs[0], logs[1])


def backward_kernel(meta, start_ref, q_ref, k_ref, v_ref, log_ref, grad_ref, out_ref, sum_ref, key_sum, value_sum):
    core = meta[0]
    keys = ordered(k_ref, core)
    values = ordered(v_ref, core)
    lane = lax.broadcasted_iota(jnp.int32, (BLOCK, PAIR), 1)
    first_head = lane < HEAD_DIM
    key_sum[...] = jnp.zeros_like(key_sum)
    value_sum[...] = jnp.zeros_like(value_sum)
    query_total = None
    for first, low, high in row_ranges():
        here = local_row(first, core)
        query = q_ref[0, pl.ds(here, BLOCK), :] * SCALE
        grad = grad_ref[0, pl.ds(here, BLOCK), :]
        logs = log_ref[pl.ds(here, BLOCK), :]
        allowed = allowed_tile(start_ref, first, low, high)
        query_flip = query.T
        grad_flip = grad.T
        outs = []
        for head in range(2):
            mask = first_head if head == 0 else ~first_head
            band = slice(head * HEAD_DIM, (head + 1) * HEAD_DIM)
            query_one = jnp.where(mask, query, jnp.zeros_like(query))
            grad_one = jnp.where(mask, grad, jnp.zeros_like(grad))
            log_one = logs[:, head * HEAD_DIM : head * HEAD_DIM + 1]
            scores = jnp.where(allowed, nt(query_one, keys[low:high]), -1e30)
            weights = jnp.exp(scores - log_one)
            grad_probs = nt(grad_one, values[low:high])
            inner = jnp.sum(grad_probs * weights, axis=-1, keepdims=True)
            grad_scores = (weights * (grad_probs - inner)).astype(LOW)
            outs.append(dot(grad_scores, keys[low:high]))
            key_sum[band, low:high] += dot(query_flip[band, :], grad_scores)
            value_sum[band, low:high] += dot(grad_flip[band, :], weights.astype(LOW))
        grad_query = (jnp.where(first_head, outs[0], outs[1]) * SCALE).astype(LOW)
        out_ref[0, pl.ds(here, BLOCK), :] = grad_query
        part = jnp.sum(grad_query.astype(FULL), axis=0, keepdims=True)
        query_total = part if query_total is None else query_total + part
    half = LENGTH // 2
    value_total = None
    for part in range(2):
        there = pl.multiple_of(lax.rem(part + core, 2) * half, half)
        out_ref[1, pl.ds(there, half), :] = key_sum[:, part * half : (part + 1) * half].T.astype(LOW)
        grad_value = value_sum[:, part * half : (part + 1) * half].T.astype(LOW)
        out_ref[2, pl.ds(there, half), :] = grad_value
        part_total = jnp.sum(grad_value.astype(FULL), axis=0, keepdims=True)
        value_total = part_total if value_total is None else value_total + part_total
    sum_ref[0] = query_total
    sum_ref[1] = value_total


def pair_spec(at):
    return pl.BlockSpec((1, LENGTH, PAIR), lambda pair, m: (at, 0, pair))


ROW_SPEC = pl.BlockSpec((LENGTH, PAIR), lambda pair, m: (0, pair))
START_SPEC = pl.BlockSpec((LENGTH, 1), lambda pair, m: (0, 0))


def attend(meta, starts, query_key, value):
    width = value.shape[-1]
    return call(
        forward_kernel,
        meta,
        (width // PAIR,),
        [starts, query_key, query_key, value],
        [START_SPEC, pair_spec(0), pair_spec(1), pair_spec(0)],
        [like((LENGTH, width), LOW), like((LENGTH, width), FULL)],
        [ROW_SPEC, ROW_SPEC],
        flops=4 * LENGTH * LENGTH * width * 4,
        limit=40,
    )


def attend_back(meta, starts, query_key, value, logs, grad):
    width = value.shape[-1]
    return call(
        backward_kernel,
        meta,
        (width // PAIR,),
        [starts, query_key, query_key, value, logs, grad],
        [START_SPEC, pair_spec(0), pair_spec(1), pair_spec(0), ROW_SPEC, pair_spec(0)],
        [like((3, LENGTH, width), LOW), like((2, 1, width), FULL)],
        [
            pl.BlockSpec((3, LENGTH, PAIR), lambda pair, m: (0, 0, pair)),
            pl.BlockSpec((2, 1, PAIR), lambda pair, m: (0, 0, pair)),
        ],
        [pltpu.VMEM((PAIR, LENGTH), FULL)] * 2,
        flops=10 * LENGTH * LENGTH * width * 4,
        limit=40,
    )


def normalize(values):
    center = values - jnp.mean(values, axis=-1, keepdims=True)
    spread = jnp.mean(center * center, axis=-1, keepdims=True)
    rate = lax.rsqrt(spread + EPSILON)
    return center * rate, rate


def norm_kernel(meta, tokens, gain, shift, out):
    hat, _ = normalize(tokens[...].astype(FULL))
    out[...] = (hat * gain[...] + shift[...]).astype(LOW)


def join_kernel(meta, tokens, own, got, bias, gain, shift, hidden, out):
    total = tokens[...].astype(FULL) + (own[...] + got[...].astype(FULL)) + bias[...]
    hidden[...] = total
    hat, _ = normalize(total)
    out[...] = (hat * gain[...] + shift[...]).astype(LOW)


def keep_sums(step, sums, values):
    rows = values[0].shape[0]
    for at, value in enumerate(values):
        part = jnp.sum(value.reshape(rows // 8, 8, value.shape[1]), axis=0)

        @pl.when(step == 0)
        def _():
            sums[at] = part

        @pl.when(step > 0)
        def _():
            sums[at] = sums[at] + part


def norm_back(grad, values, gain):
    hat, rate = normalize(values)
    scaled = grad * gain
    row = rate * (
        scaled
        - jnp.mean(scaled, axis=-1, keepdims=True)
        - hat * jnp.mean(scaled * hat, axis=-1, keepdims=True)
    )
    return row, grad * hat


def second_kernel(meta, own, got, hidden, pulled, gain, out, low, sums):
    grad = own[...] + got[...].astype(FULL)
    row, gain_part = norm_back(grad, hidden[...], gain[...])
    total = pulled[...] + row
    out[...] = total
    low[...] = total.astype(LOW)
    keep_sums(pl.program_id(0), sums, [gain_part, grad, total, pulled[...]])


def first_kernel(meta, own, got, tokens, hidden_grad, gain, out, sums):
    grad = own[...] + got[...].astype(FULL)
    row, gain_part = norm_back(grad, tokens[...].astype(FULL), gain[...])
    out[...] = hidden_grad[...] + row
    keep_sums(pl.program_id(0), sums, [gain_part, grad])


def by_rows(kernel, meta, arrays, vectors, outs, sums=0, tile=128):
    rows, wide = arrays[0].shape
    row_spec = pl.BlockSpec((tile, wide), lambda i, m: (i, 0))
    out_shapes = [like((rows, wide), kind) for kind in outs]
    out_specs = [row_spec] * len(outs)
    if sums:
        out_shapes.append(like((sums, 8, wide), FULL))
        out_specs.append(fixed((sums, 8, wide)))
    return call(
        kernel,
        meta,
        (rows // tile,),
        arrays + vectors,
        [row_spec] * len(arrays) + [fixed((1, wide))] * len(vectors),
        out_shapes,
        out_specs,
        flops=20 * rows * wide,
    )


def document_starts(lengths):
    places = jnp.arange(LENGTH, dtype=jnp.int32)
    start = jnp.zeros((LENGTH,), jnp.int32)
    end = jnp.int32(0)
    for one in range(lengths.shape[0]):
        end = end + lengths[one]
        start = jnp.where(places >= end, end, start)
    return start[:, None]


def gather(shard, route):
    if lax.axis_size("w") > 1:
        shard = lax.all_gather(shard, "w", axis=shard.ndim - 2, tiled=True)
    mine = lax.all_gather(shard, "z", axis=0, tiled=False)
    by_x = swap(mine, "x")
    by_y = swap(mine, "y")
    return mine, by_x, by_y, swap(by_y, "x") if route == "x" else swap(by_x, "y")


def add_low(left, right):
    return (left.astype(FULL) + right.astype(FULL)).astype(LOW)


def return_blocks(own, own_far, other, other_far, route):
    if route == "x":
        got_y = swap(add_low(own_far, swap(other_far, "x")), "y")
        got_x = swap(other, "x")
    else:
        got_x = swap(add_low(other, swap(other_far, "y")), "x")
        got_y = swap(own_far, "y")
    return (own.astype(FULL) + got_y.astype(FULL) + got_x.astype(FULL)).astype(LOW)


def scatter_deep(total):
    total = lax.psum_scatter(total, "z", scatter_dimension=0, tiled=False)
    if lax.axis_size("w") > 1:
        total = lax.psum_scatter(total, "w", scatter_dimension=total.ndim - 2, tiled=True)
    return total.astype(FULL)


def on_device(
    inputs,
    doc_lengths,
    first_gain,
    first_bias,
    w_query,
    b_query,
    w_key,
    w_value,
    b_value,
    w_out,
    b_out,
    second_gain,
    second_bias,
    w_up,
    b_up,
    w_down,
    b_down,
    cotangent,
):
    rows, wide = inputs.shape
    here = w_query.shape[1]
    core = lax.axis_index("c").astype(jnp.int32)
    at_y = lax.axis_index("y").astype(jnp.int32)
    at_x = lax.axis_index("x")
    meta = jnp.stack([core, at_y])

    def line(vector):
        return vector.reshape(1, -1)

    shard = jnp.stack([w_query, w_key, w_value, w_out.T])
    if lax.axis_size("w") > 1:
        shard = lax.all_gather(shard, "w", axis=1, tiled=True)
    attn_mine = lax.all_gather(shard, "z", axis=0, tiled=False)
    attn_x = swap(attn_mine, "x")
    attn_y = swap(attn_mine, "y")
    attn_qk = swap(attn_y[:, :2], "x")
    attn_vo = swap(attn_x[:, 2:], "y")
    up = gather(w_up, "x")
    down = gather(w_down.T, "y")

    biases = jnp.concatenate([b_query, b_value, b_up])
    far = swap(biases, "x")
    starts = document_starts(lax.dynamic_index_in_dim(doc_lengths, at_x, 0, keepdims=False))

    cot_low = cotangent.astype(LOW)
    cot_other = swap(cot_low, "c")
    cot_flip = flip(meta, cot_low, cot_other)
    [normed] = by_rows(norm_kernel, meta, [inputs], [line(first_gain), line(first_bias)], [LOW])
    normed_other = swap(normed, "c")
    normed_flip = flip(meta, normed, normed_other)

    attn_low = [attn_mine, attn_x]
    attn_high = [[(attn_y, which) for which in range(4)], [(attn_qk, 0), (attn_qk, 1), (attn_vo, 0), (attn_vo, 1)]]
    query_key, value, context, logs = [], [], [], []
    for x in range(2):
        vector = biases if x == 0 else far
        bias_q, bias_v = vector[:here], vector[here : 2 * here]
        bias_qk = jnp.stack([bias_q, jnp.zeros_like(bias_q)])[:, None]
        high, at = attn_high[x][0]
        query_key.append(project(meta, normed, normed_other, attn_low[x], 0, high, at, 2, bias_qk))
        high, at = attn_high[x][2]
        value.append(project(meta, normed, normed_other, attn_low[x], 2, high, at, 1, bias_v[None, None]))
        one, two = attend(meta, starts, query_key[x], value[x])
        context.append(one)
        logs.append(two)
    own, sent = outof(meta, [(context[x], None, attn_low[x], 3, *attn_high[x][3]) for x in range(2)], wide)
    hidden, normed_two = by_rows(
        join_kernel,
        meta,
        [inputs, own, swap(sent, "c")],
        [line(b_out), line(second_gain), line(second_bias)],
        [FULL, LOW],
    )
    two_other = swap(normed_two, "c")
    two_flip = flip(meta, normed_two, two_other)

    up_sides = [(up[0], up[2]), (up[1], up[3])]
    down_sides = [(down[0], down[2]), (down[1], down[3])]
    active, slope = [], []
    for x in range(2):
        bias = line((biases if x == 0 else far)[2 * here :])
        one, two = up_gelu(meta, normed_two, two_other, *up_sides[x], bias)
        active.append(one)
        slope.append(two)
    down_grads = [weight_grad(meta, cot_flip, active[x]) for x in range(2)]
    owner_down = scatter_deep(return_blocks(*down_grads[0], *down_grads[1], "x"))

    before_grads = [down_back(meta, cot_low, cot_other, *down_sides[x], slope[x]) for x in range(2)]
    up_grads = [weight_grad(meta, two_flip, before_grads[x][0]) for x in range(2)]
    owner_up = scatter_deep(return_blocks(*up_grads[0], *up_grads[1], "y"))

    own, sent = outof(
        meta, [(before_grads[x][0], None, up_sides[x][0], None, up_sides[x][1], None) for x in range(2)], wide
    )
    hidden_grad, attn_grad, second_sums = by_rows(
        second_kernel, meta, [own, swap(sent, "c"), hidden, cotangent], [line(second_gain)], [FULL, LOW], sums=4
    )
    attn_other = swap(attn_grad, "c")
    attn_flip = flip(meta, attn_grad, attn_other)

    own, sent = outof(meta, [(active[x], None, down_sides[x][0], None, down_sides[x][1], None) for x in range(2)], wide)
    layer_out = (hidden + own + swap(sent, "c").astype(FULL) + b_down).astype(LOW)

    no_bias = jnp.zeros((1, 1, here), FULL)
    back, unit_sums, pieces = [None] * 2, [None] * 2, [None] * 2
    for x in (1, 0):
        high, at = attn_high[x][3]
        context_grad = project(meta, attn_grad, attn_other, attn_low[x], 3, high, at, 1, no_bias)
        back[x], unit_sums[x] = attend_back(meta, starts, query_key[x], value[x], logs[x], context_grad)
        pieces[x] = (
            pair_grad(meta, [(normed_flip, back[x], 0), (normed_flip, back[x], 1)]),
            pair_grad(meta, [(normed_flip, back[x], 2), (attn_flip, context[x], None)]),
        )
    attn_total = [return_blocks(*pieces[0][part], *pieces[1][part], "xy"[part]) for part in range(2)]
    owner_attn = scatter_deep(jnp.concatenate(attn_total, axis=1))

    own, sent = outof(
        meta,
        [(back[x], which, attn_low[x], which, *attn_high[x][which]) for x in range(2) for which in range(3)],
        wide,
    )
    input_grad, first_sums = by_rows(
        first_kernel, meta, [own, swap(sent, "c"), inputs, hidden_grad], [line(first_gain)], [FULL], sums=2
    )

    replicated = all_sum(jnp.sum(jnp.concatenate([first_sums, second_sums]), axis=1).reshape(-1), "c")
    own_units, far_units = [
        jnp.concatenate([unit_sums[x][0, 0], unit_sums[x][1, 0], before_grads[x][1][0]]) for x in range(2)
    ]
    got = swap(jnp.concatenate([replicated, far_units]), "x")
    summed = jnp.concatenate([replicated, own_units]) + got
    for axis in ("y", "z", "w"):
        summed = all_sum(summed, axis)
    vectors = summed[: 6 * wide].reshape(6, wide)
    units = summed[6 * wide :]

    return (
        layer_out,
        input_grad,
        vectors[0],
        vectors[1],
        owner_attn[0],
        units[:here],
        owner_attn[1],
        owner_attn[2],
        units[here : 2 * here],
        owner_attn[3].T,
        vectors[4],
        vectors[2],
        vectors[3],
        owner_up,
        units[2 * here :],
        owner_down.T,
        vectors[5],
    )


def solution(mesh):
    groups, lanes = mesh.shape["fsdp"], mesh.shape["tp"]
    inner = Mesh(
        mesh.devices.reshape(DEEP, 2, groups // (2 * DEEP), lanes // 2, 2), ("z", "y", "w", "x", "c")
    )
    f, t = ("z", "y", "w"), ("x", "c")
    tokens, rows, columns, units = P(f + t, None), P(f, t), P(t, f), P(t)
    return jax.shard_map(
        on_device,
        mesh=inner,
        in_specs=(
            tokens,
            P(f, None),
            P(),
            P(),
            rows,
            units,
            rows,
            rows,
            units,
            columns,
            P(),
            P(),
            P(),
            rows,
            units,
            columns,
            P(),
            tokens,
        ),
        out_specs=(
            tokens,
            tokens,
            P(),
            P(),
            rows,
            units,
            rows,
            rows,
            units,
            columns,
            P(),
            P(),
            P(),
            rows,
            units,
            columns,
            P(),
        ),
        check_vma=False,
    )
```

```python
import jax
import jax.numpy as jnp
from jax import lax
from jax.experimental import pallas as pl
from jax.experimental.pallas import tpu as pltpu
from jax.sharding import Mesh, PartitionSpec as P

HEAD_DIM = 64
LENGTH = 1024
BLOCK = 256
PAIR = 2 * HEAD_DIM
EPSILON = 1e-05
SCALE = HEAD_DIM**-0.5
LOW = jnp.bfloat16
FULL = jnp.float32
SWAP = ((0, 1), (1, 0))
DEEP = 4
LANES = 128
HALF = DEEP * LANES


def swap(values, axis):
    return lax.ppermute(values, axis, SWAP)


def swap_both(values):
    return lax.ppermute(values, ("y", "x"), ((0, 3), (1, 2), (2, 1), (3, 0)))


def all_sum(values, axis):
    size, step = lax.axis_size(axis), 1
    while step < size:
        values = values + lax.ppermute(values, axis, [(i, i ^ step) for i in range(size)])
        step *= 2
    return values


def after(values, *others):
    return lax.optimization_barrier((values, *others))[0]


def like(shape, kind):
    return jax.ShapeDtypeStruct(shape, kind)


ALL = slice(None)


ALL = slice(None)


class Operands:
    def __init__(self):
        self.parts = []

    def add(self, array, *index):
        for at, (one, where) in enumerate(self.parts):
            if one is array and where == index:
                return at
        self.parts.append((array, index))
        return len(self.parts) - 1

    def side(self, blocks):
        return [(self.add(array), index) for array, index in blocks]


class Buffers:
    def __init__(self, buffers, copies):
        self.buffers, self.copies = buffers, dict(enumerate(copies))

    def __getitem__(self, at):
        if at in self.copies:
            self.copies.pop(at).wait()
        return self.buffers[at]


def call(kernel, meta, ops, outs, scratch=(), time=3, limit=60):
    arrays = []
    for array, _ in ops.parts:
        if not any(array is one for one in arrays):
            arrays.append(array)
    source = [next(at for at, one in enumerate(arrays) if one is array) for array, _ in ops.parts]
    blocks = [jax.eval_shape(lambda a, index=index: a[index], like(array.shape, array.dtype)) for array, index in ops.parts]
    count, parts, results = len(arrays), len(ops.parts), len(outs)

    def body(*refs):
        meta_ref, sources, targets = refs[0], refs[1 : 1 + count], refs[1 + count : 1 + count + results]
        rest = refs[1 + count + results :]
        buffers, copies = rest[:parts], rest[parts : parts + results]
        in_sems, out_sems, *extra = rest[parts + results :]
        fetches = []
        for at, (_, index) in enumerate(ops.parts):
            ref = sources[source[at]]
            fetches.append(pltpu.make_async_copy(ref.at[index] if index else ref, buffers[at], in_sems.at[at]))
            fetches[-1].start()
        sent = []

        def put(at, *index):
            one, two = (copies[at].at[index], targets[at].at[index]) if index else (copies[at], targets[at])
            sent.append(pltpu.make_async_copy(one, two, out_sems.at[len(sent)]))
            sent[-1].start()

        kernel(meta_ref, Buffers(buffers, fetches), copies, put, *extra)
        for one in sent:
            one.wait()

    whole = pl.BlockSpec(memory_space=pl.ANY)
    return pl.pallas_call(
        body,
        out_shape=outs,
        in_specs=[pl.BlockSpec(memory_space=pltpu.SMEM)] + [whole] * count,
        out_specs=[whole] * results,
        scratch_shapes=[pltpu.VMEM(one.shape, one.dtype) for one in blocks]
        + [pltpu.VMEM(one.shape, one.dtype) for one in outs]
        + [pltpu.SemaphoreType.DMA((parts,)), pltpu.SemaphoreType.DMA((64,))]
        + list(scratch),
        compiler_params=pltpu.CompilerParams(vmem_limit_bytes=limit << 20),
        cost_estimate=pl.CostEstimate(flops=time << 20, bytes_accessed=1 << 16, transcendentals=0),
    )(meta, *arrays)


def whole_side(array):
    return [(array, (z,)) for z in range(DEEP)]


def stacked_side(array, which):
    return [(array, (z, which)) for z in range(DEEP)]


def split_side(low, high):
    return [((low, high)[z // 2], (z % 2,)) for z in range(DEEP)]


def dot(left, right):
    return jnp.dot(left, right, preferred_element_type=FULL)


def nt(left, right):
    return lax.dot_general(left, right, (((1,), (1,)), ((), ())), preferred_element_type=FULL)


def tn(left, right):
    return lax.dot_general(left, right, (((0,), (0,)), ((), ())), preferred_element_type=FULL)


def tall(refs, side, units=ALL):
    return jnp.concatenate([refs[at][(*index, ALL, units)] for at, index in side], axis=0)


def flat(refs, side, units):
    return jnp.concatenate([refs[at][(*index, units)] for at, index in side], axis=1)


def unfold(block):
    return jnp.concatenate([block[:, :LANES], block[:, LANES:]], axis=0)


def row_slices(count=LENGTH // BLOCK):
    return [slice(at * BLOCK, (at + 1) * BLOCK) for at in range(count)]


def rows_of(refs, pair, columns=ALL):
    for at in pair:
        for first in range(0, refs[at].shape[0], BLOCK):
            yield refs[at][first : first + BLOCK, columns]


def chunk_pairs():
    for first in range(0, 2 * DEEP, 2):
        yield (first, first + 1), slice(first * LANES, (first + 2) * LANES)


def by_tokens(lefts, rights):
    total = None
    for left, right in zip(lefts, rights):
        part = tn(left, right)
        total = part if total is None else total + part
    return total.astype(LOW)


def spread(even, terms, own, far, put, at):
    rows = own.shape[0]
    for z in range(DEEP):
        columns = slice(2 * z * LANES, 2 * (z + 1) * LANES)
        rights = []
        for _, chunks, product in terms:
            one, two = chunks(z)
            pair = [jnp.where(even, one, two), jnp.where(even, two, one)]
            rights.append(jnp.concatenate(pair, axis=0 if product is nt else 1))
        for block, here in enumerate(row_slices()):
            total = None
            for (left, _, product), right in zip(terms, rights):
                part = product(left(block), right)
                total = part if total is None else total + part
            if here.start < rows:
                own[here, columns] = total
            else:
                far[here.start - rows : here.stop - rows, columns] = total.astype(LOW)
        if z % 2:
            done = slice(columns.stop - 4 * LANES, columns.stop)
            put(at, ALL, done)
            put(at + 1, ALL, done)


def pick(refs, low, high, change=lambda block: block):
    return lambda z: [change(refs[at][one]) for at, one in (low[z], high[z])]


def to_local(at_y, target, rows, values):
    for chunk in range(2 * DEEP):
        place = chunk // 2 + DEEP * lax.rem(chunk + at_y, 2)
        columns = pl.ds(pl.multiple_of(place * LANES, LANES), LANES)
        target[rows, columns] = values[:, chunk * LANES : (chunk + 1) * LANES]


def row_ranges():
    for first in range(0, LENGTH, BLOCK):
        yield first, max(0, first - LENGTH // 2), first + BLOCK


def ordered(ref, which, core, columns):
    half = LENGTH // 2
    start = pl.multiple_of(core * half, half)
    rest = pl.multiple_of((1 - core) * half, half)
    return jnp.concatenate([ref[which, pl.ds(start, half), columns], ref[which, pl.ds(rest, half), columns]], axis=0)


def local_row(first, core):
    return pl.multiple_of(lax.rem(first + core * (LENGTH // 2), LENGTH), BLOCK)


def allowed_tile(meta, first, low, high):
    shape = (BLOCK, high - low)
    places = first + lax.broadcasted_iota(jnp.int32, (BLOCK, 1), 0)
    start = jnp.zeros((BLOCK, 1), jnp.int32)
    for at in range(2, meta.shape[0]):
        start = jnp.where(places >= meta[at], meta[at], start)
    keys = low + lax.broadcasted_iota(jnp.int32, shape, 1)
    return (keys <= places) & (keys >= start)


def first_lanes():
    return lax.broadcasted_iota(jnp.int32, (BLOCK, PAIR), 1) < HEAD_DIM


def attend(meta, qkv, context, logs, put):
    core = meta[0]
    first_head = first_lanes()
    for pair in range(context.shape[1] // PAIR):
        columns = slice(pair * PAIR, (pair + 1) * PAIR)
        keys = ordered(qkv, 1, core, columns)
        values = ordered(qkv, 2, core, columns)
        for first, low, high in row_ranges():
            here = local_row(first, core)
            query = qkv[0, pl.ds(here, BLOCK), columns] * SCALE
            allowed = allowed_tile(meta, first, low, high)
            outs = []
            sums = []
            for head in range(2):
                picked = jnp.where(first_head if head == 0 else ~first_head, query, jnp.zeros_like(query))
                scores = jnp.where(allowed, nt(picked, keys[low:high]), -1e30)
                highest = jnp.max(scores, axis=-1, keepdims=True)
                expos = jnp.exp(scores - highest)
                totals = jnp.sum(expos, axis=-1, keepdims=True)
                outs.append(dot(expos.astype(LOW), values[low:high]) * (1.0 / totals))
                sums.append(highest + jnp.log(totals))
            context[pl.ds(here, BLOCK), columns] = jnp.where(first_head, outs[0], outs[1]).astype(LOW)
            logs[pl.ds(here, BLOCK), columns] = jnp.where(first_head, sums[0], sums[1])
        put(1, ALL, columns)
        put(2, ALL, columns)


def attend_back(meta, qkv, logs, grads, out, sums, key_sum, value_sum):
    core = meta[0]
    first_head = first_lanes()
    half = LENGTH // 2
    for pair in range(grads.shape[1] // PAIR):
        columns = slice(pair * PAIR, (pair + 1) * PAIR)
        keys = ordered(qkv, 1, core, columns)
        values = ordered(qkv, 2, core, columns)
        key_sum[...] = jnp.zeros_like(key_sum)
        value_sum[...] = jnp.zeros_like(value_sum)
        query_total = value_total = jnp.zeros((1, PAIR), FULL)
        for first, low, high in row_ranges():
            here = local_row(first, core)
            query = qkv[0, pl.ds(here, BLOCK), columns] * SCALE
            grad = grads[pl.ds(here, BLOCK), columns]
            log_pair = logs[pl.ds(here, BLOCK), columns]
            allowed = allowed_tile(meta, first, low, high)
            query_flip = query.T
            grad_flip = grad.T
            outs = []
            for head in range(2):
                mask = first_head if head == 0 else ~first_head
                band = slice(head * HEAD_DIM, (head + 1) * HEAD_DIM)
                query_one = jnp.where(mask, query, jnp.zeros_like(query))
                grad_one = jnp.where(mask, grad, jnp.zeros_like(grad))
                log_one = log_pair[:, head * HEAD_DIM : head * HEAD_DIM + 1]
                scores = jnp.where(allowed, nt(query_one, keys[low:high]), -1e30)
                weights = jnp.exp(scores - log_one)
                grad_probs = nt(grad_one, values[low:high])
                inner = jnp.sum(grad_probs * weights, axis=-1, keepdims=True)
                grad_scores = (weights * (grad_probs - inner)).astype(LOW)
                outs.append(dot(grad_scores, keys[low:high]))
                key_sum[band, low:high] += dot(query_flip[band, :], grad_scores)
                value_sum[band, low:high] += dot(grad_flip[band, :], weights.astype(LOW))
            grad_query = (jnp.where(first_head, outs[0], outs[1]) * SCALE).astype(LOW)
            out[0, pl.ds(here, BLOCK), columns] = grad_query
            query_total = query_total + jnp.sum(grad_query.astype(FULL), axis=0, keepdims=True)
        for part in range(2):
            there = pl.multiple_of(lax.rem(part + core, 2) * half, half)
            out[1, pl.ds(there, half), columns] = key_sum[:, part * half : (part + 1) * half].T.astype(LOW)
            grad_value = value_sum[:, part * half : (part + 1) * half].T.astype(LOW)
            out[2, pl.ds(there, half), columns] = grad_value
            value_total = value_total + jnp.sum(grad_value.astype(FULL), axis=0, keepdims=True)
        sums[0:1, columns] = query_total
        sums[1:2, columns] = value_total


def attention_forward(meta, normed, sides, biases, last=None):
    ops = Operands()
    normed_at = [ops.add(normed[0])]
    sides_at = [[ops.side(one) for one in pair] for pair in sides]
    bias_at = ops.add(biases)
    normed_at.append(ops.add(normed[1]))
    width = sides[0][0][0][0].shape[-1]
    rows, wide = normed[0].shape
    outs = [like((3, LENGTH, width), LOW), like((LENGTH, width), LOW), like((LENGTH, width), FULL)]
    if last:
        first_at = ops.add(last[0])
        out_sides = [[ops.side(one) for one in pair] for pair in last[1]]
        outs += [like((rows, wide), FULL), like((rows, wide), LOW)]

    def kernel(meta, refs, results, put):
        qkv, context, logs = results[:3]
        for which, (low, high) in enumerate(sides_at):
            low_w = high_w = None
            for here, block in zip(row_slices(), rows_of(refs, normed_at)):
                if low_w is None:
                    low_w, high_w = tall(refs, low), tall(refs, high)
                total = dot(block[:, :HALF], low_w) + dot(block[:, HALF:], high_w)
                if which != 1:
                    total = total + refs[bias_at][:, which // 2 * width : (which // 2 + 1) * width]
                qkv[which, here, :] = total.astype(LOW)
        put(0)
        attend(meta, qkv, context, logs, put)
        if last:
            terms = [
                (lambda block, left=left: left[row_slices()[block], :], pick(refs, *pair, unfold), dot)
                for left, pair in zip((refs[first_at], context), out_sides)
            ]
            spread(meta[1] == 0, terms, *results[3:], put, 3)

    return call(kernel, meta, ops, outs, time=12 if last else 8)


def attention_backward(meta, grad, side, qkv, logs, context, normed):
    ops = Operands()
    grad_at = [ops.add(grad[0])]
    low, high = [ops.side(one) for one in side]
    grad_at.append(ops.add(grad[1]))
    qkv_at, log_at = [ops.add(one) for one in (qkv, logs)]
    normed_at = [ops.add(one) for one in normed]
    context_at = ops.add(context)
    width = context.shape[1]
    blocks = like((DEEP, 2, LANES, width), LOW)

    def kernel(meta, refs, results, put, grads, key_sum, value_sum):
        out, sums = results[:2]
        low_w = high_w = None
        for here, block in zip(row_slices(), rows_of(refs, grad_at)):
            if low_w is None:
                low_w, high_w = [
                    jnp.concatenate([unfold(refs[at][index]) for at, index in one], axis=1) for one in (low, high)
                ]
            grads[here, :] = (nt(block[:, :HALF], low_w) + nt(block[:, HALF:], high_w)).astype(LOW)
        attend_back(meta, refs[qkv_at], refs[log_at], grads, out, sums, key_sum, value_sum)
        put(0)
        put(1)
        for which in range(3):
            right = [out[which, here, :] for here in row_slices()]
            for places, columns in chunk_pairs():
                block = by_tokens(rows_of(refs, normed_at, columns), right)
                for part, place in enumerate(places):
                    target = results[2 + which // 2 + 2 * (place // DEEP)]
                    target[place % DEEP, which % 2] = block[part * LANES : (part + 1) * LANES, :]
            if which == 1:
                put(2)
                put(4)
        left = [refs[context_at][here, :] for here in row_slices()]
        for places, columns in chunk_pairs():
            block = by_tokens(left, rows_of(refs, grad_at, columns))
            for part, place in enumerate(places):
                target = results[3 + 2 * (place // DEEP)]
                one = block[:, part * LANES : (part + 1) * LANES]
                target[place % DEEP, 1] = jnp.concatenate([one[:LANES], one[LANES:]], axis=1)
        put(3)
        put(5)

    return call(
        kernel,
        meta,
        ops,
        [like((3, LENGTH, width), LOW), like((2, width), FULL)] + [blocks] * 4,
        [pltpu.VMEM((LENGTH, width), LOW)] + [pltpu.VMEM((PAIR, LENGTH), FULL)] * 2,
        time=15,
    )


def unit_tiles(width):
    for first in range(0, width, BLOCK):
        stop = first + BLOCK
        yield slice(first, stop), slice(stop - width // 2, stop) if stop % (width // 2) == 0 else None


def up_kernel(meta, normed, side, biases, at, cot):
    ops = Operands()
    normed_at = [ops.add(normed[0])]
    low, high = [ops.side(one) for one in side]
    bias_at = ops.add(biases)
    normed_at.append(ops.add(normed[1]))
    cot_at = [ops.add(one) for one in cot]
    width = side[0][0][0].shape[-1]
    blocks = like((DEEP, width, LANES), LOW)

    def kernel(meta, refs, results, put):
        active, slope = results[:2]
        for units, done in unit_tiles(width):
            low_w = high_w = None
            for here, block in zip(row_slices(), rows_of(refs, normed_at)):
                if low_w is None:
                    low_w, high_w = tall(refs, low, units), tall(refs, high, units)
                before = dot(block[:, :HALF], low_w) + dot(block[:, HALF:], high_w)
                before = before + refs[bias_at][:, at + units.start : at + units.stop]
                phi = 0.5 * (1.0 + lax.erf(before * (2.0**-0.5)))
                active[here, units] = (before * phi).astype(LOW)
                bell = jnp.exp(-0.5 * before * before) * (2.0 * jnp.pi) ** -0.5
                slope[here, units] = (phi + before * bell).astype(LOW)
            left = [active[here, units] for here in row_slices()]
            for places, chunks in chunk_pairs():
                block = by_tokens(left, rows_of(refs, cot_at, chunks))
                for part, place in enumerate(places):
                    results[2 + place // DEEP][place % DEEP, units, :] = block[:, part * LANES : (part + 1) * LANES]
            if done:
                for one in range(4):
                    put(one, ALL, done)

    return call(kernel, meta, ops, [like((LENGTH, width), LOW)] * 2 + [blocks] * 2, time=9)


def down_kernel(meta, cot, side, slope, normed, last=None):
    ops = Operands()
    rows, wide = normed[0].shape
    width = slope.shape[1]
    cot_at = [ops.add(cot[0])]
    low, high = [ops.side(one) for one in side]
    slope_at = ops.add(slope)
    cot_at.append(ops.add(cot[1]))
    normed_at = [ops.add(one) for one in normed]
    outs = [like((LENGTH, width), LOW), like((1, width), FULL)] + [like((2, LANES, width), LOW)] * 4
    if last:
        first_at = ops.add(last[0])
        up_sides = [[ops.side(one) for one in pair] for pair in last[1]]
        outs += [like((rows, wide), FULL), like((rows, wide), LOW)]

    def kernel(meta, refs, results, put):
        grads, sums = results[:2]
        for units, done in unit_tiles(width):
            total = jnp.zeros((1, BLOCK), FULL)
            low_w = high_w = None
            for here, block in zip(row_slices(), rows_of(refs, cot_at)):
                if low_w is None:
                    low_w, high_w = flat(refs, low, units), flat(refs, high, units)
                grad = nt(block[:, :HALF], low_w) + nt(block[:, HALF:], high_w)
                grad = (grad * refs[slope_at][here, units].astype(FULL)).astype(LOW)
                grads[here, units] = grad
                total = total + jnp.sum(grad.astype(FULL), axis=0, keepdims=True)
            sums[:, units] = total
            right = [grads[here, units] for here in row_slices()]
            for places, chunks in chunk_pairs():
                block = by_tokens(rows_of(refs, normed_at, chunks), right)
                for part, place in enumerate(places):
                    results[2 + place // 2][place % 2, :, units] = block[part * LANES : (part + 1) * LANES, :]
            if done:
                put(0, ALL, done)
                for one in range(2, 6):
                    put(one, ALL, ALL, done)
        put(1)
        if last:
            terms = [
                (lambda block, left=left: left[row_slices()[block], :], pick(refs, *pair), nt)
                for left, pair in zip((refs[first_at], grads), up_sides)
            ]
            spread(meta[1] == 0, terms, *results[6:], put, 6)

    return call(kernel, meta, ops, outs, time=12 if last else 7)


def spread_kernel(meta, terms, rows, wide, product):
    ops = Operands()
    places = [(ops.add(left), at, ops.side(low), ops.side(high)) for left, at, low, high in terms]

    def kernel(meta, refs, results, put):
        def left_of(one, at):
            index = () if at is None else (at,)
            return lambda block: refs[one][(*index, row_slices()[block])]

        parts = [(left_of(one, at), pick(refs, low, high), product) for one, at, low, high in places]
        spread(meta[1] == 0, parts, *results, put, 0)

    return call(kernel, meta, ops, [like((rows, wide), FULL), like((rows, wide), LOW)], time=6)


STRIP = 128


def normalize(values):
    center = values - jnp.mean(values, axis=-1, keepdims=True)
    spread_ = jnp.mean(center * center, axis=-1, keepdims=True)
    rate = lax.rsqrt(spread_ + EPSILON)
    return center * rate, rate


def strips(rows):
    return [slice(first, first + STRIP) for first in range(0, rows, STRIP)]


def by_strips(kernel, meta, arrays, vectors, outs, sums=0):
    ops = Operands()
    rows, wide = arrays[0].shape
    halves = [slice(0, rows // 2), slice(rows // 2, rows)]
    first = [ops.add(array, halves[0]) for array in arrays]
    vector_at = [ops.add(one) for one in vectors]
    places = [first, [ops.add(array, halves[1]) for array in arrays]]
    shapes = [like((rows, wide), kind) for kind in outs]
    if sums:
        shapes.append(like((sums, wide), FULL))

    def body(meta, refs, results, put):
        parts = [None] * sums
        for at, half in zip(places, halves):
            for here in strips(rows // 2):
                kernel(
                    meta,
                    [refs[one][here, :] for one in at],
                    [refs[one][...] for one in vector_at],
                    [(result, slice(half.start + here.start, half.start + here.stop)) for result in results[: len(outs)]],
                    parts,
                )
            for one in range(len(outs)):
                put(one, half)
        if sums:
            for at, value in enumerate(parts):
                results[-1][at : at + 1, :] = jnp.sum(value, axis=0, keepdims=True)
            put(len(outs))

    return call(body, meta, ops, shapes, time=4)


def start_kernel(meta, values, vectors, results, sums):
    tokens, cot = values
    gain, shift = vectors
    hat, _ = normalize(tokens.astype(FULL))
    to_local(meta[1], *results[0], (hat * gain + shift).astype(LOW))
    to_local(meta[1], *results[1], cot.astype(LOW))


def join_kernel(meta, values, vectors, results, sums):
    tokens, own, got = values
    bias, gain, shift = vectors
    total = tokens.astype(FULL) + (own + got.astype(FULL)) + bias
    hidden, here = results[0]
    hidden[here, :] = total
    hat, _ = normalize(total)
    to_local(meta[1], *results[1], (hat * gain + shift).astype(LOW))


def add_sums(sums, values):
    for at, value in enumerate(values):
        part = jnp.sum(value.reshape(STRIP // 8, 8, value.shape[1]), axis=0)
        sums[at] = part if sums[at] is None else sums[at] + part


def norm_back(grad, values, gain):
    hat, rate = normalize(values)
    scaled = grad * gain
    row = rate * (
        scaled
        - jnp.mean(scaled, axis=-1, keepdims=True)
        - hat * jnp.mean(scaled * hat, axis=-1, keepdims=True)
    )
    return row, grad * hat


def second_kernel(meta, values, vectors, results, sums):
    own, got, hidden, pulled = values
    grad = own + got.astype(FULL)
    row, gain_part = norm_back(grad, hidden, vectors[0])
    total = pulled + row
    out, here = results[0]
    out[here, :] = total
    to_local(meta[1], *results[1], total.astype(LOW))
    add_sums(sums, [gain_part, grad, total, pulled])


def first_kernel(meta, values, vectors, results, sums):
    own, got, tokens, hidden_grad = values
    grad = own + got.astype(FULL)
    row, gain_part = norm_back(grad, tokens.astype(FULL), vectors[0])
    out, here = results[0]
    out[here, :] = hidden_grad + row
    add_sums(sums, [gain_part, grad])


def end_kernel(meta, values, vectors, results, sums):
    hidden, own, got = values
    out, here = results[0]
    out[here, :] = (hidden + (own + got.astype(FULL)) + vectors[0]).astype(LOW)


def wide_shard(shard, axis):
    return lax.all_gather(shard, "w", axis=axis, tiled=True) if lax.axis_size("w") > 1 else shard


def gather_deep(shard):
    return lax.all_gather(shard, "z", axis=0, tiled=False)


def add(*values):
    total = values[0].astype(FULL)
    for value in values[1:]:
        total = total + value.astype(FULL)
    return total.astype(LOW)


def scatter_deep(total):
    total = lax.psum_scatter(total, "z", scatter_dimension=0, tiled=False)
    if lax.axis_size("w") > 1:
        total = lax.psum_scatter(total, "w", scatter_dimension=total.ndim - 2, tiled=True)
    return total.astype(FULL)


def on_device(
    inputs,
    doc_lengths,
    first_gain,
    first_bias,
    w_query,
    b_query,
    w_key,
    w_value,
    b_value,
    w_out,
    b_out,
    second_gain,
    second_bias,
    w_up,
    b_up,
    w_down,
    b_down,
    cotangent,
):
    rows, wide = inputs.shape
    here = w_query.shape[1]
    core = lax.axis_index("c").astype(jnp.int32)
    at_y = lax.axis_index("y").astype(jnp.int32)
    at_x = lax.axis_index("x")
    lengths = lax.dynamic_index_in_dim(doc_lengths, at_x, 0, keepdims=False)
    ends = [lengths[0]]
    for one in range(1, lengths.shape[0]):
        ends.append(ends[-1] + lengths[one])
    meta = jnp.stack([core, at_y, *ends])

    def line(vector):
        return vector.reshape(1, -1)

    out_shard = wide_shard(w_out, 1)
    out_shard = jnp.concatenate([out_shard[: here // 2], out_shard[here // 2 :]], axis=1)
    attn_shard = jnp.stack([wide_shard(w_query, 0), wide_shard(w_key, 0), wide_shard(w_value, 0), out_shard])
    up_shard = wide_shard(w_up, 0)
    down_shard = wide_shard(w_down, 1)
    biases = line(jnp.concatenate([b_query, b_value, b_up]))
    far = swap(biases, "x")
    down_raw = swap_both(down_shard)
    attn_mine = after(gather_deep(attn_shard), down_raw, far)
    attn_x = swap(attn_mine, "x")
    attn_y = swap(attn_mine, "y")
    attn_qk = swap(attn_y[:, :2], "x")
    attn_vo = swap(attn_x[:, 2:], "y")


    normed, cot = by_strips(start_kernel, meta, [inputs, cotangent], [line(first_gain), line(first_bias)], [LOW, LOW])
    normed = (normed, swap(normed, "c"))
    cot = (cot, swap(cot, "c"))

    attn_sides = [
        [(stacked_side(attn_mine, which), stacked_side(attn_y, which)) for which in range(4)],
        [
            (stacked_side(attn_x, which), stacked_side((attn_qk, attn_vo)[which // 2], which % 2))
            for which in range(4)
        ],
    ]

    qkv, context, logs = [None] * 2, [None] * 2, [None] * 2
    qkv[0], context[0], logs[0] = attention_forward(meta, normed, attn_sides[0][:3], biases)

    half = DEEP // 2
    up_mine = after(gather_deep(up_shard), context[0])
    up_parts = [up_mine[:half], up_mine[half:]]
    up_x = [swap(up_parts[0], "x"), None]
    up_y = [swap(up_parts[0], "y"), None]

    qkv[1], context[1], logs[1], own, sent = attention_forward(
        meta,
        normed,
        attn_sides[1][:3],
        far,
        (context[0], [attn_sides[0][3], attn_sides[1][3]]),
    )
    up_next = after(up_parts[1], sent)
    up_x[1], up_y[1] = swap(up_next, "x"), swap(up_next, "y")
    sent = after(sent, up_x[0], up_y[0])
    hidden, normed_two = by_strips(
        join_kernel,
        meta,
        [inputs, own, swap(sent, "c")],
        [line(b_out), line(second_gain), line(second_bias)],
        [FULL, LOW],
    )
    normed_two = (normed_two, swap(after(normed_two, up_x[1], up_y[1]), "c"))

    up_far = [swap(up_y[0], "x"), swap(up_x[1], "y")]
    up_sides = [
        (whole_side(up_mine), split_side(*up_y)),
        (split_side(*up_x), split_side(*up_far)),
    ]
    active, slope, down_own, down_far = [None] * 2, [None] * 2, [None] * 2, [None] * 2
    active[0], slope[0], down_own[0], down_far[0] = up_kernel(
        meta, normed_two, up_sides[0], biases, 2 * here, cot
    )

    down_mine = after(gather_deep(down_shard), *up_far, active[0])
    down_x = swap(down_mine, "x")
    down_y = swap(down_mine, "y")
    down_both = gather_deep(down_raw)
    down_sides = [
        (whole_side(down_mine), whole_side(down_y)),
        (whole_side(down_x), whole_side(down_both)),
    ]
    active[1], slope[1], down_own[1], down_far[1] = up_kernel(
        meta, (after(normed_two[0], active[0]), normed_two[1]), up_sides[1], far, 2 * here, cot
    )

    grads, sums = [None] * 2, [None] * 2
    grads[0], sums[0], *up_parts = down_kernel(
        meta, (after(cot[0], active[1]), cot[1]), down_sides[0], slope[0], normed_two
    )
    up_own = up_parts[:2]
    up_beyond = up_parts[2:]
    grads[1], sums[1], *up_parts, own, sent = down_kernel(
        meta, cot, down_sides[1], slope[1], normed_two, (grads[0], up_sides)
    )
    up_other = up_parts[:2]
    up_both = up_parts[2:]

    down_diagonal = swap_both(lax.psum_scatter(down_far[1], "z", scatter_dimension=0, tiled=False))
    down_total = add(
        down_own[0], swap(after(down_far[0], down_x, down_y), "y"), swap(after(down_own[1], down_x, down_y), "x")
    )
    owner_down = lax.psum_scatter(down_total, "z", scatter_dimension=0, tiled=False)
    owner_down = owner_down.astype(FULL) + down_diagonal.astype(FULL)
    if lax.axis_size("w") > 1:
        owner_down = lax.psum_scatter(owner_down, "w", scatter_dimension=1, tiled=True)

    got_low = swap(up_both[0], "x")
    got_high = swap(up_both[1], "y")
    got_x = [swap(up_other[0], "x"), None]
    got_y = [None, swap(up_beyond[1], "y")]

    hidden_grad, attn_grad, second_sums = by_strips(
        second_kernel, meta, [own, swap(sent, "c"), hidden, cotangent], [line(second_gain)], [FULL, LOW], sums=4
    )
    attn_grad = (attn_grad, swap(attn_grad, "c"))

    got_y[0] = swap(add(up_beyond[0], after(got_low, attn_grad[0])), "y")
    got_x[1] = swap(add(up_other[1], after(got_high, attn_grad[0])), "x")

    back, unit_sums = [None] * 2, [None] * 2
    back[1], unit_sums[1], other_qk, other_vo, both_qk, both_vo = attention_backward(
        meta, attn_grad, attn_sides[1][3], qkv[1], logs[1], context[1], normed
    )
    got_qk = swap(both_qk, "x")
    got_vo = swap(both_vo, "y")
    x_qk = swap(other_qk, "x")
    got_x, got_y = [[after(one, back[1]) for one in parts] for parts in (got_x, got_y)]
    up_total = jnp.concatenate([add(up_own[part], got_x[part], got_y[part]) for part in range(2)])
    owner_up = scatter_deep(up_total)
    back[0], unit_sums[0], own_qk, own_vo, far_qk, far_vo = attention_backward(
        meta, (after(attn_grad[0], back[1]), attn_grad[1]), attn_sides[0][3], qkv[0], logs[0], context[0], normed
    )
    y_vo = swap(far_vo, "y")
    x_vo = swap(add(other_vo, after(got_vo, back[0])), "x")
    y_qk = swap(add(far_qk, after(got_qk, back[0])), "y")
    attn_total = jnp.concatenate([add(own_qk, x_qk, y_qk), add(own_vo, x_vo, y_vo)], axis=1)
    owner_attn = lax.psum_scatter(attn_total, "z", scatter_dimension=0, tiled=False)
    owner_out = owner_attn[3].astype(FULL)
    owner_out = jnp.concatenate([owner_out[:, :LANES], owner_out[:, LANES:]])
    owner_attn = owner_attn[:3].astype(FULL)
    if lax.axis_size("w") > 1:
        owner_attn = lax.psum_scatter(owner_attn, "w", scatter_dimension=1, tiled=True)
        owner_out = lax.psum_scatter(owner_out, "w", scatter_dimension=1, tiled=True)

    own, sent = spread_kernel(
        meta,
        [(back[x], which, *attn_sides[x][which]) for x in range(2) for which in range(3)],
        rows,
        wide,
        nt,
    )
    input_grad, first_sums = by_strips(
        first_kernel, meta, [own, swap(sent, "c"), inputs, hidden_grad], [line(first_gain)], [FULL], sums=2
    )

    later = after(active[0], input_grad)
    own, sent = spread_kernel(
        meta, [(later, None, *down_sides[0]), (active[1], None, *down_sides[1])], rows, wide, dot
    )
    [layer_out] = by_strips(end_kernel, meta, [hidden, own, swap(sent, "c")], [line(b_down)], [LOW])

    replicated = all_sum(jnp.concatenate([first_sums, second_sums]).reshape(-1), "c")
    own_units, far_units = [
        jnp.concatenate([unit_sums[x][0], unit_sums[x][1], sums[x][0]]) for x in range(2)
    ]
    got = swap(jnp.concatenate([replicated, far_units]), "x")
    summed = jnp.concatenate([replicated, own_units]) + got
    for axis in ("y", "z", "w"):
        summed = all_sum(summed, axis)
    vectors = summed[: 6 * wide].reshape(6, wide)
    units = summed[6 * wide :]

    return (
        layer_out,
        input_grad,
        vectors[0],
        vectors[1],
        owner_attn[0],
        units[:here],
        owner_attn[1],
        owner_attn[2],
        units[here : 2 * here],
        owner_out,
        vectors[4],
        vectors[2],
        vectors[3],
        owner_up,
        units[2 * here :],
        owner_down,
        vectors[5],
    )


def solution(mesh):
    groups, lanes = mesh.shape["fsdp"], mesh.shape["tp"]
    inner = Mesh(
        mesh.devices.reshape(DEEP, 2, groups // (2 * DEEP), lanes // 2, 2), ("z", "y", "w", "x", "c")
    )
    f, t = ("z", "y", "w"), ("x", "c")
    tokens, rows, columns, units = P(f + t, None), P(f, t), P(t, f), P(t)
    return jax.shard_map(
        on_device,
        mesh=inner,
        in_specs=(
            tokens,
            P(f, None),
            P(),
            P(),
            rows,
            units,
            rows,
            rows,
            units,
            columns,
            P(),
            P(),
            P(),
            rows,
            units,
            columns,
            P(),
            tokens,
        ),
        out_specs=(
            tokens,
            tokens,
            P(),
            P(),
            rows,
            units,
            rows,
            rows,
            units,
            columns,
            P(),
            P(),
            P(),
            rows,
            units,
            columns,
            P(),
        ),
        check_vma=False,
    )
```

```python
import jax
import jax.numpy as jnp
from jax import lax
from jax.experimental import pallas as pl
from jax.experimental.pallas import tpu as pltpu
from jax.sharding import Mesh, PartitionSpec as P

HEAD_DIM = 64
LENGTH = 1024
BLOCK = 256
PAIR = 2 * HEAD_DIM
EPSILON = 1e-05
SCALE = HEAD_DIM**-0.5
LOW = jnp.bfloat16
FULL = jnp.float32
SWAP = ((0, 1), (1, 0))
DEEP = 4
LANES = 128
HALF = DEEP * LANES


def swap(values, axis):
    return lax.ppermute(values, axis, SWAP)


def swap_both(values):
    return lax.ppermute(values, ("y", "x"), ((0, 3), (1, 2), (2, 1), (3, 0)))


def all_sum(values, axis):
    size, step = lax.axis_size(axis), 1
    while step < size:
        values = values + lax.ppermute(values, axis, [(i, i ^ step) for i in range(size)])
        step *= 2
    return values


def after(values, *others):
    return lax.optimization_barrier((values, *others))[0]


def like(shape, kind):
    return jax.ShapeDtypeStruct(shape, kind)


ALL = slice(None)


ALL = slice(None)


class Operands:
    def __init__(self):
        self.parts = []

    def add(self, array, *index):
        for at, (one, where) in enumerate(self.parts):
            if one is array and where == index:
                return at
        self.parts.append((array, index))
        return len(self.parts) - 1

    def side(self, blocks):
        return [(self.add(array), index) for array, index in blocks]


class Buffers:
    def __init__(self, buffers, copies):
        self.buffers, self.copies = buffers, dict(enumerate(copies))

    def __getitem__(self, at):
        if at in self.copies:
            self.copies.pop(at).wait()
        return self.buffers[at]


def call(kernel, meta, ops, outs, scratch=(), time=3, limit=60):
    arrays = []
    for array, _ in ops.parts:
        if not any(array is one for one in arrays):
            arrays.append(array)
    source = [next(at for at, one in enumerate(arrays) if one is array) for array, _ in ops.parts]
    blocks = [jax.eval_shape(lambda a, index=index: a[index], like(array.shape, array.dtype)) for array, index in ops.parts]
    count, parts, results = len(arrays), len(ops.parts), len(outs)

    def body(*refs):
        meta_ref, sources, targets = refs[0], refs[1 : 1 + count], refs[1 + count : 1 + count + results]
        rest = refs[1 + count + results :]
        buffers, copies = rest[:parts], rest[parts : parts + results]
        in_sems, out_sems, *extra = rest[parts + results :]
        fetches = []
        for at, (_, index) in enumerate(ops.parts):
            ref = sources[source[at]]
            fetches.append(pltpu.make_async_copy(ref.at[index] if index else ref, buffers[at], in_sems.at[at]))
            fetches[-1].start()
        sent = []

        def put(at, *index):
            one, two = (copies[at].at[index], targets[at].at[index]) if index else (copies[at], targets[at])
            sent.append(pltpu.make_async_copy(one, two, out_sems.at[len(sent)]))
            sent[-1].start()

        kernel(meta_ref, Buffers(buffers, fetches), copies, put, *extra)
        for one in sent:
            one.wait()

    whole = pl.BlockSpec(memory_space=pl.ANY)
    return pl.pallas_call(
        body,
        out_shape=outs,
        in_specs=[pl.BlockSpec(memory_space=pltpu.SMEM)] + [whole] * count,
        out_specs=[whole] * results,
        scratch_shapes=[pltpu.VMEM(one.shape, one.dtype) for one in blocks]
        + [pltpu.VMEM(one.shape, one.dtype) for one in outs]
        + [pltpu.SemaphoreType.DMA((parts,)), pltpu.SemaphoreType.DMA((64,))]
        + list(scratch),
        compiler_params=pltpu.CompilerParams(vmem_limit_bytes=limit << 20),
        cost_estimate=pl.CostEstimate(flops=time << 20, bytes_accessed=1 << 16, transcendentals=0),
    )(meta, *arrays)


def whole_side(array):
    return [(array, (z,)) for z in range(DEEP)]


def stacked_side(array, which):
    return [(array, (z, which)) for z in range(DEEP)]


def split_side(low, high):
    return [((low, high)[z // 2], (z % 2,)) for z in range(DEEP)]


def dot(left, right):
    return jnp.dot(left, right, preferred_element_type=FULL)


def nt(left, right):
    return lax.dot_general(left, right, (((1,), (1,)), ((), ())), preferred_element_type=FULL)


def tn(left, right):
    return lax.dot_general(left, right, (((0,), (0,)), ((), ())), preferred_element_type=FULL)


def tall(refs, side, units=ALL):
    return jnp.concatenate([refs[at][(*index, ALL, units)] for at, index in side], axis=0)


def flat(refs, side, units):
    return jnp.concatenate([refs[at][(*index, units)] for at, index in side], axis=1)


def unfold(block):
    return jnp.concatenate([block[:, :LANES], block[:, LANES:]], axis=0)


def row_slices(count=LENGTH // BLOCK):
    return [slice(at * BLOCK, (at + 1) * BLOCK) for at in range(count)]


def rows_of(refs, pair, columns=ALL):
    for at in pair:
        for first in range(0, refs[at].shape[0], BLOCK):
            yield refs[at][first : first + BLOCK, columns]


def chunk_pairs():
    for first in range(0, 2 * DEEP, 2):
        yield (first, first + 1), slice(first * LANES, (first + 2) * LANES)


def by_tokens(lefts, rights):
    total = None
    for left, right in zip(lefts, rights):
        part = tn(left, right)
        total = part if total is None else total + part
    return total.astype(LOW)


def spread(even, terms, own, far, put, at):
    rows = own.shape[0]
    for z in range(DEEP):
        columns = slice(2 * z * LANES, 2 * (z + 1) * LANES)
        rights = []
        for _, chunks, product in terms:
            one, two = chunks(z)
            pair = [jnp.where(even, one, two), jnp.where(even, two, one)]
            rights.append(jnp.concatenate(pair, axis=0 if product is nt else 1))
        for block, here in enumerate(row_slices()):
            total = None
            for (left, _, product), right in zip(terms, rights):
                part = product(left(block), right)
                total = part if total is None else total + part
            if here.start < rows:
                own[here, columns] = total
            else:
                far[here.start - rows : here.stop - rows, columns] = total.astype(LOW)
        if z % 2:
            done = slice(columns.stop - 4 * LANES, columns.stop)
            put(at, ALL, done)
            put(at + 1, ALL, done)


def pick(refs, low, high, change=lambda block: block):
    return lambda z: [change(refs[at][one]) for at, one in (low[z], high[z])]


def to_local(at_y, target, rows, values):
    for chunk in range(2 * DEEP):
        place = chunk // 2 + DEEP * lax.rem(chunk + at_y, 2)
        columns = pl.ds(pl.multiple_of(place * LANES, LANES), LANES)
        target[rows, columns] = values[:, chunk * LANES : (chunk + 1) * LANES]


def row_ranges():
    for first in range(0, LENGTH, BLOCK):
        yield first, max(0, first - LENGTH // 2), first + BLOCK


def ordered(ref, which, core, columns):
    half = LENGTH // 2
    start = pl.multiple_of(core * half, half)
    rest = pl.multiple_of((1 - core) * half, half)
    return jnp.concatenate([ref[which, pl.ds(start, half), columns], ref[which, pl.ds(rest, half), columns]], axis=0)


def local_row(first, core):
    return pl.multiple_of(lax.rem(first + core * (LENGTH // 2), LENGTH), BLOCK)


def allowed_tile(meta, first, low, high):
    shape = (BLOCK, high - low)
    places = first + lax.broadcasted_iota(jnp.int32, (BLOCK, 1), 0)
    start = jnp.zeros((BLOCK, 1), jnp.int32)
    for at in range(2, meta.shape[0]):
        start = jnp.where(places >= meta[at], meta[at], start)
    keys = low + lax.broadcasted_iota(jnp.int32, shape, 1)
    return (keys <= places) & (keys >= start)


def first_lanes():
    return lax.broadcasted_iota(jnp.int32, (BLOCK, PAIR), 1) < HEAD_DIM


def attend(meta, qkv, context, logs, put):
    core = meta[0]
    first_head = first_lanes()
    for pair in range(context.shape[1] // PAIR):
        columns = slice(pair * PAIR, (pair + 1) * PAIR)
        keys = ordered(qkv, 1, core, columns)
        values = ordered(qkv, 2, core, columns)
        for first, low, high in row_ranges():
            here = local_row(first, core)
            query = qkv[0, pl.ds(here, BLOCK), columns] * SCALE
            allowed = allowed_tile(meta, first, low, high)
            outs = []
            sums = []
            for head in range(2):
                picked = jnp.where(first_head if head == 0 else ~first_head, query, jnp.zeros_like(query))
                scores = jnp.where(allowed, nt(picked, keys[low:high]), -1e30)
                highest = jnp.max(scores, axis=-1, keepdims=True)
                expos = jnp.exp(scores - highest)
                totals = jnp.sum(expos, axis=-1, keepdims=True)
                outs.append(dot(expos.astype(LOW), values[low:high]) * (1.0 / totals))
                sums.append(highest + jnp.log(totals))
            context[pl.ds(here, BLOCK), columns] = jnp.where(first_head, outs[0], outs[1]).astype(LOW)
            logs[pl.ds(here, BLOCK), columns] = jnp.where(first_head, sums[0], sums[1])
        put(1, ALL, columns)
        put(2, ALL, columns)


def attend_back(meta, qkv, logs, grads, out, sums, key_sum, value_sum):
    core = meta[0]
    first_head = first_lanes()
    half = LENGTH // 2
    for pair in range(grads.shape[1] // PAIR):
        columns = slice(pair * PAIR, (pair + 1) * PAIR)
        keys = ordered(qkv, 1, core, columns)
        values = ordered(qkv, 2, core, columns)
        key_sum[...] = jnp.zeros_like(key_sum)
        value_sum[...] = jnp.zeros_like(value_sum)
        query_total = value_total = jnp.zeros((1, PAIR), FULL)
        for first, low, high in row_ranges():
            here = local_row(first, core)
            query = qkv[0, pl.ds(here, BLOCK), columns] * SCALE
            grad = grads[pl.ds(here, BLOCK), columns]
            log_pair = logs[pl.ds(here, BLOCK), columns]
            allowed = allowed_tile(meta, first, low, high)
            query_flip = query.T
            grad_flip = grad.T
            outs = []
            for head in range(2):
                mask = first_head if head == 0 else ~first_head
                band = slice(head * HEAD_DIM, (head + 1) * HEAD_DIM)
                query_one = jnp.where(mask, query, jnp.zeros_like(query))
                grad_one = jnp.where(mask, grad, jnp.zeros_like(grad))
                log_one = log_pair[:, head * HEAD_DIM : head * HEAD_DIM + 1]
                scores = jnp.where(allowed, nt(query_one, keys[low:high]), -1e30)
                weights = jnp.exp(scores - log_one)
                grad_probs = nt(grad_one, values[low:high])
                inner = jnp.sum(grad_probs * weights, axis=-1, keepdims=True)
                grad_scores = (weights * (grad_probs - inner)).astype(LOW)
                outs.append(dot(grad_scores, keys[low:high]))
                key_sum[band, low:high] += dot(query_flip[band, :], grad_scores)
                value_sum[band, low:high] += dot(grad_flip[band, :], weights.astype(LOW))
            grad_query = (jnp.where(first_head, outs[0], outs[1]) * SCALE).astype(LOW)
            out[0, pl.ds(here, BLOCK), columns] = grad_query
            query_total = query_total + jnp.sum(grad_query.astype(FULL), axis=0, keepdims=True)
        for part in range(2):
            there = pl.multiple_of(lax.rem(part + core, 2) * half, half)
            out[1, pl.ds(there, half), columns] = key_sum[:, part * half : (part + 1) * half].T.astype(LOW)
            grad_value = value_sum[:, part * half : (part + 1) * half].T.astype(LOW)
            out[2, pl.ds(there, half), columns] = grad_value
            value_total = value_total + jnp.sum(grad_value.astype(FULL), axis=0, keepdims=True)
        sums[0:1, columns] = query_total
        sums[1:2, columns] = value_total


def attention_forward(meta, normed, sides, biases, last=None):
    ops = Operands()
    normed_at = [ops.add(normed[0])]
    sides_at = [[ops.side(one) for one in pair] for pair in sides]
    bias_at = ops.add(biases)
    normed_at.append(ops.add(normed[1]))
    width = sides[0][0][0][0].shape[-1]
    rows, wide = normed[0].shape
    outs = [like((3, LENGTH, width), LOW), like((LENGTH, width), LOW), like((LENGTH, width), FULL)]
    if last:
        first_at = ops.add(last[0])
        out_sides = [[ops.side(one) for one in pair] for pair in last[1]]
        outs += [like((rows, wide), FULL), like((rows, wide), LOW)]

    def kernel(meta, refs, results, put):
        qkv, context, logs = results[:3]
        for which, (low, high) in enumerate(sides_at):
            low_w = high_w = None
            for here, block in zip(row_slices(), rows_of(refs, normed_at)):
                if low_w is None:
                    low_w, high_w = tall(refs, low), tall(refs, high)
                total = dot(block[:, :HALF], low_w) + dot(block[:, HALF:], high_w)
                if which != 1:
                    total = total + refs[bias_at][:, which // 2 * width : (which // 2 + 1) * width]
                qkv[which, here, :] = total.astype(LOW)
        put(0)
        attend(meta, qkv, context, logs, put)
        if last:
            terms = [
                (lambda block, left=left: left[row_slices()[block], :], pick(refs, *pair, unfold), dot)
                for left, pair in zip((refs[first_at], context), out_sides)
            ]
            spread(meta[1] == 0, terms, *results[3:], put, 3)

    return call(kernel, meta, ops, outs, time=12 if last else 8)


def attention_backward(meta, grad, side, qkv, logs, context, normed):
    ops = Operands()
    grad_at = [ops.add(grad[0])]
    low, high = [ops.side(one) for one in side]
    grad_at.append(ops.add(grad[1]))
    qkv_at, log_at = [ops.add(one) for one in (qkv, logs)]
    normed_at = [ops.add(one) for one in normed]
    context_at = ops.add(context)
    width = context.shape[1]
    blocks = like((DEEP, 2, LANES, width), LOW)

    def kernel(meta, refs, results, put, grads, key_sum, value_sum):
        out, sums = results[:2]
        low_w = high_w = None
        for here, block in zip(row_slices(), rows_of(refs, grad_at)):
            if low_w is None:
                low_w, high_w = [
                    jnp.concatenate([unfold(refs[at][index]) for at, index in one], axis=1) for one in (low, high)
                ]
            grads[here, :] = (nt(block[:, :HALF], low_w) + nt(block[:, HALF:], high_w)).astype(LOW)
        attend_back(meta, refs[qkv_at], refs[log_at], grads, out, sums, key_sum, value_sum)
        put(0)
        put(1)
        for which in range(3):
            right = [out[which, here, :] for here in row_slices()]
            for places, columns in chunk_pairs():
                block = by_tokens(rows_of(refs, normed_at, columns), right)
                for part, place in enumerate(places):
                    target = results[2 + which // 2 + 2 * (place // DEEP)]
                    target[place % DEEP, which % 2] = block[part * LANES : (part + 1) * LANES, :]
            if which == 1:
                put(2)
                put(4)
        left = [refs[context_at][here, :] for here in row_slices()]
        for places, columns in chunk_pairs():
            block = by_tokens(left, rows_of(refs, grad_at, columns))
            for part, place in enumerate(places):
                target = results[3 + 2 * (place // DEEP)]
                one = block[:, part * LANES : (part + 1) * LANES]
                target[place % DEEP, 1] = jnp.concatenate([one[:LANES], one[LANES:]], axis=1)
        put(3)
        put(5)

    return call(
        kernel,
        meta,
        ops,
        [like((3, LENGTH, width), LOW), like((2, width), FULL)] + [blocks] * 4,
        [pltpu.VMEM((LENGTH, width), LOW)] + [pltpu.VMEM((PAIR, LENGTH), FULL)] * 2,
        time=15,
    )


def unit_tiles(width):
    for first in range(0, width, BLOCK):
        stop = first + BLOCK
        yield slice(first, stop), slice(stop - width // 2, stop) if stop % (width // 2) == 0 else None


def up_kernel(meta, normed, sides, biases, at, cot):
    ops = Operands()
    normed_at = [ops.add(normed[0])]
    sides_at, bias_at = [[ops.side(one) for one in sides[0]]], [ops.add(biases[0])]
    normed_at.append(ops.add(normed[1]))
    cot_at = [ops.add(one) for one in cot]
    sides_at.append([ops.side(one) for one in sides[1]])
    bias_at.append(ops.add(biases[1]))
    width = sides[0][0][0][0].shape[-1]
    blocks = like((DEEP, width, LANES), LOW)

    def kernel(meta, refs, results, put):
        for x in range(2):
            active, slope, *grads = results[4 * x : 4 * x + 4]
            low, high = sides_at[x]
            for units, done in unit_tiles(width):
                low_w = high_w = None
                for here, block in zip(row_slices(), rows_of(refs, normed_at)):
                    if low_w is None:
                        low_w, high_w = tall(refs, low, units), tall(refs, high, units)
                    before = dot(block[:, :HALF], low_w) + dot(block[:, HALF:], high_w)
                    before = before + refs[bias_at[x]][:, at + units.start : at + units.stop]
                    phi = 0.5 * (1.0 + lax.erf(before * (2.0**-0.5)))
                    active[here, units] = (before * phi).astype(LOW)
                    bell = jnp.exp(-0.5 * before * before) * (2.0 * jnp.pi) ** -0.5
                    slope[here, units] = (phi + before * bell).astype(LOW)
                left = [active[here, units] for here in row_slices()]
                for places, chunks in chunk_pairs():
                    block = by_tokens(left, rows_of(refs, cot_at, chunks))
                    for part, place in enumerate(places):
                        grads[place // DEEP][place % DEEP, units, :] = block[:, part * LANES : (part + 1) * LANES]
                if done:
                    for one in range(4 * x, 4 * x + 4):
                        put(one, ALL, done)

    return call(kernel, meta, ops, ([like((LENGTH, width), LOW)] * 2 + [blocks] * 2) * 2, time=18)


def down_kernel(meta, cot, sides, slopes, normed, up_sides, actives):
    ops = Operands()
    rows, wide = normed[0].shape
    width = slopes[0].shape[1]
    cot_at = [ops.add(cot[0])]
    sides_at, slope_at = [[ops.side(one) for one in sides[0]]], [ops.add(slopes[0])]
    cot_at.append(ops.add(cot[1]))
    sides_at.append([ops.side(one) for one in sides[1]])
    slope_at.append(ops.add(slopes[1]))
    up_at = [[ops.side(one) for one in pair] for pair in up_sides]
    normed_at = [ops.add(one) for one in normed]
    active_at = [ops.add(one) for one in actives]
    pair = [like((rows, wide), FULL), like((rows, wide), LOW)]
    outs = [like((1, width), FULL)] * 2 + pair + [like((2, LANES, width), LOW)] * 8 + pair

    def kernel(meta, refs, results, put, *grads):
        for x in range(2):
            low, high = sides_at[x]
            for units, _ in unit_tiles(width):
                total = jnp.zeros((1, BLOCK), FULL)
                low_w = high_w = None
                for here, block in zip(row_slices(), rows_of(refs, cot_at)):
                    if low_w is None:
                        low_w, high_w = flat(refs, low, units), flat(refs, high, units)
                    grad = nt(block[:, :HALF], low_w) + nt(block[:, HALF:], high_w)
                    grad = (grad * refs[slope_at[x]][here, units].astype(FULL)).astype(LOW)
                    grads[x][here, units] = grad
                    total = total + jnp.sum(grad.astype(FULL), axis=0, keepdims=True)
                results[x][:, units] = total
            put(x)

        def terms(lefts, sides, product):
            return [
                (lambda block, left=left: left[row_slices()[block], :], pick(refs, *one), product)
                for left, one in zip(lefts, sides)
            ]

        spread(meta[1] == 0, terms(grads, up_at, nt), *results[2:4], put, 2)
        for x in (1, 0):
            targets = results[4 + 4 * x : 8 + 4 * x]
            for units, done in unit_tiles(width):
                right = [grads[x][here, units] for here in row_slices()]
                for places, chunks in chunk_pairs():
                    block = by_tokens(rows_of(refs, normed_at, chunks), right)
                    for part, place in enumerate(places):
                        targets[place // 2][place % 2, :, units] = block[part * LANES : (part + 1) * LANES, :]
            for one in range(4 + 4 * x, 8 + 4 * x):
                put(one)
        spread(meta[1] == 0, terms([refs[at] for at in active_at], sides_at, dot), *results[12:14], put, 12)

    return call(kernel, meta, ops, outs, [pltpu.VMEM((LENGTH, width), LOW)] * 2, time=20)


def spread_kernel(meta, terms, rows, wide, product):
    ops = Operands()
    places = [(ops.add(left), at, ops.side(low), ops.side(high)) for left, at, low, high in terms]

    def kernel(meta, refs, results, put):
        def left_of(one, at):
            index = () if at is None else (at,)
            return lambda block: refs[one][(*index, row_slices()[block])]

        parts = [(left_of(one, at), pick(refs, low, high), product) for one, at, low, high in places]
        spread(meta[1] == 0, parts, *results, put, 0)

    return call(kernel, meta, ops, [like((rows, wide), FULL), like((rows, wide), LOW)], time=6)


STRIP = 128


def normalize(values):
    center = values - jnp.mean(values, axis=-1, keepdims=True)
    spread_ = jnp.mean(center * center, axis=-1, keepdims=True)
    rate = lax.rsqrt(spread_ + EPSILON)
    return center * rate, rate


def strips(rows):
    return [slice(first, first + STRIP) for first in range(0, rows, STRIP)]


def by_strips(kernel, meta, arrays, vectors, outs, sums=0):
    ops = Operands()
    rows, wide = arrays[0].shape
    halves = [slice(0, rows // 2), slice(rows // 2, rows)]
    first = [ops.add(array, halves[0]) for array in arrays]
    vector_at = [ops.add(one) for one in vectors]
    places = [first, [ops.add(array, halves[1]) for array in arrays]]
    shapes = [like((rows, wide), kind) for kind in outs]
    if sums:
        shapes.append(like((sums, wide), FULL))

    def body(meta, refs, results, put):
        parts = [None] * sums
        for at, half in zip(places, halves):
            for here in strips(rows // 2):
                kernel(
                    meta,
                    [refs[one][here, :] for one in at],
                    [refs[one][...] for one in vector_at],
                    [(result, slice(half.start + here.start, half.start + here.stop)) for result in results[: len(outs)]],
                    parts,
                )
            for one in range(len(outs)):
                put(one, half)
        if sums:
            for at, value in enumerate(parts):
                results[-1][at : at + 1, :] = jnp.sum(value, axis=0, keepdims=True)
            put(len(outs))

    return call(body, meta, ops, shapes, time=4)


def start_kernel(meta, values, vectors, results, sums):
    tokens, cot = values
    gain, shift = vectors
    hat, _ = normalize(tokens.astype(FULL))
    to_local(meta[1], *results[0], (hat * gain + shift).astype(LOW))
    to_local(meta[1], *results[1], cot.astype(LOW))


def join_kernel(meta, values, vectors, results, sums):
    tokens, own, got = values
    bias, gain, shift = vectors
    total = tokens.astype(FULL) + (own + got.astype(FULL)) + bias
    hidden, here = results[0]
    hidden[here, :] = total
    hat, _ = normalize(total)
    to_local(meta[1], *results[1], (hat * gain + shift).astype(LOW))


def add_sums(sums, values):
    for at, value in enumerate(values):
        part = jnp.sum(value.reshape(STRIP // 8, 8, value.shape[1]), axis=0)
        sums[at] = part if sums[at] is None else sums[at] + part


def norm_back(grad, values, gain):
    hat, rate = normalize(values)
    scaled = grad * gain
    row = rate * (
        scaled
        - jnp.mean(scaled, axis=-1, keepdims=True)
        - hat * jnp.mean(scaled * hat, axis=-1, keepdims=True)
    )
    return row, grad * hat


def second_kernel(meta, values, vectors, results, sums):
    own, got, hidden, pulled = values
    grad = own + got.astype(FULL)
    row, gain_part = norm_back(grad, hidden, vectors[0])
    total = pulled + row
    out, here = results[0]
    out[here, :] = total
    to_local(meta[1], *results[1], total.astype(LOW))
    add_sums(sums, [gain_part, grad, total, pulled])


def first_kernel(meta, values, vectors, results, sums):
    own, got, tokens, hidden_grad = values
    grad = own + got.astype(FULL)
    row, gain_part = norm_back(grad, tokens.astype(FULL), vectors[0])
    out, here = results[0]
    out[here, :] = hidden_grad + row
    add_sums(sums, [gain_part, grad])


def end_kernel(meta, values, vectors, results, sums):
    hidden, own, got = values
    out, here = results[0]
    out[here, :] = (hidden + (own + got.astype(FULL)) + vectors[0]).astype(LOW)


def wide_shard(shard, axis):
    return lax.all_gather(shard, "w", axis=axis, tiled=True) if lax.axis_size("w") > 1 else shard


def gather_deep(shard):
    return lax.all_gather(shard, "z", axis=0, tiled=False)


def add(*values):
    total = values[0].astype(FULL)
    for value in values[1:]:
        total = total + value.astype(FULL)
    return total.astype(LOW)


def scatter_deep(total):
    total = lax.psum_scatter(total, "z", scatter_dimension=0, tiled=False)
    if lax.axis_size("w") > 1:
        total = lax.psum_scatter(total, "w", scatter_dimension=total.ndim - 2, tiled=True)
    return total.astype(FULL)


def on_device(
    inputs,
    doc_lengths,
    first_gain,
    first_bias,
    w_query,
    b_query,
    w_key,
    w_value,
    b_value,
    w_out,
    b_out,
    second_gain,
    second_bias,
    w_up,
    b_up,
    w_down,
    b_down,
    cotangent,
):
    rows, wide = inputs.shape
    here = w_query.shape[1]
    core = lax.axis_index("c").astype(jnp.int32)
    at_y = lax.axis_index("y").astype(jnp.int32)
    at_x = lax.axis_index("x")
    lengths = lax.dynamic_index_in_dim(doc_lengths, at_x, 0, keepdims=False)
    ends = [lengths[0]]
    for one in range(1, lengths.shape[0]):
        ends.append(ends[-1] + lengths[one])
    meta = jnp.stack([core, at_y, *ends])

    def line(vector):
        return vector.reshape(1, -1)

    out_shard = wide_shard(w_out, 1)
    out_shard = jnp.concatenate([out_shard[: here // 2], out_shard[here // 2 :]], axis=1)
    attn_shard = jnp.stack([wide_shard(w_query, 0), wide_shard(w_key, 0), wide_shard(w_value, 0), out_shard])
    up_shard = wide_shard(w_up, 0)
    down_shard = wide_shard(w_down, 1)
    biases = line(jnp.concatenate([b_query, b_value, b_up]))
    far = swap(biases, "x")
    down_raw = swap_both(down_shard)
    attn_mine = after(gather_deep(attn_shard), down_raw, far)
    attn_pairs = [attn_mine[:, :2], attn_mine[:, 2:]]
    attn_x = [swap(one, "x") for one in attn_pairs]
    attn_y = [swap(one, "y") for one in attn_pairs]
    attn_far = [swap(attn_y[0], "x"), swap(attn_x[1], "y")]


    normed, cot = by_strips(start_kernel, meta, [inputs, cotangent], [line(first_gain), line(first_bias)], [LOW, LOW])
    normed = (normed, swap(normed, "c"))
    cot = (cot, swap(cot, "c"))

    attn_sides = [
        [(stacked_side(attn_mine, which), stacked_side(attn_y[which // 2], which % 2)) for which in range(4)],
        [(stacked_side(attn_x[which // 2], which % 2), stacked_side(attn_far[which // 2], which % 2)) for which in range(4)],
    ]

    qkv, context, logs = [None] * 2, [None] * 2, [None] * 2
    qkv[0], context[0], logs[0] = attention_forward(meta, normed, attn_sides[0][:3], biases)

    half = DEEP // 2
    up_mine = after(gather_deep(up_shard), context[0], *attn_far)
    up_parts = [up_mine[:half], up_mine[half:]]
    up_x = [swap(one, "x") for one in up_parts]
    up_y = [swap(one, "y") for one in up_parts]

    qkv[1], context[1], logs[1], own, sent = attention_forward(
        meta,
        normed,
        attn_sides[1][:3],
        far,
        (context[0], [attn_sides[0][3], attn_sides[1][3]]),
    )
    sent = after(sent, *up_x, *up_y)
    hidden, normed_two = by_strips(
        join_kernel,
        meta,
        [inputs, own, swap(sent, "c")],
        [line(b_out), line(second_gain), line(second_bias)],
        [FULL, LOW],
    )
    up_far = [swap(up_y[0], "x"), swap(up_x[1], "y")]
    normed_two = (normed_two, swap(after(normed_two, *up_far), "c"))

    up_sides = [
        (whole_side(up_mine), split_side(*up_y)),
        (split_side(*up_x), split_side(*up_far)),
    ]
    down_mine = after(gather_deep(down_shard), *up_far)
    down_x = swap(down_mine, "x")
    down_y = swap(down_mine, "y")
    down_both = gather_deep(down_raw)
    down_sides = [
        (whole_side(down_mine), whole_side(down_y)),
        (whole_side(down_x), whole_side(down_both)),
    ]
    active, slope, down_own, down_far = [None] * 2, [None] * 2, [None] * 2, [None] * 2
    (
        active[0],
        slope[0],
        down_own[0],
        down_far[0],
        active[1],
        slope[1],
        down_own[1],
        down_far[1],
    ) = up_kernel(meta, normed_two, up_sides, (biases, far), 2 * here, cot)

    *sums, own, sent, own_low, own_high, far_low, far_high, other_low, other_high, both_low, both_high, last, last_sent = down_kernel(
        meta, cot, down_sides, slope, normed_two, up_sides, active
    )
    up_own, up_beyond, up_other, up_both = (own_low, own_high), (far_low, far_high), (other_low, other_high), (both_low, both_high)

    down_diagonal = swap_both(lax.psum_scatter(down_far[1], "z", scatter_dimension=0, tiled=False))
    down_total = add(
        down_own[0], swap(after(down_far[0], down_x, down_y), "y"), swap(after(down_own[1], down_x, down_y), "x")
    )
    owner_down = lax.psum_scatter(down_total, "z", scatter_dimension=0, tiled=False)
    owner_down = owner_down.astype(FULL) + down_diagonal.astype(FULL)
    if lax.axis_size("w") > 1:
        owner_down = lax.psum_scatter(owner_down, "w", scatter_dimension=1, tiled=True)

    got_low = swap(up_both[0], "x")
    got_high = swap(up_both[1], "y")
    got_x = [swap(up_other[0], "x"), None]
    got_y = [None, swap(up_beyond[1], "y")]

    hidden_grad, attn_grad, second_sums = by_strips(
        second_kernel, meta, [own, swap(sent, "c"), hidden, cotangent], [line(second_gain)], [FULL, LOW], sums=4
    )
    attn_grad = (attn_grad, swap(attn_grad, "c"))

    got_y[0] = swap(add(up_beyond[0], after(got_low, attn_grad[0])), "y")
    got_x[1] = swap(add(up_other[1], after(got_high, attn_grad[0])), "x")

    back, unit_sums = [None] * 2, [None] * 2
    back[1], unit_sums[1], other_qk, other_vo, both_qk, both_vo = attention_backward(
        meta, attn_grad, attn_sides[1][3], qkv[1], logs[1], context[1], normed
    )
    got_qk = swap(both_qk, "x")
    got_vo = swap(both_vo, "y")
    x_qk = swap(other_qk, "x")
    got_x, got_y = [[after(one, back[1]) for one in parts] for parts in (got_x, got_y)]
    up_total = jnp.concatenate([add(up_own[part], got_x[part], got_y[part]) for part in range(2)])
    owner_up = scatter_deep(up_total)
    back[0], unit_sums[0], own_qk, own_vo, far_qk, far_vo = attention_backward(
        meta, (after(attn_grad[0], back[1]), attn_grad[1]), attn_sides[0][3], qkv[0], logs[0], context[0], normed
    )
    y_vo = swap(far_vo, "y")
    x_vo = swap(add(other_vo, after(got_vo, back[0])), "x")
    y_qk = swap(add(far_qk, after(got_qk, back[0])), "y")
    attn_total = jnp.concatenate([add(own_qk, x_qk, y_qk), add(own_vo, x_vo, y_vo)], axis=1)
    owner_attn = lax.psum_scatter(attn_total, "z", scatter_dimension=0, tiled=False)
    owner_out = owner_attn[3].astype(FULL)
    owner_out = jnp.concatenate([owner_out[:, :LANES], owner_out[:, LANES:]])
    owner_attn = owner_attn[:3].astype(FULL)
    if lax.axis_size("w") > 1:
        owner_attn = lax.psum_scatter(owner_attn, "w", scatter_dimension=1, tiled=True)
        owner_out = lax.psum_scatter(owner_out, "w", scatter_dimension=1, tiled=True)

    own, sent = spread_kernel(
        meta,
        [(back[x], which, *attn_sides[x][which]) for x in range(2) for which in range(3)],
        rows,
        wide,
        nt,
    )
    input_grad, first_sums = by_strips(
        first_kernel, meta, [own, swap(sent, "c"), inputs, hidden_grad], [line(first_gain)], [FULL], sums=2
    )

    [layer_out] = by_strips(
        end_kernel, meta, [hidden, last, swap(last_sent, "c")], [line(b_down)], [LOW]
    )

    replicated = all_sum(jnp.concatenate([first_sums, second_sums]).reshape(-1), "c")
    own_units, far_units = [
        jnp.concatenate([unit_sums[x][0], unit_sums[x][1], sums[x][0]]) for x in range(2)
    ]
    got = swap(jnp.concatenate([replicated, far_units]), "x")
    summed = jnp.concatenate([replicated, own_units]) + got
    for axis in ("y", "z", "w"):
        summed = all_sum(summed, axis)
    vectors = summed[: 6 * wide].reshape(6, wide)
    units = summed[6 * wide :]

    return (
        layer_out,
        input_grad,
        vectors[0],
        vectors[1],
        owner_attn[0],
        units[:here],
        owner_attn[1],
        owner_attn[2],
        units[here : 2 * here],
        owner_out,
        vectors[4],
        vectors[2],
        vectors[3],
        owner_up,
        units[2 * here :],
        owner_down,
        vectors[5],
    )


def solution(mesh):
    groups, lanes = mesh.shape["fsdp"], mesh.shape["tp"]
    inner = Mesh(
        mesh.devices.reshape(DEEP, 2, groups // (2 * DEEP), lanes // 2, 2), ("z", "y", "w", "x", "c")
    )
    f, t = ("z", "y", "w"), ("x", "c")
    tokens, rows, columns, units = P(f + t, None), P(f, t), P(t, f), P(t)
    return jax.shard_map(
        on_device,
        mesh=inner,
        in_specs=(
            tokens,
            P(f, None),
            P(),
            P(),
            rows,
            units,
            rows,
            rows,
            units,
            columns,
            P(),
            P(),
            P(),
            rows,
            units,
            columns,
            P(),
            tokens,
        ),
        out_specs=(
            tokens,
            tokens,
            P(),
            P(),
            rows,
            units,
            rows,
            rows,
            units,
            columns,
            P(),
            P(),
            P(),
            rows,
            units,
            columns,
            P(),
        ),
        check_vma=False,
    )
```

```python
import jax
import jax.numpy as jnp
from jax import lax
from jax.experimental import pallas as pl
from jax.experimental.pallas import tpu as pltpu
from jax.sharding import Mesh, PartitionSpec as P

HEAD_DIM = 64
LENGTH = 1024
BLOCK = 256
PAIR = 2 * HEAD_DIM
EPSILON = 1e-05
SCALE = HEAD_DIM**-0.5
LOW = jnp.bfloat16
FULL = jnp.float32
SWAP = ((0, 1), (1, 0))
DEEP = 4
LANES = 128
HALF = DEEP * LANES


def swap(values, axis):
    return lax.ppermute(values, axis, SWAP)


def swap_both(values):
    return lax.ppermute(values, ("y", "x"), ((0, 3), (1, 2), (2, 1), (3, 0)))


def all_sum(values, axis, *cover):
    size, step = lax.axis_size(axis), 1
    while step < size:
        if cover:
            values, cover = after(values, *cover[0]), cover[1:]
        values = values + lax.ppermute(values, axis, [(i, i ^ step) for i in range(size)])
        step *= 2
    return values


def after(values, *others):
    return lax.optimization_barrier((values, *others))[0]


def like(shape, kind):
    return jax.ShapeDtypeStruct(shape, kind)


ALL = slice(None)


ALL = slice(None)


class Operands:
    def __init__(self):
        self.parts = []

    def add(self, array, *index):
        for at, (one, where) in enumerate(self.parts):
            if one is array and where == index:
                return at
        self.parts.append((array, index))
        return len(self.parts) - 1

    def side(self, blocks):
        return [(self.add(array), index) for array, index in blocks]


class Buffers:
    def __init__(self, buffers, copies):
        self.buffers, self.copies = buffers, dict(enumerate(copies))

    def __getitem__(self, at):
        if at in self.copies:
            self.copies.pop(at).wait()
        return self.buffers[at]


def call(kernel, meta, ops, outs, scratch=(), time=3, limit=60):
    arrays = []
    for array, _ in ops.parts:
        if not any(array is one for one in arrays):
            arrays.append(array)
    source = [next(at for at, one in enumerate(arrays) if one is array) for array, _ in ops.parts]
    blocks = [jax.eval_shape(lambda a, index=index: a[index], like(array.shape, array.dtype)) for array, index in ops.parts]
    count, parts, results = len(arrays), len(ops.parts), len(outs)

    def body(*refs):
        meta_ref, sources, targets = refs[0], refs[1 : 1 + count], refs[1 + count : 1 + count + results]
        rest = refs[1 + count + results :]
        buffers, copies = rest[:parts], rest[parts : parts + results]
        in_sems, out_sems, *extra = rest[parts + results :]
        fetches = []
        for at, (_, index) in enumerate(ops.parts):
            ref = sources[source[at]]
            fetches.append(pltpu.make_async_copy(ref.at[index] if index else ref, buffers[at], in_sems.at[at]))
            fetches[-1].start()
        sent = []

        def put(at, *index):
            one, two = (copies[at].at[index], targets[at].at[index]) if index else (copies[at], targets[at])
            sent.append(pltpu.make_async_copy(one, two, out_sems.at[len(sent)]))
            sent[-1].start()

        kernel(meta_ref, Buffers(buffers, fetches), copies, put, *extra)
        for one in sent:
            one.wait()

    whole = pl.BlockSpec(memory_space=pl.ANY)
    return pl.pallas_call(
        body,
        out_shape=outs,
        in_specs=[pl.BlockSpec(memory_space=pltpu.SMEM)] + [whole] * count,
        out_specs=[whole] * results,
        scratch_shapes=[pltpu.VMEM(one.shape, one.dtype) for one in blocks]
        + [pltpu.VMEM(one.shape, one.dtype) for one in outs]
        + [pltpu.SemaphoreType.DMA((parts,)), pltpu.SemaphoreType.DMA((64,))]
        + list(scratch),
        compiler_params=pltpu.CompilerParams(vmem_limit_bytes=limit << 20),
        cost_estimate=pl.CostEstimate(flops=time << 20, bytes_accessed=1 << 16, transcendentals=0),
    )(meta, *arrays)


def whole_side(array):
    return [(array, (z,)) for z in range(DEEP)]


def stacked_side(array, which):
    return [(array, (z, which)) for z in range(DEEP)]


def split_side(low, high):
    return [((low, high)[z // 2], (z % 2,)) for z in range(DEEP)]


def dot(left, right):
    return jnp.dot(left, right, preferred_element_type=FULL)


def nt(left, right):
    return lax.dot_general(left, right, (((1,), (1,)), ((), ())), preferred_element_type=FULL)


def tn(left, right):
    return lax.dot_general(left, right, (((0,), (0,)), ((), ())), preferred_element_type=FULL)


def tall(refs, side, units=ALL):
    return jnp.concatenate([refs[at][(*index, ALL, units)] for at, index in side], axis=0)


def flat(refs, side, units):
    return jnp.concatenate([refs[at][(*index, units)] for at, index in side], axis=1)


def unfold(block):
    return jnp.concatenate([block[:, :LANES], block[:, LANES:]], axis=0)


def row_slices(count=LENGTH // BLOCK):
    return [slice(at * BLOCK, (at + 1) * BLOCK) for at in range(count)]


def rows_of(refs, pair, columns=ALL):
    for at in pair:
        for first in range(0, refs[at].shape[0], BLOCK):
            yield refs[at][first : first + BLOCK, columns]


def chunk_pairs():
    for first in range(0, 2 * DEEP, 2):
        yield (first, first + 1), slice(first * LANES, (first + 2) * LANES)


def by_tokens(lefts, rights):
    total = None
    for left, right in zip(lefts, rights):
        part = tn(left, right)
        total = part if total is None else total + part
    return total.astype(LOW)


def spread(even, terms, own, far, put, at):
    rows = own.shape[0]
    for z in range(DEEP):
        columns = slice(2 * z * LANES, 2 * (z + 1) * LANES)
        rights = []
        for _, chunks, product in terms:
            one, two = chunks(z)
            pair = [jnp.where(even, one, two), jnp.where(even, two, one)]
            rights.append(jnp.concatenate(pair, axis=0 if product is nt else 1))
        for block, here in enumerate(row_slices()):
            total = None
            for (left, _, product), right in zip(terms, rights):
                part = product(left(block), right)
                total = part if total is None else total + part
            if here.start < rows:
                own[here, columns] = total
            else:
                far[here.start - rows : here.stop - rows, columns] = total.astype(LOW)
        if z % 2:
            done = slice(columns.stop - 4 * LANES, columns.stop)
            put(at, ALL, done)
            put(at + 1, ALL, done)


def pick(refs, low, high, change=lambda block: block):
    return lambda z: [change(refs[at][one]) for at, one in (low[z], high[z])]


def to_local(at_y, target, rows, values):
    for chunk in range(2 * DEEP):
        place = chunk // 2 + DEEP * lax.rem(chunk + at_y, 2)
        columns = pl.ds(pl.multiple_of(place * LANES, LANES), LANES)
        target[rows, columns] = values[:, chunk * LANES : (chunk + 1) * LANES]


def row_ranges():
    for first in range(0, LENGTH, BLOCK):
        yield first, max(0, first - LENGTH // 2), first + BLOCK


def ordered(ref, which, core, columns):
    half = LENGTH // 2
    start = pl.multiple_of(core * half, half)
    rest = pl.multiple_of((1 - core) * half, half)
    return jnp.concatenate([ref[which, pl.ds(start, half), columns], ref[which, pl.ds(rest, half), columns]], axis=0)


def local_row(first, core):
    return pl.multiple_of(lax.rem(first + core * (LENGTH // 2), LENGTH), BLOCK)


def allowed_tile(meta, first, low, high):
    shape = (BLOCK, high - low)
    places = first + lax.broadcasted_iota(jnp.int32, (BLOCK, 1), 0)
    start = jnp.zeros((BLOCK, 1), jnp.int32)
    for at in range(2, meta.shape[0]):
        start = jnp.where(places >= meta[at], meta[at], start)
    keys = low + lax.broadcasted_iota(jnp.int32, shape, 1)
    return (keys <= places) & (keys >= start)


def first_lanes():
    return lax.broadcasted_iota(jnp.int32, (BLOCK, PAIR), 1) < HEAD_DIM


def attend(meta, qkv, context, logs, put):
    core = meta[0]
    first_head = first_lanes()
    for pair in range(context.shape[1] // PAIR):
        columns = slice(pair * PAIR, (pair + 1) * PAIR)
        keys = ordered(qkv, 1, core, columns)
        values = ordered(qkv, 2, core, columns)
        values = jnp.concatenate([values, jnp.ones_like(values)], axis=1)
        for first, low, high in row_ranges():
            here = local_row(first, core)
            query = qkv[0, pl.ds(here, BLOCK), columns] * SCALE
            allowed = allowed_tile(meta, first, low, high)
            outs = []
            sums = []
            for head in range(2):
                picked = jnp.where(first_head if head == 0 else ~first_head, query, jnp.zeros_like(query))
                scores = jnp.where(allowed, nt(picked, keys[low:high]), -1e30)
                highest = jnp.max(scores, axis=-1, keepdims=True)
                mixed = dot(jnp.exp(scores - highest).astype(LOW), values[low:high])
                totals = mixed[:, PAIR:]
                outs.append(mixed[:, :PAIR] / totals)
                sums.append(highest + jnp.log(totals))
            context[pl.ds(here, BLOCK), columns] = jnp.where(first_head, outs[0], outs[1]).astype(LOW)
            logs[pl.ds(here, BLOCK), columns] = jnp.where(first_head, sums[0], sums[1])
        put(1, ALL, columns)
        put(2, ALL, columns)


def attend_back(meta, qkv, logs, grads, out, sums, key_sum, value_sum):
    core = meta[0]
    first_head = first_lanes()
    half = LENGTH // 2
    for pair in range(grads.shape[1] // PAIR):
        columns = slice(pair * PAIR, (pair + 1) * PAIR)
        keys = ordered(qkv, 1, core, columns)
        values = ordered(qkv, 2, core, columns)
        key_sum[...] = jnp.zeros_like(key_sum)
        value_sum[...] = jnp.zeros_like(value_sum)
        query_total = value_total = jnp.zeros((1, PAIR), FULL)
        for first, low, high in row_ranges():
            here = local_row(first, core)
            query = qkv[0, pl.ds(here, BLOCK), columns] * SCALE
            grad = grads[pl.ds(here, BLOCK), columns]
            log_pair = logs[pl.ds(here, BLOCK), columns]
            allowed = allowed_tile(meta, first, low, high)
            query_flip = query.T
            grad_flip = grad.T
            outs = []
            for head in range(2):
                mask = first_head if head == 0 else ~first_head
                band = slice(head * HEAD_DIM, (head + 1) * HEAD_DIM)
                query_one = jnp.where(mask, query, jnp.zeros_like(query))
                grad_one = jnp.where(mask, grad, jnp.zeros_like(grad))
                log_one = log_pair[:, head * HEAD_DIM : head * HEAD_DIM + 1]
                scores = jnp.where(allowed, nt(query_one, keys[low:high]), -1e30)
                weights = jnp.exp(scores - log_one)
                grad_probs = nt(grad_one, values[low:high])
                inner = jnp.sum(grad_probs * weights, axis=-1, keepdims=True)
                grad_scores = (weights * (grad_probs - inner)).astype(LOW)
                outs.append(dot(grad_scores, keys[low:high]))
                key_sum[band, low:high] += dot(query_flip[band, :], grad_scores)
                value_sum[band, low:high] += dot(grad_flip[band, :], weights.astype(LOW))
            grad_query = (jnp.where(first_head, outs[0], outs[1]) * SCALE).astype(LOW)
            out[0, pl.ds(here, BLOCK), columns] = grad_query
            query_total = query_total + jnp.sum(grad_query.astype(FULL), axis=0, keepdims=True)
        for part in range(2):
            there = pl.multiple_of(lax.rem(part + core, 2) * half, half)
            out[1, pl.ds(there, half), columns] = key_sum[:, part * half : (part + 1) * half].T.astype(LOW)
            grad_value = value_sum[:, part * half : (part + 1) * half].T.astype(LOW)
            out[2, pl.ds(there, half), columns] = grad_value
            value_total = value_total + jnp.sum(grad_value.astype(FULL), axis=0, keepdims=True)
        sums[0:1, columns] = query_total
        sums[1:2, columns] = value_total


def attention_forward(meta, normed, sides, biases, last=None):
    ops = Operands()
    normed_at = [ops.add(normed[0])]
    sides_at = [[ops.side(one) for one in pair] for pair in sides]
    bias_at = ops.add(biases)
    normed_at.append(ops.add(normed[1]))
    width = sides[0][0][0][0].shape[-1]
    rows, wide = normed[0].shape
    outs = [like((3, LENGTH, width), LOW), like((LENGTH, width), LOW), like((LENGTH, width), FULL)]
    if last:
        first_at = ops.add(last[0])
        out_sides = [[ops.side(one) for one in pair] for pair in last[1]]
        outs += [like((rows, wide), FULL), like((rows, wide), LOW)]

    def kernel(meta, refs, results, put):
        qkv, context, logs = results[:3]
        for which, (low, high) in enumerate(sides_at):
            low_w = high_w = None
            for here, block in zip(row_slices(), rows_of(refs, normed_at)):
                if low_w is None:
                    low_w, high_w = tall(refs, low), tall(refs, high)
                total = dot(block[:, :HALF], low_w) + dot(block[:, HALF:], high_w)
                if which != 1:
                    total = total + refs[bias_at][:, which // 2 * width : (which // 2 + 1) * width]
                qkv[which, here, :] = total.astype(LOW)
        put(0)
        attend(meta, qkv, context, logs, put)
        if last:
            terms = [
                (lambda block, left=left: left[row_slices()[block], :], pick(refs, *pair, unfold), dot)
                for left, pair in zip((refs[first_at], context), out_sides)
            ]
            spread(meta[1] == 0, terms, *results[3:], put, 3)

    return call(kernel, meta, ops, outs, time=12 if last else 8)


def attention_backward(meta, grad, side, qkv, logs, context, normed):
    ops = Operands()
    grad_at = [ops.add(grad[0])]
    low, high = [ops.side(one) for one in side]
    grad_at.append(ops.add(grad[1]))
    qkv_at, log_at = [ops.add(one) for one in (qkv, logs)]
    normed_at = [ops.add(one) for one in normed]
    context_at = ops.add(context)
    width = context.shape[1]
    blocks = like((DEEP, 4, LANES, width), LOW)

    def kernel(meta, refs, results, put, grads, key_sum, value_sum):
        out, sums = results[:2]
        low_w = high_w = None
        for here, block in zip(row_slices(), rows_of(refs, grad_at)):
            if low_w is None:
                low_w, high_w = [
                    jnp.concatenate([unfold(refs[at][index]) for at, index in one], axis=1) for one in (low, high)
                ]
            grads[here, :] = (nt(block[:, :HALF], low_w) + nt(block[:, HALF:], high_w)).astype(LOW)
        attend_back(meta, refs[qkv_at], refs[log_at], grads, out, sums, key_sum, value_sum)
        put(0)
        put(1)
        for which in range(3):
            right = [out[which, here, :] for here in row_slices()]
            for places, columns in chunk_pairs():
                block = by_tokens(rows_of(refs, normed_at, columns), right)
                for part, place in enumerate(places):
                    results[2 + place // DEEP][place % DEEP, which] = block[part * LANES : (part + 1) * LANES, :]
        left = [refs[context_at][here, :] for here in row_slices()]
        for places, columns in chunk_pairs():
            block = by_tokens(left, rows_of(refs, grad_at, columns))
            for part, place in enumerate(places):
                one = block[:, part * LANES : (part + 1) * LANES]
                results[2 + place // DEEP][place % DEEP, 3] = jnp.concatenate([one[:LANES], one[LANES:]], axis=1)
        put(2)
        put(3)

    return call(
        kernel,
        meta,
        ops,
        [like((3, LENGTH, width), LOW), like((2, width), FULL)] + [blocks] * 2,
        [pltpu.VMEM((LENGTH, width), LOW)] + [pltpu.VMEM((PAIR, LENGTH), FULL)] * 2,
        time=15,
    )


def unit_tiles(width):
    for first in range(0, width, BLOCK):
        stop = first + BLOCK
        yield slice(first, stop), slice(stop - width // 2, stop) if stop % (width // 2) == 0 else None


def up_kernel(meta, normed, sides, biases, at, cot):
    ops = Operands()
    normed_at = [ops.add(normed[0])]
    sides_at, bias_at = [[ops.side(one) for one in sides[0]]], [ops.add(biases[0])]
    normed_at.append(ops.add(normed[1]))
    cot_at = [ops.add(one) for one in cot]
    sides_at.append([ops.side(one) for one in sides[1]])
    bias_at.append(ops.add(biases[1]))
    width = sides[0][0][0][0].shape[-1]
    blocks = like((DEEP, width, LANES), LOW)

    def kernel(meta, refs, results, put):
        for x in range(2):
            active, slope, *grads = results[4 * x : 4 * x + 4]
            low, high = sides_at[x]
            for units, done in unit_tiles(width):
                low_w = high_w = None
                for here, block in zip(row_slices(), rows_of(refs, normed_at)):
                    if low_w is None:
                        low_w, high_w = tall(refs, low, units), tall(refs, high, units)
                    before = dot(block[:, :HALF], low_w) + dot(block[:, HALF:], high_w)
                    before = before + refs[bias_at[x]][:, at + units.start : at + units.stop]
                    phi = 0.5 * (1.0 + lax.erf(before * (2.0**-0.5)))
                    active[here, units] = (before * phi).astype(LOW)
                    bell = jnp.exp(-0.5 * before * before) * (2.0 * jnp.pi) ** -0.5
                    slope[here, units] = (phi + before * bell).astype(LOW)
                left = [active[here, units] for here in row_slices()]
                for places, chunks in chunk_pairs():
                    block = by_tokens(left, rows_of(refs, cot_at, chunks))
                    for part, place in enumerate(places):
                        grads[place // DEEP][place % DEEP, units, :] = block[:, part * LANES : (part + 1) * LANES]
                if done:
                    for one in range(4 * x, 4 * x + 4):
                        put(one, ALL, done)

    return call(kernel, meta, ops, ([like((LENGTH, width), LOW)] * 2 + [blocks] * 2) * 2, time=18)


def down_kernel(meta, cot, sides, slopes, normed, up_sides):
    ops = Operands()
    rows, wide = normed[0].shape
    width = slopes[0].shape[1]
    cot_at = [ops.add(cot[0])]
    sides_at, slope_at = [[ops.side(one) for one in sides[0]]], [ops.add(slopes[0])]
    cot_at.append(ops.add(cot[1]))
    sides_at.append([ops.side(one) for one in sides[1]])
    slope_at.append(ops.add(slopes[1]))
    up_at = [[ops.side(one) for one in pair] for pair in up_sides]
    normed_at = [ops.add(one) for one in normed]
    pair = [like((rows, wide), FULL), like((rows, wide), LOW)]
    block, half = like((DEEP, LANES, width), LOW), like((DEEP // 2, LANES, width), LOW)
    outs = [like((1, width), FULL)] * 2 + pair + [block] * 3 + [half] * 2

    def kernel(meta, refs, results, put, *grads):
        for x in range(2):
            low, high = sides_at[x]
            for units, _ in unit_tiles(width):
                total = jnp.zeros((1, BLOCK), FULL)
                low_w = high_w = None
                for here, block in zip(row_slices(), rows_of(refs, cot_at)):
                    if low_w is None:
                        low_w, high_w = flat(refs, low, units), flat(refs, high, units)
                    grad = nt(block[:, :HALF], low_w) + nt(block[:, HALF:], high_w)
                    grad = (grad * refs[slope_at[x]][here, units].astype(FULL)).astype(LOW)
                    grads[x][here, units] = grad
                    total = total + jnp.sum(grad.astype(FULL), axis=0, keepdims=True)
                results[x][:, units] = total
            put(x)

        terms = [
            (lambda block, left=left: left[row_slices()[block], :], pick(refs, *one), nt)
            for left, one in zip(grads, up_at)
        ]
        spread(meta[1] == 0, terms, *results[2:4], put, 2)
        for x in (1, 0):
            own, low, high = (results[6], *results[7:9]) if x else (results[4], None, None)

            def target(place, own=own, low=low, high=high):
                if place < DEEP:
                    return own.at[place]
                place -= DEEP
                return (low, high)[place // 2].at[place % 2] if low is not None else results[5].at[place]

            for units, done in unit_tiles(width):
                right = [grads[x][here, units] for here in row_slices()]
                for places, chunks in chunk_pairs():
                    block = by_tokens(rows_of(refs, normed_at, chunks), right)
                    for part, place in enumerate(places):
                        target(place)[:, units] = block[part * LANES : (part + 1) * LANES, :]
            for one in (6, 7, 8) if x else (4, 5):
                put(one)

    return call(kernel, meta, ops, outs, [pltpu.VMEM((LENGTH, width), LOW)] * 2, time=20)


def spread_kernel(meta, terms, rows, wide, product):
    ops = Operands()
    places = [(ops.add(left), at, ops.side(low), ops.side(high)) for left, at, low, high in terms]

    def kernel(meta, refs, results, put):
        def left_of(one, at):
            index = () if at is None else (at,)
            return lambda block: refs[one][(*index, row_slices()[block])]

        parts = [(left_of(one, at), pick(refs, low, high), product) for one, at, low, high in places]
        spread(meta[1] == 0, parts, *results, put, 0)

    return call(kernel, meta, ops, [like((rows, wide), FULL), like((rows, wide), LOW)], time=6)


STRIP = 128


def normalize(values):
    center = values - jnp.mean(values, axis=-1, keepdims=True)
    spread_ = jnp.mean(center * center, axis=-1, keepdims=True)
    rate = lax.rsqrt(spread_ + EPSILON)
    return center * rate, rate


def strips(rows):
    return [slice(first, first + STRIP) for first in range(0, rows, STRIP)]


def by_strips(kernel, meta, arrays, vectors, outs, sums=0):
    ops = Operands()
    rows, wide = arrays[0].shape
    halves = [slice(0, rows // 2), slice(rows // 2, rows)]
    first = [ops.add(array, halves[0]) for array in arrays]
    vector_at = [ops.add(one) for one in vectors]
    places = [first, [ops.add(array, halves[1]) for array in arrays]]
    shapes = [like((rows, wide), kind) for kind in outs]
    if sums:
        shapes.append(like((sums, wide), FULL))

    def body(meta, refs, results, put):
        parts = [None] * sums
        for at, half in zip(places, halves):
            for here in strips(rows // 2):
                kernel(
                    meta,
                    [refs[one][here, :] for one in at],
                    [refs[one][...] for one in vector_at],
                    [(result, slice(half.start + here.start, half.start + here.stop)) for result in results[: len(outs)]],
                    parts,
                )
            for one in range(len(outs)):
                put(one, half)
        if sums:
            for at, value in enumerate(parts):
                results[-1][at : at + 1, :] = jnp.sum(value, axis=0, keepdims=True)
            put(len(outs))

    return call(body, meta, ops, shapes, time=4)


def start_kernel(meta, values, vectors, results, sums):
    tokens, cot = values
    gain, shift = vectors
    hat, _ = normalize(tokens.astype(FULL))
    to_local(meta[1], *results[0], (hat * gain + shift).astype(LOW))
    to_local(meta[1], *results[1], cot.astype(LOW))


def join_kernel(meta, values, vectors, results, sums):
    tokens, own, got = values
    bias, gain, shift = vectors
    total = tokens.astype(FULL) + (own + got.astype(FULL)) + bias
    hidden, here = results[0]
    hidden[here, :] = total
    hat, _ = normalize(total)
    to_local(meta[1], *results[1], (hat * gain + shift).astype(LOW))


def add_sums(sums, values):
    for at, value in enumerate(values):
        part = jnp.sum(value.reshape(STRIP // 8, 8, value.shape[1]), axis=0)
        sums[at] = part if sums[at] is None else sums[at] + part


def norm_back(grad, values, gain):
    hat, rate = normalize(values)
    scaled = grad * gain
    row = rate * (
        scaled
        - jnp.mean(scaled, axis=-1, keepdims=True)
        - hat * jnp.mean(scaled * hat, axis=-1, keepdims=True)
    )
    return row, grad * hat


def second_kernel(meta, values, vectors, results, sums):
    own, got, hidden, pulled = values
    grad = own + got.astype(FULL)
    row, gain_part = norm_back(grad, hidden, vectors[0])
    total = pulled + row
    out, here = results[0]
    out[here, :] = total
    to_local(meta[1], *results[1], total.astype(LOW))
    add_sums(sums, [gain_part, grad, total, pulled])


def first_kernel(meta, values, vectors, results, sums):
    own, got, tokens, hidden_grad = values
    grad = own + got.astype(FULL)
    row, gain_part = norm_back(grad, tokens.astype(FULL), vectors[0])
    out, here = results[0]
    out[here, :] = hidden_grad + row
    add_sums(sums, [gain_part, grad])


def end_kernel(meta, values, vectors, results, sums):
    hidden, own, got = values
    out, here = results[0]
    out[here, :] = (hidden + (own + got.astype(FULL)) + vectors[0]).astype(LOW)


def wide_shard(shard, axis):
    return lax.all_gather(shard, "w", axis=axis, tiled=True) if lax.axis_size("w") > 1 else shard


def gather_deep(shard):
    return lax.all_gather(shard, "z", axis=0, tiled=False)


def add(*values):
    total = values[0].astype(FULL)
    for value in values[1:]:
        total = total + value.astype(FULL)
    return total.astype(LOW)


def scatter_deep(total):
    total = lax.psum_scatter(total, "z", scatter_dimension=0, tiled=False)
    if lax.axis_size("w") > 1:
        total = lax.psum_scatter(total, "w", scatter_dimension=total.ndim - 2, tiled=True)
    return total.astype(FULL)


def on_device(
    inputs,
    doc_lengths,
    first_gain,
    first_bias,
    w_query,
    b_query,
    w_key,
    w_value,
    b_value,
    w_out,
    b_out,
    second_gain,
    second_bias,
    w_up,
    b_up,
    w_down,
    b_down,
    cotangent,
):
    rows, wide = inputs.shape
    here = w_query.shape[1]
    core = lax.axis_index("c").astype(jnp.int32)
    at_y = lax.axis_index("y").astype(jnp.int32)
    at_x = lax.axis_index("x")
    lengths = lax.dynamic_index_in_dim(doc_lengths, at_x, 0, keepdims=False)
    ends = [lengths[0]]
    for one in range(1, lengths.shape[0]):
        ends.append(ends[-1] + lengths[one])
    meta = jnp.stack([core, at_y, *ends])

    def line(vector):
        return vector.reshape(1, -1)

    out_shard = wide_shard(w_out, 1)
    out_shard = jnp.concatenate([out_shard[: here // 2], out_shard[here // 2 :]], axis=1)
    attn_shard = jnp.stack([wide_shard(w_query, 0), wide_shard(w_key, 0), wide_shard(w_value, 0), out_shard])
    up_shard = wide_shard(w_up, 0)
    down_shard = wide_shard(w_down, 1)
    biases = line(jnp.concatenate([b_query, b_value, b_up]))
    far = swap(biases, "x")
    down_raw = swap_both(down_shard)
    attn_mine = after(gather_deep(attn_shard), down_raw, far)
    attn_pairs = [attn_mine[:, :2], attn_mine[:, 2:]]
    attn_x = [swap(one, "x") for one in attn_pairs]
    attn_y = [swap(one, "y") for one in attn_pairs]
    attn_far = [
        swap(after(attn_y[0], attn_y[1], *attn_x), "x"),
        swap(after(attn_x[1], attn_x[0], *attn_y), "y"),
    ]


    normed, cot = by_strips(start_kernel, meta, [inputs, cotangent], [line(first_gain), line(first_bias)], [LOW, LOW])
    normed = (normed, swap(normed, "c"))
    cot = (cot, swap(cot, "c"))

    attn_sides = [
        [(stacked_side(attn_mine, which), stacked_side(attn_y[which // 2], which % 2)) for which in range(4)],
        [(stacked_side(attn_x[which // 2], which % 2), stacked_side(attn_far[which // 2], which % 2)) for which in range(4)],
    ]

    qkv, context, logs = [None] * 2, [None] * 2, [None] * 2
    qkv[0], context[0], logs[0] = attention_forward(meta, normed, attn_sides[0][:3], biases)

    half = DEEP // 2
    up_mine = after(gather_deep(up_shard), context[0], *attn_far)
    up_parts = [up_mine[:half], up_mine[half:]]
    up_x = [swap(one, "x") for one in up_parts]
    up_y = [swap(one, "y") for one in up_parts]

    qkv[1], context[1], logs[1], own, sent = attention_forward(
        meta,
        normed,
        attn_sides[1][:3],
        far,
        (context[0], [attn_sides[0][3], attn_sides[1][3]]),
    )
    sent = after(sent, *up_x, *up_y)
    hidden, normed_two = by_strips(
        join_kernel,
        meta,
        [inputs, own, swap(sent, "c")],
        [line(b_out), line(second_gain), line(second_bias)],
        [FULL, LOW],
    )
    up_far = [swap(up_y[0], "x"), swap(up_x[1], "y")]
    normed_two = (normed_two, swap(after(normed_two, *up_far), "c"))

    up_sides = [
        (whole_side(up_mine), split_side(*up_y)),
        (split_side(*up_x), split_side(*up_far)),
    ]
    down_mine = after(gather_deep(down_shard), *up_far)
    down_x = swap(down_mine, "x")
    down_y = swap(down_mine, "y")
    down_both = gather_deep(down_raw)
    down_sides = [
        (whole_side(down_mine), whole_side(down_y)),
        (whole_side(down_x), whole_side(down_both)),
    ]
    active, slope, down_own, down_far = [None] * 2, [None] * 2, [None] * 2, [None] * 2
    (
        active[0],
        slope[0],
        down_own[0],
        down_far[0],
        active[1],
        slope[1],
        down_own[1],
        down_far[1],
    ) = up_kernel(meta, normed_two, up_sides, (biases, far), 2 * here, cot)

    *sums, own, sent, up_own, up_beyond, up_other, up_both_low, up_both_high = down_kernel(
        meta, cot, down_sides, slope, normed_two, up_sides
    )

    down_diagonal = swap_both(lax.psum_scatter(down_far[1], "z", scatter_dimension=0, tiled=False))
    down_total = add(
        down_own[0], swap(after(down_far[0], down_x, down_y), "y"), swap(after(down_own[1], down_x, down_y), "x")
    )
    owner_down = lax.psum_scatter(down_total, "z", scatter_dimension=0, tiled=False)
    owner_down = owner_down.astype(FULL) + down_diagonal.astype(FULL)
    if lax.axis_size("w") > 1:
        owner_down = lax.psum_scatter(owner_down, "w", scatter_dimension=1, tiled=True)

    got_low = swap(up_both_low, "x")
    got_high = swap(up_both_high, "y")

    hidden_grad, attn_grad, second_sums = by_strips(
        second_kernel, meta, [own, swap(sent, "c"), hidden, cotangent], [line(second_gain)], [FULL, LOW], sums=4
    )
    attn_grad = (attn_grad, swap(attn_grad, "c"))

    got_low, got_high = [after(one, attn_grad[0]).astype(FULL) for one in (got_low, got_high)]
    half = ((DEEP // 2, 0, 0), (0, 0, 0), (0, 0, 0))
    got_y = swap(add(up_beyond, lax.pad(got_low, FULL(0), ((0, DEEP // 2, 0), *half[1:]))), "y")
    got_x = swap(add(up_other, lax.pad(got_high, FULL(0), half)), "x")

    back, unit_sums = [None] * 2, [None] * 2
    back[1], unit_sums[1], attn_other_x, attn_both = attention_backward(
        meta, attn_grad, attn_sides[1][3], qkv[1], logs[1], context[1], normed
    )
    got_both = swap(attn_both, "x")
    attn_got_x = swap(attn_other_x, "x")
    back[0], unit_sums[0], attn_own, attn_beyond = attention_backward(
        meta, (after(attn_grad[0], back[1]), attn_grad[1]), attn_sides[0][3], qkv[0], logs[0], context[0], normed
    )
    attn_got_y = swap(add(attn_beyond, after(got_both, back[0])), "y")
    owner_up = scatter_deep(add(up_own, *[after(one, back[0]) for one in (got_x, got_y)]))
    last, last_sent = spread_kernel(
        meta,
        [(after(active[0], back[0]), None, *down_sides[0]), (active[1], None, *down_sides[1])],
        rows,
        wide,
        dot,
    )
    attn_total = add(attn_own, after(attn_got_x, last_sent), attn_got_y)
    owner_attn = lax.psum_scatter(attn_total, "z", scatter_dimension=0, tiled=False)
    owner_out = owner_attn[3].astype(FULL)
    owner_out = jnp.concatenate([owner_out[:, :LANES], owner_out[:, LANES:]])
    owner_attn = owner_attn[:3].astype(FULL)
    if lax.axis_size("w") > 1:
        owner_attn = lax.psum_scatter(owner_attn, "w", scatter_dimension=1, tiled=True)
        owner_out = lax.psum_scatter(owner_out, "w", scatter_dimension=1, tiled=True)

    own, sent = spread_kernel(
        meta,
        [(back[x], which, *attn_sides[x][which]) for x in range(2) for which in range(3)],
        rows,
        wide,
        nt,
    )
    input_grad, first_sums = by_strips(
        first_kernel, meta, [own, swap(sent, "c"), inputs, hidden_grad], [line(first_gain)], [FULL], sums=2
    )

    [layer_out] = by_strips(
        end_kernel, meta, [hidden, after(last, attn_total), swap(last_sent, "c")], [line(b_down)], [LOW]
    )

    replicated = all_sum(jnp.concatenate([first_sums, second_sums]).reshape(-1), "c")
    own_units, far_units = [
        jnp.concatenate([unit_sums[x][0], unit_sums[x][1], sums[x][0]]) for x in range(2)
    ]
    got = swap(jnp.concatenate([replicated, far_units]), "x")
    summed = jnp.concatenate([replicated, own_units]) + got
    summed = all_sum(summed, "y")
    summed = all_sum(summed, "z", (layer_out,), (owner_up, owner_down))
    summed = all_sum(summed, "w")
    vectors = summed[: 6 * wide].reshape(6, wide)
    units = summed[6 * wide :]

    return (
        layer_out,
        input_grad,
        vectors[0],
        vectors[1],
        owner_attn[0],
        units[:here],
        owner_attn[1],
        owner_attn[2],
        units[here : 2 * here],
        owner_out,
        vectors[4],
        vectors[2],
        vectors[3],
        owner_up,
        units[2 * here :],
        owner_down,
        vectors[5],
    )


def solution(mesh):
    groups, lanes = mesh.shape["fsdp"], mesh.shape["tp"]
    inner = Mesh(
        mesh.devices.reshape(DEEP, 2, groups // (2 * DEEP), lanes // 2, 2), ("z", "y", "w", "x", "c")
    )
    f, t = ("z", "y", "w"), ("x", "c")
    tokens, rows, columns, units = P(f + t, None), P(f, t), P(t, f), P(t)
    return jax.shard_map(
        on_device,
        mesh=inner,
        in_specs=(
            tokens,
            P(f, None),
            P(),
            P(),
            rows,
            units,
            rows,
            rows,
            units,
            columns,
            P(),
            P(),
            P(),
            rows,
            units,
            columns,
            P(),
            tokens,
        ),
        out_specs=(
            tokens,
            tokens,
            P(),
            P(),
            rows,
            units,
            rows,
            rows,
            units,
            columns,
            P(),
            P(),
            P(),
            rows,
            units,
            columns,
            P(),
        ),
        check_vma=False,
    )
```

```python
import jax
import jax.numpy as jnp
from jax import lax
from jax.experimental import pallas as pl
from jax.experimental.pallas import tpu as pltpu
from jax.sharding import Mesh, PartitionSpec as P

HEAD_DIM = 64
LENGTH = 1024
BLOCK = 256
PAIR = 2 * HEAD_DIM
EPSILON = 1e-05
SCALE = HEAD_DIM**-0.5
LOW = jnp.bfloat16
FULL = jnp.float32
SWAP = ((0, 1), (1, 0))
DEEP = 4
LANES = 128
HALF = DEEP * LANES


def swap(values, axis):
    return lax.ppermute(values, axis, SWAP)


def swap_both(values):
    return lax.ppermute(values, ("y", "x"), ((0, 3), (1, 2), (2, 1), (3, 0)))


def all_sum(values, axis, *cover):
    size, step = lax.axis_size(axis), 1
    while step < size:
        if cover:
            values, cover = after(values, *cover[0]), cover[1:]
        values = values + lax.ppermute(values, axis, [(i, i ^ step) for i in range(size)])
        step *= 2
    return values


def after(values, *others):
    return lax.optimization_barrier((values, *others))[0]


def like(shape, kind):
    return jax.ShapeDtypeStruct(shape, kind)


ALL = slice(None)


ALL = slice(None)


class Operands:
    def __init__(self):
        self.parts = []

    def add(self, array, *index):
        for at, (one, where) in enumerate(self.parts):
            if one is array and where == index:
                return at
        self.parts.append((array, index))
        return len(self.parts) - 1

    def side(self, blocks):
        return [(self.add(array), index) for array, index in blocks]


class Buffers:
    def __init__(self, buffers, copies):
        self.buffers, self.copies = buffers, dict(enumerate(copies))

    def __getitem__(self, at):
        if at in self.copies:
            self.copies.pop(at).wait()
        return self.buffers[at]


def call(kernel, meta, ops, outs, scratch=(), time=3, limit=60):
    arrays = []
    for array, _ in ops.parts:
        if not any(array is one for one in arrays):
            arrays.append(array)
    source = [next(at for at, one in enumerate(arrays) if one is array) for array, _ in ops.parts]
    blocks = [jax.eval_shape(lambda a, index=index: a[index], like(array.shape, array.dtype)) for array, index in ops.parts]
    count, parts, results = len(arrays), len(ops.parts), len(outs)

    def body(*refs):
        meta_ref, sources, targets = refs[0], refs[1 : 1 + count], refs[1 + count : 1 + count + results]
        rest = refs[1 + count + results :]
        buffers, copies = rest[:parts], rest[parts : parts + results]
        in_sems, out_sems, *extra = rest[parts + results :]
        fetches = []
        for at, (_, index) in enumerate(ops.parts):
            ref = sources[source[at]]
            fetches.append(pltpu.make_async_copy(ref.at[index] if index else ref, buffers[at], in_sems.at[at]))
            fetches[-1].start()
        sent = []

        def put(at, *index):
            one, two = (copies[at].at[index], targets[at].at[index]) if index else (copies[at], targets[at])
            sent.append(pltpu.make_async_copy(one, two, out_sems.at[len(sent)]))
            sent[-1].start()

        kernel(meta_ref, Buffers(buffers, fetches), copies, put, *extra)
        for one in sent:
            one.wait()

    whole = pl.BlockSpec(memory_space=pl.ANY)
    return pl.pallas_call(
        body,
        out_shape=outs,
        in_specs=[pl.BlockSpec(memory_space=pltpu.SMEM)] + [whole] * count,
        out_specs=[whole] * results,
        scratch_shapes=[pltpu.VMEM(one.shape, one.dtype) for one in blocks]
        + [pltpu.VMEM(one.shape, one.dtype) for one in outs]
        + [pltpu.SemaphoreType.DMA((parts,)), pltpu.SemaphoreType.DMA((64,))]
        + list(scratch),
        compiler_params=pltpu.CompilerParams(vmem_limit_bytes=limit << 20),
        cost_estimate=pl.CostEstimate(flops=time << 20, bytes_accessed=1 << 16, transcendentals=0),
    )(meta, *arrays)


def whole_side(array):
    return [(array, (z,)) for z in range(DEEP)]


def stacked_side(array, which):
    return [(array, (z, which)) for z in range(DEEP)]


def split_side(low, high):
    return [((low, high)[z // 2], (z % 2,)) for z in range(DEEP)]


def dot(left, right):
    return jnp.dot(left, right, preferred_element_type=FULL)


def nt(left, right):
    return lax.dot_general(left, right, (((1,), (1,)), ((), ())), preferred_element_type=FULL)


def tn(left, right):
    return lax.dot_general(left, right, (((0,), (0,)), ((), ())), preferred_element_type=FULL)


def tall(refs, side, units=ALL):
    return jnp.concatenate([refs[at][(*index, ALL, units)] for at, index in side], axis=0)


def flat(refs, side, units):
    return jnp.concatenate([refs[at][(*index, units)] for at, index in side], axis=1)


def unfold(block):
    return jnp.concatenate([block[:, :LANES], block[:, LANES:]], axis=0)


def row_slices(count=LENGTH // BLOCK):
    return [slice(at * BLOCK, (at + 1) * BLOCK) for at in range(count)]


def rows_of(refs, pair, columns=ALL):
    for at in pair:
        for first in range(0, refs[at].shape[0], BLOCK):
            yield refs[at][first : first + BLOCK, columns]


def chunk_pairs():
    for first in range(0, 2 * DEEP, 2):
        yield (first, first + 1), slice(first * LANES, (first + 2) * LANES)


def by_tokens(lefts, rights):
    total = None
    for left, right in zip(lefts, rights):
        part = tn(left, right)
        total = part if total is None else total + part
    return total.astype(LOW)


def spread(even, terms, own, far, put, at):
    rows = own.shape[0]
    for z in range(DEEP):
        columns = slice(2 * z * LANES, 2 * (z + 1) * LANES)
        rights = []
        for _, chunks, product in terms:
            one, two = chunks(z)
            pair = [jnp.where(even, one, two), jnp.where(even, two, one)]
            rights.append(jnp.concatenate(pair, axis=0 if product is nt else 1))
        for block, here in enumerate(row_slices()):
            total = None
            for (left, _, product), right in zip(terms, rights):
                part = product(left(block), right)
                total = part if total is None else total + part
            if here.start < rows:
                own[here, columns] = total.astype(LOW)
            else:
                far[here.start - rows : here.stop - rows, columns] = total.astype(LOW)
        if z % 2:
            done = slice(columns.stop - 4 * LANES, columns.stop)
            put(at, ALL, done)
            put(at + 1, ALL, done)


def pick(refs, low, high, change=lambda block: block):
    return lambda z: [change(refs[at][one]) for at, one in (low[z], high[z])]


def to_local(at_y, target, rows, values):
    for chunk in range(2 * DEEP):
        place = chunk // 2 + DEEP * lax.rem(chunk + at_y, 2)
        columns = pl.ds(pl.multiple_of(place * LANES, LANES), LANES)
        target[rows, columns] = values[:, chunk * LANES : (chunk + 1) * LANES]


def row_ranges():
    for first in range(0, LENGTH, BLOCK):
        yield first, max(0, first - LENGTH // 2), first + BLOCK


def ordered(ref, which, core, columns):
    half = LENGTH // 2
    start = pl.multiple_of(core * half, half)
    rest = pl.multiple_of((1 - core) * half, half)
    return jnp.concatenate([ref[which, pl.ds(start, half), columns], ref[which, pl.ds(rest, half), columns]], axis=0)


def local_row(first, core):
    return pl.multiple_of(lax.rem(first + core * (LENGTH // 2), LENGTH), BLOCK)


def allowed_tile(meta, first, low, high):
    shape = (BLOCK, high - low)
    places = first + lax.broadcasted_iota(jnp.int32, (BLOCK, 1), 0)
    start = jnp.zeros((BLOCK, 1), jnp.int32)
    for at in range(2, meta.shape[0]):
        start = jnp.where(places >= meta[at], meta[at], start)
    keys = low + lax.broadcasted_iota(jnp.int32, shape, 1)
    return (keys <= places) & (keys >= start)


def first_lanes():
    return lax.broadcasted_iota(jnp.int32, (BLOCK, PAIR), 1) < HEAD_DIM


def attend(meta, qkv, context, logs, put):
    core = meta[0]
    first_head = first_lanes()
    for pair in range(context.shape[1] // PAIR):
        columns = slice(pair * PAIR, (pair + 1) * PAIR)
        keys = ordered(qkv, 1, core, columns)
        values = ordered(qkv, 2, core, columns)
        values = jnp.concatenate([values, jnp.ones_like(values)], axis=1)
        for first, low, high in row_ranges():
            here = local_row(first, core)
            query = qkv[0, pl.ds(here, BLOCK), columns] * SCALE
            allowed = allowed_tile(meta, first, low, high)
            outs = []
            sums = []
            for head in range(2):
                picked = jnp.where(first_head if head == 0 else ~first_head, query, jnp.zeros_like(query))
                scores = jnp.where(allowed, nt(picked, keys[low:high]), -1e30)
                highest = jnp.max(scores, axis=-1, keepdims=True)
                mixed = dot(jnp.exp(scores - highest).astype(LOW), values[low:high])
                totals = mixed[:, PAIR:]
                outs.append(mixed[:, :PAIR] / totals)
                sums.append(highest + jnp.log(totals))
            context[pl.ds(here, BLOCK), columns] = jnp.where(first_head, outs[0], outs[1]).astype(LOW)
            logs[pl.ds(here, BLOCK), columns] = jnp.where(first_head, sums[0], sums[1])
        put(1, ALL, columns)
        put(2, ALL, columns)


def attend_back(meta, qkv, logs, grads, out, sums, key_sum, value_sum):
    core = meta[0]
    first_head = first_lanes()
    half = LENGTH // 2
    for pair in range(grads.shape[1] // PAIR):
        columns = slice(pair * PAIR, (pair + 1) * PAIR)
        keys = ordered(qkv, 1, core, columns)
        values = ordered(qkv, 2, core, columns)
        key_sum[...] = jnp.zeros_like(key_sum)
        value_sum[...] = jnp.zeros_like(value_sum)
        query_total = value_total = jnp.zeros((1, PAIR), FULL)
        for first, low, high in row_ranges():
            here = local_row(first, core)
            query = qkv[0, pl.ds(here, BLOCK), columns] * SCALE
            grad = grads[pl.ds(here, BLOCK), columns]
            log_pair = logs[pl.ds(here, BLOCK), columns]
            allowed = allowed_tile(meta, first, low, high)
            query_flip = query.T
            grad_flip = grad.T
            outs = []
            for head in range(2):
                mask = first_head if head == 0 else ~first_head
                band = slice(head * HEAD_DIM, (head + 1) * HEAD_DIM)
                query_one = jnp.where(mask, query, jnp.zeros_like(query))
                grad_one = jnp.where(mask, grad, jnp.zeros_like(grad))
                log_one = log_pair[:, head * HEAD_DIM : head * HEAD_DIM + 1]
                scores = jnp.where(allowed, nt(query_one, keys[low:high]), -1e30)
                weights = jnp.exp(scores - log_one)
                grad_probs = nt(grad_one, values[low:high])
                inner = jnp.sum(grad_probs * weights, axis=-1, keepdims=True)
                grad_scores = (weights * (grad_probs - inner)).astype(LOW)
                outs.append(dot(grad_scores, keys[low:high]))
                key_sum[band, low:high] += dot(query_flip[band, :], grad_scores)
                value_sum[band, low:high] += dot(grad_flip[band, :], weights.astype(LOW))
            grad_query = (jnp.where(first_head, outs[0], outs[1]) * SCALE).astype(LOW)
            out[0, pl.ds(here, BLOCK), columns] = grad_query
            query_total = query_total + jnp.sum(grad_query.astype(FULL), axis=0, keepdims=True)
        for part in range(2):
            there = pl.multiple_of(lax.rem(part + core, 2) * half, half)
            out[1, pl.ds(there, half), columns] = key_sum[:, part * half : (part + 1) * half].T.astype(LOW)
            grad_value = value_sum[:, part * half : (part + 1) * half].T.astype(LOW)
            out[2, pl.ds(there, half), columns] = grad_value
            value_total = value_total + jnp.sum(grad_value.astype(FULL), axis=0, keepdims=True)
        sums[0:1, columns] = query_total
        sums[1:2, columns] = value_total


def attention_forward(meta, normed, sides, biases, last=None):
    ops = Operands()
    normed_at = [ops.add(normed[0])]
    sides_at = [[ops.side(one) for one in pair] for pair in sides]
    bias_at = ops.add(biases)
    normed_at.append(ops.add(normed[1]))
    width = sides[0][0][0][0].shape[-1]
    rows, wide = normed[0].shape
    outs = [like((3, LENGTH, width), LOW), like((LENGTH, width), LOW), like((LENGTH, width), FULL)]
    if last:
        first_at = ops.add(last[0])
        out_sides = [[ops.side(one) for one in pair] for pair in last[1]]
        outs += [like((rows, wide), LOW), like((rows, wide), LOW)]

    def kernel(meta, refs, results, put):
        qkv, context, logs = results[:3]
        for which, (low, high) in enumerate(sides_at):
            low_w = high_w = None
            for here, block in zip(row_slices(), rows_of(refs, normed_at)):
                if low_w is None:
                    low_w, high_w = tall(refs, low), tall(refs, high)
                total = dot(block[:, :HALF], low_w) + dot(block[:, HALF:], high_w)
                if which != 1:
                    total = total + refs[bias_at][:, which // 2 * width : (which // 2 + 1) * width]
                qkv[which, here, :] = total.astype(LOW)
        put(0)
        attend(meta, qkv, context, logs, put)
        if last:
            terms = [
                (lambda block, left=left: left[row_slices()[block], :], pick(refs, *pair, unfold), dot)
                for left, pair in zip((refs[first_at], context), out_sides)
            ]
            spread(meta[1] == 0, terms, *results[3:], put, 3)

    return call(kernel, meta, ops, outs, time=12 if last else 8)


def attention_backward(meta, grad, side, qkv, logs, context, normed, split):
    ops = Operands()
    grad_at = [ops.add(grad[0])]
    low, high = [[(ops.add(array, ALL, index[1]), (z,)) for z, (array, index) in enumerate(one)] for one in side]
    grad_at.append(ops.add(grad[1]))
    qkv_at, log_at = [ops.add(one) for one in (qkv, logs)]
    normed_at = [ops.add(one) for one in normed]
    context_at = ops.add(context)
    width = context.shape[1]
    blocks, half = like((DEEP, 4, LANES, width), LOW), like((DEEP // 2, 4, LANES, width), LOW)
    far = [half, half] if split else [blocks]

    def kernel(meta, refs, results, put, grads, key_sum, value_sum):
        out, sums = results[:2]

        def target(place):
            if place < DEEP or not split:
                return results[2 + place // DEEP].at[place % DEEP]
            return results[3 + place // 2 - DEEP // 2].at[place % 2]

        low_w = high_w = None
        for here, block in zip(row_slices(), rows_of(refs, grad_at)):
            if low_w is None:
                low_w, high_w = [
                    jnp.concatenate([unfold(refs[at][index]) for at, index in one], axis=1) for one in (low, high)
                ]
            grads[here, :] = (nt(block[:, :HALF], low_w) + nt(block[:, HALF:], high_w)).astype(LOW)
        attend_back(meta, refs[qkv_at], refs[log_at], grads, out, sums, key_sum, value_sum)
        put(0)
        put(1)
        for which in range(3):
            right = [out[which, here, :] for here in row_slices()]
            for places, columns in chunk_pairs():
                block = by_tokens(rows_of(refs, normed_at, columns), right)
                for part, place in enumerate(places):
                    target(place)[which] = block[part * LANES : (part + 1) * LANES, :]
            for one in range(2, 3 + len(far)):
                put(one, ALL, which)
        left = [refs[context_at][here, :] for here in row_slices()]
        for places, columns in chunk_pairs():
            block = by_tokens(left, rows_of(refs, grad_at, columns))
            for part, place in enumerate(places):
                one = block[:, part * LANES : (part + 1) * LANES]
                target(place)[3] = jnp.concatenate([one[:LANES], one[LANES:]], axis=1)
        for one in range(2, 3 + len(far)):
            put(one, ALL, 3)

    return call(
        kernel,
        meta,
        ops,
        [like((3, LENGTH, width), LOW), like((2, width), FULL), blocks] + far,
        [pltpu.VMEM((LENGTH, width), LOW)] + [pltpu.VMEM((PAIR, LENGTH), FULL)] * 2,
        time=15,
    )


def unit_tiles(width):
    for first in range(0, width, BLOCK):
        stop = first + BLOCK
        yield slice(first, stop), slice(stop - width // 2, stop) if stop % (width // 2) == 0 else None


def up_kernel(meta, normed, sides, biases, at, cot):
    ops = Operands()
    normed_at = [ops.add(normed[0])]
    sides_at, bias_at = [[ops.side(one) for one in sides[0]]], [ops.add(biases[0])]
    normed_at.append(ops.add(normed[1]))
    cot_at = [ops.add(one) for one in cot]
    sides_at.append([ops.side(one) for one in sides[1]])
    bias_at.append(ops.add(biases[1]))
    width = sides[0][0][0][0].shape[-1]
    blocks = like((DEEP, width, LANES), LOW)

    def kernel(meta, refs, results, put):
        for x in range(2):
            active, slope, *grads = results[4 * x : 4 * x + 4]
            low, high = sides_at[x]
            for units, done in unit_tiles(width):
                low_w = high_w = None
                for here, block in zip(row_slices(), rows_of(refs, normed_at)):
                    if low_w is None:
                        low_w, high_w = tall(refs, low, units), tall(refs, high, units)
                    before = dot(block[:, :HALF], low_w) + dot(block[:, HALF:], high_w)
                    before = before + refs[bias_at[x]][:, at + units.start : at + units.stop]
                    phi = 0.5 * (1.0 + lax.erf(before * (2.0**-0.5)))
                    active[here, units] = (before * phi).astype(LOW)
                    bell = jnp.exp(-0.5 * before * before) * (2.0 * jnp.pi) ** -0.5
                    slope[here, units] = (phi + before * bell).astype(LOW)
                left = [active[here, units] for here in row_slices()]
                for places, chunks in chunk_pairs():
                    block = by_tokens(left, rows_of(refs, cot_at, chunks))
                    for part, place in enumerate(places):
                        grads[place // DEEP][place % DEEP, units, :] = block[:, part * LANES : (part + 1) * LANES]
                if done:
                    for one in range(4 * x, 4 * x + 4):
                        put(one, ALL, done)

    return call(kernel, meta, ops, ([like((LENGTH, width), LOW)] * 2 + [blocks] * 2) * 2, time=18)


def down_kernel(meta, cot, sides, slopes, normed, up_sides):
    ops = Operands()
    rows, wide = normed[0].shape
    width = slopes[0].shape[1]
    cot_at = [ops.add(cot[0])]
    sides_at, slope_at = [[ops.side(one) for one in sides[0]]], [ops.add(slopes[0])]
    cot_at.append(ops.add(cot[1]))
    sides_at.append([ops.side(one) for one in sides[1]])
    slope_at.append(ops.add(slopes[1]))
    up_at = [[ops.side(one) for one in pair] for pair in up_sides]
    normed_at = [ops.add(one) for one in normed]
    pair = [like((rows, wide), LOW), like((rows, wide), LOW)]
    block, half = like((DEEP, LANES, width), LOW), like((DEEP // 2, LANES, width), LOW)
    outs = [like((1, width), FULL)] * 2 + pair + [block] * 3 + [half] * 2

    def kernel(meta, refs, results, put, *grads):
        for x in range(2):
            low, high = sides_at[x]
            for units, _ in unit_tiles(width):
                total = jnp.zeros((1, BLOCK), FULL)
                low_w = high_w = None
                for here, block in zip(row_slices(), rows_of(refs, cot_at)):
                    if low_w is None:
                        low_w, high_w = flat(refs, low, units), flat(refs, high, units)
                    grad = nt(block[:, :HALF], low_w) + nt(block[:, HALF:], high_w)
                    grad = (grad * refs[slope_at[x]][here, units].astype(FULL)).astype(LOW)
                    grads[x][here, units] = grad
                    total = total + jnp.sum(grad.astype(FULL), axis=0, keepdims=True)
                results[x][:, units] = total
            put(x)

        terms = [
            (lambda block, left=left: left[row_slices()[block], :], pick(refs, *one), nt)
            for left, one in zip(grads, up_at)
        ]
        spread(meta[1] == 0, terms, *results[2:4], put, 2)
        for x in (1, 0):
            own, low, high = (results[6], *results[7:9]) if x else (results[4], None, None)

            def target(place, own=own, low=low, high=high):
                if place < DEEP:
                    return own.at[place]
                place -= DEEP
                return (low, high)[place // 2].at[place % 2] if low is not None else results[5].at[place]

            for units, done in unit_tiles(width):
                right = [grads[x][here, units] for here in row_slices()]
                for places, chunks in chunk_pairs():
                    block = by_tokens(rows_of(refs, normed_at, chunks), right)
                    for part, place in enumerate(places):
                        target(place)[:, units] = block[part * LANES : (part + 1) * LANES, :]
                if done:
                    for one in (6, 7, 8) if x else (4, 5):
                        put(one, ALL, ALL, done)

    return call(kernel, meta, ops, outs, [pltpu.VMEM((LENGTH, width), LOW)] * 2, time=20)


def spread_kernel(meta, terms, rows, wide, product):
    ops = Operands()
    places = [(ops.add(left), at, ops.side(low), ops.side(high)) for left, at, low, high in terms]

    def kernel(meta, refs, results, put):
        def left_of(one, at):
            index = () if at is None else (at,)
            return lambda block: refs[one][(*index, row_slices()[block])]

        parts = [(left_of(one, at), pick(refs, low, high), product) for one, at, low, high in places]
        spread(meta[1] == 0, parts, *results, put, 0)

    return call(kernel, meta, ops, [like((rows, wide), LOW), like((rows, wide), LOW)], time=6)


STRIP = 128


def normalize(values):
    center = values - jnp.mean(values, axis=-1, keepdims=True)
    spread_ = jnp.mean(center * center, axis=-1, keepdims=True)
    rate = lax.rsqrt(spread_ + EPSILON)
    return center * rate, rate


def strips(rows):
    return [slice(first, first + STRIP) for first in range(0, rows, STRIP)]


def by_strips(kernel, meta, arrays, vectors, outs, sums=0):
    ops = Operands()
    rows, wide = arrays[0].shape
    halves = [slice(0, rows // 2), slice(rows // 2, rows)]
    first = [ops.add(array, halves[0]) for array in arrays]
    vector_at = [ops.add(one) for one in vectors]
    places = [first, [ops.add(array, halves[1]) for array in arrays]]
    shapes = [like((rows, wide), kind) for kind in outs]
    if sums:
        shapes.append(like((sums, wide), FULL))

    def body(meta, refs, results, put):
        parts = [None] * sums
        for at, half in zip(places, halves):
            for here in strips(rows // 2):
                kernel(
                    meta,
                    [refs[one][here, :] for one in at],
                    [refs[one][...] for one in vector_at],
                    [(result, slice(half.start + here.start, half.start + here.stop)) for result in results[: len(outs)]],
                    parts,
                )
            for one in range(len(outs)):
                put(one, half)
        if sums:
            for at, value in enumerate(parts):
                results[-1][at : at + 1, :] = jnp.sum(value, axis=0, keepdims=True)
            put(len(outs))

    return call(body, meta, ops, shapes, time=4)


def start_kernel(meta, values, vectors, results, sums):
    tokens, cot = values
    gain, shift = vectors
    hat, _ = normalize(tokens.astype(FULL))
    to_local(meta[1], *results[0], (hat * gain + shift).astype(LOW))
    to_local(meta[1], *results[1], cot.astype(LOW))


def join_kernel(meta, values, vectors, results, sums):
    tokens, own, got = values
    bias, gain, shift = vectors
    total = tokens.astype(FULL) + (own.astype(FULL) + got.astype(FULL)) + bias
    hidden, here = results[0]
    hidden[here, :] = total
    hat, _ = normalize(total)
    to_local(meta[1], *results[1], (hat * gain + shift).astype(LOW))


def add_sums(sums, values):
    for at, value in enumerate(values):
        part = jnp.sum(value.reshape(STRIP // 8, 8, value.shape[1]), axis=0)
        sums[at] = part if sums[at] is None else sums[at] + part


def norm_back(grad, values, gain):
    hat, rate = normalize(values)
    scaled = grad * gain
    row = rate * (
        scaled
        - jnp.mean(scaled, axis=-1, keepdims=True)
        - hat * jnp.mean(scaled * hat, axis=-1, keepdims=True)
    )
    return row, grad * hat


def second_kernel(meta, values, vectors, results, sums):
    own, got, hidden, pulled = values
    grad = own.astype(FULL) + got.astype(FULL)
    row, gain_part = norm_back(grad, hidden, vectors[0])
    total = pulled + row
    out, here = results[0]
    out[here, :] = total
    to_local(meta[1], *results[1], total.astype(LOW))
    add_sums(sums, [gain_part, grad, total, pulled])


def first_kernel(meta, values, vectors, results, sums):
    own, got, tokens, hidden_grad = values
    grad = own.astype(FULL) + got.astype(FULL)
    row, gain_part = norm_back(grad, tokens.astype(FULL), vectors[0])
    out, here = results[0]
    out[here, :] = hidden_grad + row
    add_sums(sums, [gain_part, grad])


def end_kernel(meta, values, vectors, results, sums):
    hidden, own, got = values
    out, here = results[0]
    out[here, :] = (hidden + (own.astype(FULL) + got.astype(FULL)) + vectors[0]).astype(LOW)


def wide_shard(shard, axis):
    return lax.all_gather(shard, "w", axis=axis, tiled=True) if lax.axis_size("w") > 1 else shard


def gather_deep(shard):
    return lax.all_gather(shard, "z", axis=0, tiled=False)


def add(*values):
    total = values[0].astype(FULL)
    for value in values[1:]:
        total = total + value.astype(FULL)
    return total.astype(LOW)


def add_half(whole, part, which):
    size = part.shape[0]
    edges = [(size * which, size * (1 - which), 0)] + [(0, 0, 0)] * (part.ndim - 1)
    return add(whole, lax.pad(part.astype(FULL), FULL(0), edges))


def scatter_deep(total):
    total = lax.psum_scatter(total, "z", scatter_dimension=0, tiled=False)
    if lax.axis_size("w") > 1:
        total = lax.psum_scatter(total, "w", scatter_dimension=total.ndim - 2, tiled=True)
    return total.astype(FULL)


def on_device(
    inputs,
    doc_lengths,
    first_gain,
    first_bias,
    w_query,
    b_query,
    w_key,
    w_value,
    b_value,
    w_out,
    b_out,
    second_gain,
    second_bias,
    w_up,
    b_up,
    w_down,
    b_down,
    cotangent,
):
    rows, wide = inputs.shape
    here = w_query.shape[1]
    core = lax.axis_index("c").astype(jnp.int32)
    at_y = lax.axis_index("y").astype(jnp.int32)
    at_x = lax.axis_index("x")
    lengths = lax.dynamic_index_in_dim(doc_lengths, at_x, 0, keepdims=False)
    ends = [lengths[0]]
    for one in range(1, lengths.shape[0]):
        ends.append(ends[-1] + lengths[one])
    meta = jnp.stack([core, at_y, *ends])

    def line(vector):
        return vector.reshape(1, -1)

    out_shard = wide_shard(w_out, 1)
    out_shard = jnp.concatenate([out_shard[: here // 2], out_shard[here // 2 :]], axis=1)
    attn_shard = jnp.stack([wide_shard(w_query, 0), wide_shard(w_key, 0), wide_shard(w_value, 0), out_shard])
    up_shard = wide_shard(w_up, 0)
    down_shard = wide_shard(w_down, 1)
    biases = line(jnp.concatenate([b_query, b_value, b_up]))
    far = swap(biases, "x")
    down_raw = swap_both(down_shard)
    attn_mine = after(gather_deep(attn_shard), down_raw, far)
    attn_pairs = [attn_mine[:, :2], attn_mine[:, 2:]]
    attn_x = [swap(one, "x") for one in attn_pairs]
    attn_y = [swap(one, "y") for one in attn_pairs]
    attn_far = [
        swap(after(attn_y[0], attn_y[1], *attn_x), "x"),
        swap(after(attn_x[1], attn_x[0], *attn_y), "y"),
    ]


    normed, cot = by_strips(start_kernel, meta, [inputs, cotangent], [line(first_gain), line(first_bias)], [LOW, LOW])
    normed = (normed, swap(normed, "c"))
    cot = (cot, swap(cot, "c"))

    attn_sides = [
        [(stacked_side(attn_mine, which), stacked_side(attn_y[which // 2], which % 2)) for which in range(4)],
        [(stacked_side(attn_x[which // 2], which % 2), stacked_side(attn_far[which // 2], which % 2)) for which in range(4)],
    ]

    qkv, context, logs = [None] * 2, [None] * 2, [None] * 2
    qkv[0], context[0], logs[0] = attention_forward(meta, normed, attn_sides[0][:3], biases)

    half = DEEP // 2
    up_mine = after(gather_deep(up_shard), context[0], *attn_far)
    up_parts = [up_mine[:half], up_mine[half:]]
    up_x = [swap(one, "x") for one in up_parts]
    up_y = [swap(one, "y") for one in up_parts]

    qkv[1], context[1], logs[1], own, sent = attention_forward(
        meta,
        normed,
        attn_sides[1][:3],
        far,
        (context[0], [attn_sides[0][3], attn_sides[1][3]]),
    )
    sent = after(sent, *up_x, *up_y)
    hidden, normed_two = by_strips(
        join_kernel,
        meta,
        [inputs, own, swap(sent, "c")],
        [line(b_out), line(second_gain), line(second_bias)],
        [FULL, LOW],
    )
    up_far = [swap(up_y[0], "x"), swap(up_x[1], "y")]
    normed_two = (normed_two, swap(after(normed_two, *up_far), "c"))

    up_sides = [
        (whole_side(up_mine), split_side(*up_y)),
        (split_side(*up_x), split_side(*up_far)),
    ]
    down_mine = after(gather_deep(down_shard), *up_far)
    down_x = swap(down_mine, "x")
    down_y = swap(down_mine, "y")
    down_both = gather_deep(down_raw)
    down_sides = [
        (whole_side(down_mine), whole_side(down_y)),
        (whole_side(down_x), whole_side(down_both)),
    ]
    active, slope, down_own, down_far = [None] * 2, [None] * 2, [None] * 2, [None] * 2
    (
        active[0],
        slope[0],
        down_own[0],
        down_far[0],
        active[1],
        slope[1],
        down_own[1],
        down_far[1],
    ) = up_kernel(meta, normed_two, up_sides, (biases, far), 2 * here, cot)

    *sums, own, sent, up_own, up_beyond, up_other, up_both_low, up_both_high = down_kernel(
        meta, cot, down_sides, slope, normed_two, up_sides
    )

    down_diagonal = swap_both(lax.psum_scatter(down_far[1], "z", scatter_dimension=0, tiled=False))
    down_total = add(
        down_own[0], swap(after(down_far[0], down_x, down_y), "y"), swap(after(down_own[1], down_x, down_y), "x")
    )
    owner_down = lax.psum_scatter(down_total, "z", scatter_dimension=0, tiled=False)
    owner_down = owner_down.astype(FULL) + down_diagonal.astype(FULL)
    if lax.axis_size("w") > 1:
        owner_down = lax.psum_scatter(owner_down, "w", scatter_dimension=1, tiled=True)

    got_low = swap(up_both_low, "x")
    got_high = swap(up_both_high, "y")

    hidden_grad, attn_grad, second_sums = by_strips(
        second_kernel, meta, [own, swap(sent, "c"), hidden, cotangent], [line(second_gain)], [FULL, LOW], sums=4
    )
    attn_grad = (attn_grad, swap(attn_grad, "c"))

    got_low, got_high = [after(one, attn_grad[0]).astype(FULL) for one in (got_low, got_high)]
    half = ((DEEP // 2, 0, 0), (0, 0, 0), (0, 0, 0))
    got_y = swap(add(up_beyond, lax.pad(got_low, FULL(0), ((0, DEEP // 2, 0), *half[1:]))), "y")
    got_x = swap(add(up_other, lax.pad(got_high, FULL(0), half)), "x")

    back, unit_sums = [None] * 2, [None] * 2
    back[1], unit_sums[1], attn_other, attn_both_low, attn_both_high = attention_backward(
        meta, attn_grad, attn_sides[1][3], qkv[1], logs[1], context[1], normed, True
    )
    attn_low = swap(attn_both_low, "x")
    attn_high = swap(attn_both_high, "y")
    back[0], unit_sums[0], attn_own, attn_beyond = attention_backward(
        meta, (after(attn_grad[0], back[1]), attn_grad[1]), attn_sides[0][3], qkv[0], logs[0], context[0], normed, False
    )
    send_y = add_half(attn_beyond, after(attn_low, back[0]), 0)
    send_x = add_half(attn_other, after(attn_high, back[0]), 1)
    attn_got_y, attn_got_x = swap(send_y, "y"), swap(send_x, "x")
    owner_up = scatter_deep(add(up_own, *[after(one, back[0]) for one in (got_x, got_y)]))
    last, last_sent = spread_kernel(
        meta,
        [(after(active[0], back[0]), None, *down_sides[0]), (active[1], None, *down_sides[1])],
        rows,
        wide,
        dot,
    )
    attn_total = add(attn_own, after(attn_got_x, last_sent), attn_got_y)
    owner_attn = lax.psum_scatter(attn_total, "z", scatter_dimension=0, tiled=False)
    owner_out = owner_attn[3].astype(FULL)
    owner_out = jnp.concatenate([owner_out[:, :LANES], owner_out[:, LANES:]])
    owner_attn = owner_attn[:3].astype(FULL)
    if lax.axis_size("w") > 1:
        owner_attn = lax.psum_scatter(owner_attn, "w", scatter_dimension=1, tiled=True)
        owner_out = lax.psum_scatter(owner_out, "w", scatter_dimension=1, tiled=True)

    own, sent = spread_kernel(
        meta,
        [(back[x], which, *attn_sides[x][which]) for x in range(2) for which in range(3)],
        rows,
        wide,
        nt,
    )
    input_grad, first_sums = by_strips(
        first_kernel, meta, [own, swap(sent, "c"), inputs, hidden_grad], [line(first_gain)], [FULL], sums=2
    )

    [layer_out] = by_strips(
        end_kernel, meta, [hidden, after(last, attn_total), swap(last_sent, "c")], [line(b_down)], [LOW]
    )

    replicated = all_sum(jnp.concatenate([first_sums, second_sums]).reshape(-1), "c")
    own_units, far_units = [
        jnp.concatenate([unit_sums[x][0], unit_sums[x][1], sums[x][0]]) for x in range(2)
    ]
    got = swap(jnp.concatenate([replicated, far_units]), "x")
    summed = jnp.concatenate([replicated, own_units]) + got
    summed = all_sum(summed, "y", (layer_out,))
    summed = all_sum(summed, "z", (owner_down,), (owner_up,))
    summed = all_sum(summed, "w")
    vectors = summed[: 6 * wide].reshape(6, wide)
    units = summed[6 * wide :]

    return (
        layer_out,
        input_grad,
        vectors[0],
        vectors[1],
        owner_attn[0],
        units[:here],
        owner_attn[1],
        owner_attn[2],
        units[here : 2 * here],
        owner_out,
        vectors[4],
        vectors[2],
        vectors[3],
        owner_up,
        units[2 * here :],
        owner_down,
        vectors[5],
    )


def solution(mesh):
    groups, lanes = mesh.shape["fsdp"], mesh.shape["tp"]
    inner = Mesh(
        mesh.devices.reshape(DEEP, 2, groups // (2 * DEEP), lanes // 2, 2), ("z", "y", "w", "x", "c")
    )
    f, t = ("z", "y", "w"), ("x", "c")
    tokens, rows, columns, units = P(f + t, None), P(f, t), P(t, f), P(t)
    return jax.shard_map(
        on_device,
        mesh=inner,
        in_specs=(
            tokens,
            P(f, None),
            P(),
            P(),
            rows,
            units,
            rows,
            rows,
            units,
            columns,
            P(),
            P(),
            P(),
            rows,
            units,
            columns,
            P(),
            tokens,
        ),
        out_specs=(
            tokens,
            tokens,
            P(),
            P(),
            rows,
            units,
            rows,
            rows,
            units,
            columns,
            P(),
            P(),
            P(),
            rows,
            units,
            columns,
            P(),
        ),
        check_vma=False,
    )
```

```python
import jax
import jax.numpy as jnp
from jax import lax
from jax.experimental import pallas as pl
from jax.experimental.pallas import tpu as pltpu
from jax.sharding import Mesh, PartitionSpec as P

HEAD_DIM = 64
LENGTH = 1024
BLOCK = 256
PAIR = 2 * HEAD_DIM
EPSILON = 1e-05
SCALE = HEAD_DIM**-0.5
LOW = jnp.bfloat16
FULL = jnp.float32
SWAP = ((0, 1), (1, 0))
DEEP = 4
LANES = 128
HALF = DEEP * LANES


def swap(values, axis):
    return lax.ppermute(values, axis, SWAP)


def swap_both(values):
    return lax.ppermute(values, ("y", "x"), ((0, 3), (1, 2), (2, 1), (3, 0)))


def all_sum(values, axis, *cover):
    size, step = lax.axis_size(axis), 1
    while step < size:
        if cover:
            values, cover = after(values, *cover[0]), cover[1:]
        values = values + lax.ppermute(values, axis, [(i, i ^ step) for i in range(size)])
        step *= 2
    return values


def after(values, *others):
    return lax.optimization_barrier((values, *others))[0]


def like(shape, kind):
    return jax.ShapeDtypeStruct(shape, kind)


ALL = slice(None)


ALL = slice(None)


class Operands:
    def __init__(self):
        self.parts = []

    def add(self, array, *index):
        for at, (one, where) in enumerate(self.parts):
            if one is array and where == index:
                return at
        self.parts.append((array, index))
        return len(self.parts) - 1

    def side(self, blocks):
        return [(self.add(array), index) for array, index in blocks]


class Buffers:
    def __init__(self, buffers, copies):
        self.buffers, self.copies = buffers, dict(enumerate(copies))

    def __getitem__(self, at):
        if at in self.copies:
            self.copies.pop(at).wait()
        return self.buffers[at]


def call(kernel, meta, ops, outs, scratch=(), time=3, limit=60):
    arrays = []
    for array, _ in ops.parts:
        if not any(array is one for one in arrays):
            arrays.append(array)
    source = [next(at for at, one in enumerate(arrays) if one is array) for array, _ in ops.parts]
    blocks = [jax.eval_shape(lambda a, index=index: a[index], like(array.shape, array.dtype)) for array, index in ops.parts]
    count, parts, results = len(arrays), len(ops.parts), len(outs)

    def body(*refs):
        meta_ref, sources, targets = refs[0], refs[1 : 1 + count], refs[1 + count : 1 + count + results]
        rest = refs[1 + count + results :]
        buffers, copies = rest[:parts], rest[parts : parts + results]
        in_sems, out_sems, *extra = rest[parts + results :]
        fetches = []
        for at, (_, index) in enumerate(ops.parts):
            ref = sources[source[at]]
            fetches.append(pltpu.make_async_copy(ref.at[index] if index else ref, buffers[at], in_sems.at[at]))
            fetches[-1].start()
        sent = []

        def put(at, *index):
            one, two = (copies[at].at[index], targets[at].at[index]) if index else (copies[at], targets[at])
            sent.append(pltpu.make_async_copy(one, two, out_sems.at[len(sent)]))
            sent[-1].start()

        kernel(meta_ref, Buffers(buffers, fetches), copies, put, *extra)
        for one in sent:
            one.wait()

    whole = pl.BlockSpec(memory_space=pl.ANY)
    return pl.pallas_call(
        body,
        out_shape=outs,
        in_specs=[pl.BlockSpec(memory_space=pltpu.SMEM)] + [whole] * count,
        out_specs=[whole] * results,
        scratch_shapes=[pltpu.VMEM(one.shape, one.dtype) for one in blocks]
        + [pltpu.VMEM(one.shape, one.dtype) for one in outs]
        + [pltpu.SemaphoreType.DMA((parts,)), pltpu.SemaphoreType.DMA((64,))]
        + list(scratch),
        compiler_params=pltpu.CompilerParams(vmem_limit_bytes=limit << 20),
        cost_estimate=pl.CostEstimate(flops=time << 20, bytes_accessed=1 << 16, transcendentals=0),
    )(meta, *arrays)


def whole_side(array):
    return [(array, (z,)) for z in range(DEEP)]


def stacked_side(array, which):
    return [(array, (z, which)) for z in range(DEEP)]


def split_side(low, high):
    return [((low, high)[z // 2], (z % 2,)) for z in range(DEEP)]


def dot(left, right):
    return jnp.dot(left, right, preferred_element_type=FULL)


def nt(left, right):
    return lax.dot_general(left, right, (((1,), (1,)), ((), ())), preferred_element_type=FULL)


def tn(left, right):
    return lax.dot_general(left, right, (((0,), (0,)), ((), ())), preferred_element_type=FULL)


def tall(refs, side, units=ALL):
    return jnp.concatenate([refs[at][(*index, ALL, units)] for at, index in side], axis=0)


def flat(refs, side, units):
    return jnp.concatenate([refs[at][(*index, units)] for at, index in side], axis=1)


def unfold(block):
    return jnp.concatenate([block[:, :LANES], block[:, LANES:]], axis=0)


def row_slices(count=LENGTH // BLOCK):
    return [slice(at * BLOCK, (at + 1) * BLOCK) for at in range(count)]


def rows_of(refs, pair, columns=ALL):
    for at in pair:
        for first in range(0, refs[at].shape[0], BLOCK):
            yield refs[at][first : first + BLOCK, columns]


def chunk_pairs():
    for first in range(0, 2 * DEEP, 2):
        yield (first, first + 1), slice(first * LANES, (first + 2) * LANES)


def by_tokens(lefts, rights):
    total = None
    for left, right in zip(lefts, rights):
        part = tn(left, right)
        total = part if total is None else total + part
    return total.astype(LOW)


def spread(even, terms, own, far, put, at):
    rows = own.shape[0]
    for z in range(DEEP):
        columns = slice(2 * z * LANES, 2 * (z + 1) * LANES)
        rights = []
        for _, chunks, product in terms:
            one, two = chunks(z)
            pair = [jnp.where(even, one, two), jnp.where(even, two, one)]
            rights.append(jnp.concatenate(pair, axis=0 if product is nt else 1))
        for block, here in enumerate(row_slices()):
            total = None
            for (left, _, product), right in zip(terms, rights):
                part = product(left(block), right)
                total = part if total is None else total + part
            if here.start < rows:
                own[here, columns] = total.astype(LOW)
            else:
                far[here.start - rows : here.stop - rows, columns] = total.astype(LOW)
        if z % 2:
            done = slice(columns.stop - 4 * LANES, columns.stop)
            put(at, ALL, done)
            put(at + 1, ALL, done)


def pick(refs, low, high, change=lambda block: block):
    return lambda z: [change(refs[at][one]) for at, one in (low[z], high[z])]


def to_local(at_y, target, rows, values):
    for chunk in range(2 * DEEP):
        place = chunk // 2 + DEEP * lax.rem(chunk + at_y, 2)
        columns = pl.ds(pl.multiple_of(place * LANES, LANES), LANES)
        target[rows, columns] = values[:, chunk * LANES : (chunk + 1) * LANES]


def row_ranges():
    for first in range(0, LENGTH, BLOCK):
        yield first, max(0, first - LENGTH // 2), first + BLOCK


def ordered(ref, which, core, columns):
    half = LENGTH // 2
    start = pl.multiple_of(core * half, half)
    rest = pl.multiple_of((1 - core) * half, half)
    return jnp.concatenate([ref[which, pl.ds(start, half), columns], ref[which, pl.ds(rest, half), columns]], axis=0)


def local_row(first, core):
    return pl.multiple_of(lax.rem(first + core * (LENGTH // 2), LENGTH), BLOCK)


def allowed_tile(meta, first, low, high):
    shape = (BLOCK, high - low)
    places = first + lax.broadcasted_iota(jnp.int32, (BLOCK, 1), 0)
    start = jnp.zeros((BLOCK, 1), jnp.int32)
    for at in range(2, meta.shape[0]):
        start = jnp.where(places >= meta[at], meta[at], start)
    keys = low + lax.broadcasted_iota(jnp.int32, shape, 1)
    return (keys <= places) & (keys >= start)


def first_lanes():
    return lax.broadcasted_iota(jnp.int32, (BLOCK, PAIR), 1) < HEAD_DIM


def attend(meta, qkv, context, logs, put):
    core = meta[0]
    first_head = first_lanes()
    for pair in range(context.shape[1] // PAIR):
        columns = slice(pair * PAIR, (pair + 1) * PAIR)
        keys = ordered(qkv, 1, core, columns)
        values = ordered(qkv, 2, core, columns)
        values = jnp.concatenate([values, jnp.ones_like(values)], axis=1)
        for first, low, high in row_ranges():
            here = local_row(first, core)
            query = qkv[0, pl.ds(here, BLOCK), columns] * SCALE
            allowed = allowed_tile(meta, first, low, high)
            outs = []
            sums = []
            for head in range(2):
                picked = jnp.where(first_head if head == 0 else ~first_head, query, jnp.zeros_like(query))
                scores = jnp.where(allowed, nt(picked, keys[low:high]), -1e30)
                highest = jnp.max(scores, axis=-1, keepdims=True)
                mixed = dot(jnp.exp(scores - highest).astype(LOW), values[low:high])
                totals = mixed[:, PAIR:]
                outs.append(mixed[:, :PAIR] / totals)
                sums.append(highest + jnp.log(totals))
            context[pl.ds(here, BLOCK), columns] = jnp.where(first_head, outs[0], outs[1]).astype(LOW)
            logs[pl.ds(here, BLOCK), columns] = jnp.where(first_head, sums[0], sums[1])
        put(1, ALL, columns)
        put(2, ALL, columns)


def attend_back(meta, qkv, logs, grads, out, sums, key_sum, value_sum):
    core = meta[0]
    first_head = first_lanes()
    half = LENGTH // 2
    for pair in range(grads.shape[1] // PAIR):
        columns = slice(pair * PAIR, (pair + 1) * PAIR)
        keys = ordered(qkv, 1, core, columns)
        values = ordered(qkv, 2, core, columns)
        key_sum[...] = jnp.zeros_like(key_sum)
        value_sum[...] = jnp.zeros_like(value_sum)
        query_total = value_total = jnp.zeros((1, PAIR), FULL)
        for first, low, high in row_ranges():
            here = local_row(first, core)
            query = qkv[0, pl.ds(here, BLOCK), columns] * SCALE
            grad = grads[pl.ds(here, BLOCK), columns]
            log_pair = logs[pl.ds(here, BLOCK), columns]
            allowed = allowed_tile(meta, first, low, high)
            query_flip = query.T
            grad_flip = grad.T
            outs = []
            for head in range(2):
                mask = first_head if head == 0 else ~first_head
                band = slice(head * HEAD_DIM, (head + 1) * HEAD_DIM)
                query_one = jnp.where(mask, query, jnp.zeros_like(query))
                grad_one = jnp.where(mask, grad, jnp.zeros_like(grad))
                log_one = log_pair[:, head * HEAD_DIM : head * HEAD_DIM + 1]
                scores = jnp.where(allowed, nt(query_one, keys[low:high]), -1e30)
                weights = jnp.exp(scores - log_one)
                grad_probs = nt(grad_one, values[low:high])
                inner = jnp.sum(grad_probs * weights, axis=-1, keepdims=True)
                grad_scores = (weights * (grad_probs - inner)).astype(LOW)
                outs.append(dot(grad_scores, keys[low:high]))
                key_sum[band, low:high] += dot(query_flip[band, :], grad_scores)
                value_sum[band, low:high] += dot(grad_flip[band, :], weights.astype(LOW))
            grad_query = (jnp.where(first_head, outs[0], outs[1]) * SCALE).astype(LOW)
            out[0, pl.ds(here, BLOCK), columns] = grad_query
            query_total = query_total + jnp.sum(grad_query.astype(FULL), axis=0, keepdims=True)
        for part in range(2):
            there = pl.multiple_of(lax.rem(part + core, 2) * half, half)
            out[1, pl.ds(there, half), columns] = key_sum[:, part * half : (part + 1) * half].T.astype(LOW)
            grad_value = value_sum[:, part * half : (part + 1) * half].T.astype(LOW)
            out[2, pl.ds(there, half), columns] = grad_value
            value_total = value_total + jnp.sum(grad_value.astype(FULL), axis=0, keepdims=True)
        sums[0:1, columns] = query_total
        sums[1:2, columns] = value_total


def attention_forward(meta, normed, sides, biases, last=None):
    ops = Operands()
    normed_at = [ops.add(normed[0])]
    sides_at = [[ops.side(one) for one in pair] for pair in sides]
    bias_at = ops.add(biases)
    normed_at.append(ops.add(normed[1]))
    width = sides[0][0][0][0].shape[-1]
    rows, wide = normed[0].shape
    outs = [like((3, LENGTH, width), LOW), like((LENGTH, width), LOW), like((LENGTH, width), FULL)]
    if last:
        first_at = ops.add(last[0])
        out_sides = [[ops.side(one) for one in pair] for pair in last[1]]
        outs += [like((rows, wide), LOW), like((rows, wide), LOW)]

    def kernel(meta, refs, results, put):
        qkv, context, logs = results[:3]
        for which, (low, high) in enumerate(sides_at):
            low_w = high_w = None
            for here, block in zip(row_slices(), rows_of(refs, normed_at)):
                if low_w is None:
                    low_w, high_w = tall(refs, low), tall(refs, high)
                total = dot(block[:, :HALF], low_w) + dot(block[:, HALF:], high_w)
                if which != 1:
                    total = total + refs[bias_at][:, which // 2 * width : (which // 2 + 1) * width]
                qkv[which, here, :] = total.astype(LOW)
        put(0)
        attend(meta, qkv, context, logs, put)
        if last:
            terms = [
                (lambda block, left=left: left[row_slices()[block], :], pick(refs, *pair, unfold), dot)
                for left, pair in zip((refs[first_at], context), out_sides)
            ]
            spread(meta[1] == 0, terms, *results[3:], put, 3)

    return call(kernel, meta, ops, outs, time=12 if last else 8)


def attention_backward(meta, grad, side, qkv, logs, context, normed, split):
    ops = Operands()
    grad_at = [ops.add(grad[0])]
    low, high = [[(ops.add(array, ALL, index[1]), (z,)) for z, (array, index) in enumerate(one)] for one in side]
    grad_at.append(ops.add(grad[1]))
    qkv_at, log_at = [ops.add(one) for one in (qkv, logs)]
    normed_at = [ops.add(one) for one in normed]
    context_at = ops.add(context)
    width = context.shape[1]
    blocks, half = like((DEEP, 4, LANES, width), LOW), like((DEEP // 2, 4, LANES, width), LOW)
    far = [half, half] if split else [blocks]

    def kernel(meta, refs, results, put, grads, key_sum, value_sum):
        out, sums = results[:2]

        def target(place):
            if place < DEEP or not split:
                return results[2 + place // DEEP].at[place % DEEP]
            return results[3 + place // 2 - DEEP // 2].at[place % 2]

        low_w = high_w = None
        for here, block in zip(row_slices(), rows_of(refs, grad_at)):
            if low_w is None:
                low_w, high_w = [
                    jnp.concatenate([unfold(refs[at][index]) for at, index in one], axis=1) for one in (low, high)
                ]
            grads[here, :] = (nt(block[:, :HALF], low_w) + nt(block[:, HALF:], high_w)).astype(LOW)
        attend_back(meta, refs[qkv_at], refs[log_at], grads, out, sums, key_sum, value_sum)
        put(0)
        put(1)
        for which in range(3):
            right = [out[which, here, :] for here in row_slices()]
            for places, columns in chunk_pairs():
                block = by_tokens(rows_of(refs, normed_at, columns), right)
                for part, place in enumerate(places):
                    target(place)[which] = block[part * LANES : (part + 1) * LANES, :]
            for one in range(2, 3 + len(far)):
                put(one, ALL, which)
        left = [refs[context_at][here, :] for here in row_slices()]
        for places, columns in chunk_pairs():
            block = by_tokens(left, rows_of(refs, grad_at, columns))
            for part, place in enumerate(places):
                one = block[:, part * LANES : (part + 1) * LANES]
                target(place)[3] = jnp.concatenate([one[:LANES], one[LANES:]], axis=1)
        for one in range(2, 3 + len(far)):
            put(one, ALL, 3)

    return call(
        kernel,
        meta,
        ops,
        [like((3, LENGTH, width), LOW), like((2, width), FULL), blocks] + far,
        [pltpu.VMEM((LENGTH, width), LOW)] + [pltpu.VMEM((PAIR, LENGTH), FULL)] * 2,
        time=15,
    )


def unit_tiles(width):
    for first in range(0, width, BLOCK):
        stop = first + BLOCK
        yield slice(first, stop), slice(stop - width // 2, stop) if stop % (width // 2) == 0 else None


def up_kernel(meta, normed, sides, biases, at, cot):
    ops = Operands()
    normed_at = [ops.add(normed[0])]
    sides_at, bias_at = [[ops.side(one) for one in sides[0]]], [ops.add(biases[0])]
    normed_at.append(ops.add(normed[1]))
    cot_at = [ops.add(one) for one in cot]
    sides_at.append([ops.side(one) for one in sides[1]])
    bias_at.append(ops.add(biases[1]))
    width = sides[0][0][0][0].shape[-1]
    blocks = like((DEEP, width, LANES), LOW)

    def kernel(meta, refs, results, put):
        for x in range(2):
            active, slope, *grads = results[4 * x : 4 * x + 4]
            low, high = sides_at[x]
            for units, done in unit_tiles(width):
                low_w = high_w = None
                for here, block in zip(row_slices(), rows_of(refs, normed_at)):
                    if low_w is None:
                        low_w, high_w = tall(refs, low, units), tall(refs, high, units)
                    before = dot(block[:, :HALF], low_w) + dot(block[:, HALF:], high_w)
                    before = before + refs[bias_at[x]][:, at + units.start : at + units.stop]
                    phi = 0.5 * (1.0 + lax.erf(before * (2.0**-0.5)))
                    active[here, units] = (before * phi).astype(LOW)
                    bell = jnp.exp(-0.5 * before * before) * (2.0 * jnp.pi) ** -0.5
                    slope[here, units] = (phi + before * bell).astype(LOW)
                left = [active[here, units] for here in row_slices()]
                for places, chunks in chunk_pairs():
                    block = by_tokens(left, rows_of(refs, cot_at, chunks))
                    for part, place in enumerate(places):
                        grads[place // DEEP][place % DEEP, units, :] = block[:, part * LANES : (part + 1) * LANES]
                if done:
                    for one in range(4 * x, 4 * x + 4):
                        put(one, ALL, done)

    return call(kernel, meta, ops, ([like((LENGTH, width), LOW)] * 2 + [blocks] * 2) * 2, time=18)


def down_kernel(meta, cot, sides, slopes, normed, up_sides):
    ops = Operands()
    rows, wide = normed[0].shape
    width = slopes[0].shape[1]
    cot_at = [ops.add(cot[0])]
    sides_at, slope_at = [[ops.side(one) for one in sides[0]]], [ops.add(slopes[0])]
    cot_at.append(ops.add(cot[1]))
    sides_at.append([ops.side(one) for one in sides[1]])
    slope_at.append(ops.add(slopes[1]))
    up_at = [[ops.side(one) for one in pair] for pair in up_sides]
    normed_at = [ops.add(one) for one in normed]
    pair = [like((rows, wide), LOW), like((rows, wide), LOW)]
    block, half = like((DEEP, LANES, width), LOW), like((DEEP // 2, LANES, width), LOW)
    outs = [like((1, width), FULL)] * 2 + pair + [block] * 3 + [half] * 2

    def kernel(meta, refs, results, put, *grads):
        for x in range(2):
            low, high = sides_at[x]
            for units, _ in unit_tiles(width):
                total = jnp.zeros((1, BLOCK), FULL)
                low_w = high_w = None
                for here, block in zip(row_slices(), rows_of(refs, cot_at)):
                    if low_w is None:
                        low_w, high_w = flat(refs, low, units), flat(refs, high, units)
                    grad = nt(block[:, :HALF], low_w) + nt(block[:, HALF:], high_w)
                    grad = (grad * refs[slope_at[x]][here, units].astype(FULL)).astype(LOW)
                    grads[x][here, units] = grad
                    total = total + jnp.sum(grad.astype(FULL), axis=0, keepdims=True)
                results[x][:, units] = total
            put(x)

        terms = [
            (lambda block, left=left: left[row_slices()[block], :], pick(refs, *one), nt)
            for left, one in zip(grads, up_at)
        ]
        spread(meta[1] == 0, terms, *results[2:4], put, 2)
        for x in (1, 0):
            own, low, high = (results[6], *results[7:9]) if x else (results[4], None, None)

            def target(place, own=own, low=low, high=high):
                if place < DEEP:
                    return own.at[place]
                place -= DEEP
                return (low, high)[place // 2].at[place % 2] if low is not None else results[5].at[place]

            for units, done in unit_tiles(width):
                right = [grads[x][here, units] for here in row_slices()]
                for places, chunks in chunk_pairs():
                    block = by_tokens(rows_of(refs, normed_at, chunks), right)
                    for part, place in enumerate(places):
                        target(place)[:, units] = block[part * LANES : (part + 1) * LANES, :]
                if done:
                    for one in (6, 7, 8) if x else (4, 5):
                        put(one, ALL, ALL, done)

    return call(kernel, meta, ops, outs, [pltpu.VMEM((LENGTH, width), LOW)] * 2, time=20)


def spread_kernel(meta, terms, rows, wide, product):
    ops = Operands()
    places = [(ops.add(left), at, ops.side(low), ops.side(high)) for left, at, low, high in terms]

    def kernel(meta, refs, results, put):
        def left_of(one, at):
            index = () if at is None else (at,)
            return lambda block: refs[one][(*index, row_slices()[block])]

        parts = [(left_of(one, at), pick(refs, low, high), product) for one, at, low, high in places]
        spread(meta[1] == 0, parts, *results, put, 0)

    return call(kernel, meta, ops, [like((rows, wide), LOW), like((rows, wide), LOW)], time=6)


STRIP = 128


def normalize(values):
    center = values - jnp.mean(values, axis=-1, keepdims=True)
    spread_ = jnp.mean(center * center, axis=-1, keepdims=True)
    rate = lax.rsqrt(spread_ + EPSILON)
    return center * rate, rate


def strips(rows):
    return [slice(first, first + STRIP) for first in range(0, rows, STRIP)]


def by_strips(kernel, meta, arrays, vectors, outs, sums=0):
    ops = Operands()
    rows, wide = arrays[0].shape
    pieces = [slice(0, STRIP), slice(STRIP, rows - STRIP), slice(rows - STRIP, rows)]
    first = [ops.add(array, pieces[0]) for array in arrays]
    vector_at = [ops.add(one) for one in vectors]
    places = [first] + [[ops.add(array, piece) for array in arrays] for piece in pieces[1:]]
    shapes = [like((rows, wide), kind) for kind in outs]
    if sums:
        shapes.append(like((sums, wide), FULL))

    def body(meta, refs, results, put):
        parts = [None] * sums
        for at, piece in zip(places, pieces):
            for here in strips(piece.stop - piece.start):
                kernel(
                    meta,
                    [refs[one][here, :] for one in at],
                    [refs[one][...] for one in vector_at],
                    [(result, slice(piece.start + here.start, piece.start + here.stop)) for result in results[: len(outs)]],
                    parts,
                )
            for one in range(len(outs)):
                put(one, piece)
        if sums:
            for at, value in enumerate(parts):
                results[-1][at : at + 1, :] = jnp.sum(value, axis=0, keepdims=True)
            put(len(outs))

    return call(body, meta, ops, shapes, time=4)


def start_kernel(meta, values, vectors, results, sums):
    tokens, cot = values
    gain, shift = vectors
    hat, _ = normalize(tokens.astype(FULL))
    to_local(meta[1], *results[0], (hat * gain + shift).astype(LOW))
    to_local(meta[1], *results[1], cot.astype(LOW))


def join_kernel(meta, values, vectors, results, sums):
    tokens, own, got = values
    bias, gain, shift = vectors
    total = tokens.astype(FULL) + (own.astype(FULL) + got.astype(FULL)) + bias
    hidden, here = results[0]
    hidden[here, :] = total
    hat, _ = normalize(total)
    to_local(meta[1], *results[1], (hat * gain + shift).astype(LOW))


def add_sums(sums, values):
    for at, value in enumerate(values):
        part = jnp.sum(value.reshape(STRIP // 8, 8, value.shape[1]), axis=0)
        sums[at] = part if sums[at] is None else sums[at] + part


def norm_back(grad, values, gain):
    hat, rate = normalize(values)
    scaled = grad * gain
    row = rate * (
        scaled
        - jnp.mean(scaled, axis=-1, keepdims=True)
        - hat * jnp.mean(scaled * hat, axis=-1, keepdims=True)
    )
    return row, grad * hat


def second_kernel(meta, values, vectors, results, sums):
    own, got, hidden, pulled = values
    grad = own.astype(FULL) + got.astype(FULL)
    row, gain_part = norm_back(grad, hidden, vectors[0])
    total = pulled + row
    out, here = results[0]
    out[here, :] = total
    to_local(meta[1], *results[1], total.astype(LOW))
    add_sums(sums, [gain_part, grad, total, pulled])


def first_kernel(meta, values, vectors, results, sums):
    own, got, tokens, hidden_grad = values
    grad = own.astype(FULL) + got.astype(FULL)
    row, gain_part = norm_back(grad, tokens.astype(FULL), vectors[0])
    out, here = results[0]
    out[here, :] = hidden_grad + row
    add_sums(sums, [gain_part, grad])


def end_kernel(meta, values, vectors, results, sums):
    hidden, own, got = values
    out, here = results[0]
    out[here, :] = (hidden + (own.astype(FULL) + got.astype(FULL)) + vectors[0]).astype(LOW)


def wide_shard(shard, axis):
    return lax.all_gather(shard, "w", axis=axis, tiled=True) if lax.axis_size("w") > 1 else shard


def gather_deep(shard):
    return lax.all_gather(shard, "z", axis=0, tiled=False)


def add(*values):
    total = values[0].astype(FULL)
    for value in values[1:]:
        total = total + value.astype(FULL)
    return total.astype(LOW)


def add_half(whole, part, which):
    size = part.shape[0]
    edges = [(size * which, size * (1 - which), 0)] + [(0, 0, 0)] * (part.ndim - 1)
    return add(whole, lax.pad(part.astype(FULL), FULL(0), edges))


def scatter_deep(total):
    total = lax.psum_scatter(total, "z", scatter_dimension=0, tiled=False)
    if lax.axis_size("w") > 1:
        total = lax.psum_scatter(total, "w", scatter_dimension=total.ndim - 2, tiled=True)
    return total.astype(FULL)


def on_device(
    inputs,
    doc_lengths,
    first_gain,
    first_bias,
    w_query,
    b_query,
    w_key,
    w_value,
    b_value,
    w_out,
    b_out,
    second_gain,
    second_bias,
    w_up,
    b_up,
    w_down,
    b_down,
    cotangent,
):
    rows, wide = inputs.shape
    here = w_query.shape[1]
    core = lax.axis_index("c").astype(jnp.int32)
    at_y = lax.axis_index("y").astype(jnp.int32)
    at_x = lax.axis_index("x")
    lengths = lax.dynamic_index_in_dim(doc_lengths, at_x, 0, keepdims=False)
    ends = [lengths[0]]
    for one in range(1, lengths.shape[0]):
        ends.append(ends[-1] + lengths[one])
    meta = jnp.stack([core, at_y, *ends])

    def line(vector):
        return vector.reshape(1, -1)

    out_shard = wide_shard(w_out, 1)
    out_shard = jnp.concatenate([out_shard[: here // 2], out_shard[here // 2 :]], axis=1)
    attn_shard = jnp.stack([wide_shard(w_query, 0), wide_shard(w_key, 0), wide_shard(w_value, 0), out_shard])
    up_shard = wide_shard(w_up, 0)
    down_shard = wide_shard(w_down, 1)
    biases = line(jnp.concatenate([b_query, b_value, b_up]))
    far = swap(biases, "x")
    down_raw = swap_both(down_shard)
    attn_mine = after(gather_deep(attn_shard), down_raw, far)
    attn_pairs = [attn_mine[:, :2], attn_mine[:, 2:]]
    attn_x = [swap(one, "x") for one in attn_pairs]
    attn_y = [swap(one, "y") for one in attn_pairs]
    attn_far = [
        swap(after(attn_y[0], attn_y[1], *attn_x), "x"),
        swap(after(attn_x[1], attn_x[0], *attn_y), "y"),
    ]


    normed, cot = by_strips(start_kernel, meta, [inputs, cotangent], [line(first_gain), line(first_bias)], [LOW, LOW])
    normed = (normed, swap(normed, "c"))
    cot = (cot, swap(cot, "c"))

    attn_sides = [
        [(stacked_side(attn_mine, which), stacked_side(attn_y[which // 2], which % 2)) for which in range(4)],
        [(stacked_side(attn_x[which // 2], which % 2), stacked_side(attn_far[which // 2], which % 2)) for which in range(4)],
    ]

    qkv, context, logs = [None] * 2, [None] * 2, [None] * 2
    qkv[0], context[0], logs[0] = attention_forward(meta, normed, attn_sides[0][:3], biases)

    half = DEEP // 2
    up_mine = after(gather_deep(up_shard), context[0], *attn_far)
    up_parts = [up_mine[:half], up_mine[half:]]
    up_x = [swap(one, "x") for one in up_parts]
    up_y = [swap(one, "y") for one in up_parts]

    qkv[1], context[1], logs[1], own, sent = attention_forward(
        meta,
        normed,
        attn_sides[1][:3],
        far,
        (context[0], [attn_sides[0][3], attn_sides[1][3]]),
    )
    sent = after(sent, *up_x, *up_y)
    hidden, normed_two = by_strips(
        join_kernel,
        meta,
        [inputs, own, swap(sent, "c")],
        [line(b_out), line(second_gain), line(second_bias)],
        [FULL, LOW],
    )
    up_far = [swap(up_y[0], "x"), swap(up_x[1], "y")]
    normed_two = (normed_two, swap(after(normed_two, *up_far), "c"))

    up_sides = [
        (whole_side(up_mine), split_side(*up_y)),
        (split_side(*up_x), split_side(*up_far)),
    ]
    down_mine = after(gather_deep(down_shard), *up_far)
    down_x = swap(down_mine, "x")
    down_y = swap(down_mine, "y")
    down_both = gather_deep(down_raw)
    down_sides = [
        (whole_side(down_mine), whole_side(down_y)),
        (whole_side(down_x), whole_side(down_both)),
    ]
    active, slope, down_own, down_far = [None] * 2, [None] * 2, [None] * 2, [None] * 2
    (
        active[0],
        slope[0],
        down_own[0],
        down_far[0],
        active[1],
        slope[1],
        down_own[1],
        down_far[1],
    ) = up_kernel(meta, normed_two, up_sides, (biases, far), 2 * here, cot)

    *sums, own, sent, up_own, up_beyond, up_other, up_both_low, up_both_high = down_kernel(
        meta, cot, down_sides, slope, normed_two, up_sides
    )

    down_diagonal = swap_both(lax.psum_scatter(down_far[1], "z", scatter_dimension=0, tiled=False))
    down_total = add(
        down_own[0], swap(after(down_far[0], down_x, down_y), "y"), swap(after(down_own[1], down_x, down_y), "x")
    )
    owner_down = lax.psum_scatter(down_total, "z", scatter_dimension=0, tiled=False)
    owner_down = owner_down.astype(FULL) + down_diagonal.astype(FULL)
    if lax.axis_size("w") > 1:
        owner_down = lax.psum_scatter(owner_down, "w", scatter_dimension=1, tiled=True)

    got_low = swap(up_both_low, "x")
    got_high = swap(up_both_high, "y")

    hidden_grad, attn_grad, second_sums = by_strips(
        second_kernel, meta, [own, swap(sent, "c"), hidden, cotangent], [line(second_gain)], [FULL, LOW], sums=4
    )
    attn_grad = (attn_grad, swap(attn_grad, "c"))

    got_low, got_high = [after(one, attn_grad[0]).astype(FULL) for one in (got_low, got_high)]
    half = ((DEEP // 2, 0, 0), (0, 0, 0), (0, 0, 0))
    got_y = swap(add(up_beyond, lax.pad(got_low, FULL(0), ((0, DEEP // 2, 0), *half[1:]))), "y")
    got_x = swap(add(up_other, lax.pad(got_high, FULL(0), half)), "x")

    back, unit_sums = [None] * 2, [None] * 2
    back[1], unit_sums[1], attn_other, attn_both_low, attn_both_high = attention_backward(
        meta, attn_grad, attn_sides[1][3], qkv[1], logs[1], context[1], normed, True
    )
    attn_low = swap(attn_both_low, "x")
    attn_high = swap(attn_both_high, "y")
    back[0], unit_sums[0], attn_own, attn_beyond = attention_backward(
        meta, (after(attn_grad[0], back[1]), attn_grad[1]), attn_sides[0][3], qkv[0], logs[0], context[0], normed, False
    )
    send_y = add_half(attn_beyond, after(attn_low, back[0]), 0)
    send_x = add_half(attn_other, after(attn_high, back[0]), 1)
    attn_got_y, attn_got_x = swap(send_y, "y"), swap(send_x, "x")
    owner_up = scatter_deep(add(up_own, *[after(one, back[0]) for one in (got_x, got_y)]))
    last, last_sent = spread_kernel(
        meta,
        [(after(active[0], back[0]), None, *down_sides[0]), (active[1], None, *down_sides[1])],
        rows,
        wide,
        dot,
    )
    attn_total = add(attn_own, after(attn_got_x, last_sent), attn_got_y)
    owner_attn = lax.psum_scatter(attn_total, "z", scatter_dimension=0, tiled=False)
    owner_out = owner_attn[3].astype(FULL)
    owner_out = jnp.concatenate([owner_out[:, :LANES], owner_out[:, LANES:]])
    owner_attn = owner_attn[:3].astype(FULL)
    if lax.axis_size("w") > 1:
        owner_attn = lax.psum_scatter(owner_attn, "w", scatter_dimension=1, tiled=True)
        owner_out = lax.psum_scatter(owner_out, "w", scatter_dimension=1, tiled=True)

    own, sent = spread_kernel(
        meta,
        [(back[x], which, *attn_sides[x][which]) for x in range(2) for which in range(3)],
        rows,
        wide,
        nt,
    )
    input_grad, first_sums = by_strips(
        first_kernel, meta, [own, swap(sent, "c"), inputs, hidden_grad], [line(first_gain)], [FULL], sums=2
    )

    [layer_out] = by_strips(
        end_kernel, meta, [hidden, after(last, attn_total), swap(last_sent, "c")], [line(b_down)], [LOW]
    )

    replicated = all_sum(jnp.concatenate([first_sums, second_sums]).reshape(-1), "c")
    own_units, far_units = [
        jnp.concatenate([unit_sums[x][0], unit_sums[x][1], sums[x][0]]) for x in range(2)
    ]
    got = swap(jnp.concatenate([replicated, far_units]), "x")
    summed = jnp.concatenate([replicated, own_units]) + got
    summed = all_sum(summed, "y", (layer_out,))
    summed = all_sum(summed, "z", (owner_down,), (owner_up,))
    summed = all_sum(summed, "w")
    vectors = summed[: 6 * wide].reshape(6, wide)
    units = summed[6 * wide :]

    return (
        layer_out,
        input_grad,
        vectors[0],
        vectors[1],
        owner_attn[0],
        units[:here],
        owner_attn[1],
        owner_attn[2],
        units[here : 2 * here],
        owner_out,
        vectors[4],
        vectors[2],
        vectors[3],
        owner_up,
        units[2 * here :],
        owner_down,
        vectors[5],
    )


def solution(mesh):
    groups, lanes = mesh.shape["fsdp"], mesh.shape["tp"]
    inner = Mesh(
        mesh.devices.reshape(DEEP, 2, groups // (2 * DEEP), lanes // 2, 2), ("z", "y", "w", "x", "c")
    )
    f, t = ("z", "y", "w"), ("x", "c")
    tokens, rows, columns, units = P(f + t, None), P(f, t), P(t, f), P(t)
    return jax.shard_map(
        on_device,
        mesh=inner,
        in_specs=(
            tokens,
            P(f, None),
            P(),
            P(),
            rows,
            units,
            rows,
            rows,
            units,
            columns,
            P(),
            P(),
            P(),
            rows,
            units,
            columns,
            P(),
            tokens,
        ),
        out_specs=(
            tokens,
            tokens,
            P(),
            P(),
            rows,
            units,
            rows,
            rows,
            units,
            columns,
            P(),
            P(),
            P(),
            rows,
            units,
            columns,
            P(),
        ),
        check_vma=False,
    )
```
